32 devices in a mesh: space: 8 (over z, y), path: 4 (over x, core).
Axes of the slice: x: 2, y: 2, z: 4, core: 2. Of those that a mesh axis runs over, the one named last changes fastest.
Arguments:
- path_field: float32 [32, 256, 1024], P('path', 'space'), may hold values from -2.5 to 2.5
- start_state: float32 [256, 1024], P('space'), may hold values from -2.5 to 2.5
- end_state: float32 [256, 1024], P('space'), may hold values from -2.5 to 2.5
Outputs:
- speed_ratio: float32 [32], P('path')
- residual: float32 [32, 256, 1024], P('path', 'space')
- gradient: float32 [32, 256, 1024], P('path', 'space')
The draws below stay inside these ranges and needn't reach their ends.
All inputs are finite; a program needn't handle non-finite values.
Results may differ from the reference program's by a relative error of at most 0.00002.
Values sent between devices are 32-bit elements; how exact they have to be, the bound alone decides.
No kernel may reach another device: no remote copies, remote signals or barrier semaphores. Data moves between devices by JAX's collectives and lax.ppermute only.
A program may use at most 64 MiB of HBM per device.

```python
import jax
import jax.numpy as jnp
from jax import lax

COLS = 1024
GRID_ROWS = 256
SLICES = 32


def draw_path_field(key, part):
    rows = jnp.arange(GRID_ROWS, dtype=jnp.float32)
    ramp = 0.3 * (1.0 + 2.0 * rows / GRID_ROWS)
    base = jax.random.truncated_normal(key, -2.5, 2.5, (SLICES, GRID_ROWS, COLS), jnp.float32)
    return base * ramp[None, :, None]


def block_levels(rng, dims, split, smallest, high):
    def one(position, blocks):
        draws = jax.random.uniform(jax.random.fold_in(jax.random.fold_in(rng, 6), position), (blocks,), jnp.float32, smallest / len(split), high / len(split))
        return jnp.repeat(jnp.exp(draws), dims[position] // blocks).reshape((-1,) + (1,) * (len(dims) - position - 1))

    gain = one(*split[0])
    for cut in split[1:]:
        gain = gain * one(*cut)
    return gain


def centred(stream_key, shape, spread, limit, cuts=(), kind=jnp.bfloat16):
    array = jax.random.normal(stream_key, shape, jnp.float32) * spread
    if len(cuts) > 0:
        array = block_levels(stream_key, shape, cuts, -0.22, 0.18) * array
    return jnp.clip(array, min=-limit, max=limit).astype(kind)


def setup_inputs(seed: int = 0) -> dict:
    streams_of = jax.random.split(jax.random.key(seed), 4)
    path_field = draw_path_field(jax.random.fold_in(streams_of[3], 71), 0)
    start_state = centred(streams_of[1], (GRID_ROWS, COLS), 0.5, 2.5, ((0, 8),), jnp.float32)
    end_state = centred(streams_of[2], (GRID_ROWS, COLS), 0.5, 2.5, ((0, 8),), jnp.float32)
    return {"path_field": path_field, "start_state": start_state, "end_state": end_state}


def laplace_field(field):
    return jnp.roll(field, 1, 1) + jnp.roll(field, -1, 1) + jnp.roll(field, 1, 2) + jnp.roll(field, -1, 2) - 4.0 * field

def reference(path_field, start_state, end_state):
    drift = laplace_field(path_field) + path_field - path_field ** 3
    extended = jnp.concatenate([start_state[None], path_field, end_state[None]], axis=0)
    tangent = extended[2:] - extended[:-2]
    drift_norm = jnp.sqrt(lax.optimization_barrier(jnp.sum(drift * drift, axis=(1, 2))) + 1e-06)
    tangent_norm = jnp.sqrt(lax.optimization_barrier(jnp.sum(tangent * tangent, axis=(1, 2))) + 1e-06)
    speed_ratio = drift_norm / tangent_norm
    residual = speed_ratio[:, None, None] * tangent - drift
    scaled = speed_ratio[:, None, None] * residual
    zero_slice = jnp.zeros_like(scaled[:1])
    padded = jnp.concatenate([zero_slice, scaled, zero_slice], axis=0)
    gradient = padded[:-2] - padded[2:] - (laplace_field(residual) + (1.0 - 3.0 * path_field ** 2) * residual)
    return (speed_ratio, residual, gradient)
```

```python
import functools

import jax
import jax.numpy as jnp
from jax import lax
from jax.experimental import pallas as pl
from jax.experimental.pallas import tpu as pltpu
from jax.sharding import PartitionSpec as P

F32 = jnp.float32
LANES = 128
TILE = 8
EPS = 1e-06
VMEM = pl.BlockSpec(memory_space=pltpu.VMEM)
ANY = pl.BlockSpec(memory_space=pl.ANY)
SUMS = 1


def lanes_sum(x):
    parts = [x[:, i : i + LANES] for i in range(0, x.shape[1], LANES)]
    while len(parts) > 1:
        parts = [a + b for a, b in zip(parts[::2], parts[1::2])] + parts[len(parts) & ~1 :]
    return parts[0]


def sides(x):
    cols = x.shape[1]
    return pltpu.roll(x, 1, 1) + pltpu.roll(x, cols - 1, 1)


def iota(shape, dim):
    return lax.broadcasted_iota(jnp.int32, shape, dim)


def edge_kernel(f_ref, up_ref, tail_ref, head_ref, buf, sem):
    count, rows, _ = f_ref.shape
    copies = [
        pltpu.make_async_copy(f_ref.at[pl.ds(count - 2, 2)], up_ref, sem.at[0]),
        pltpu.make_async_copy(f_ref.at[:, pl.ds(rows - TILE, TILE)], buf.at[0], sem.at[1]),
        pltpu.make_async_copy(f_ref.at[:, pl.ds(0, TILE)], buf.at[1], sem.at[2]),
    ]
    for copy in copies:
        copy.start()
    copies[1].wait()
    for s in range(count):
        for r in range(2):
            tail_ref[r, s : s + 1, :] = buf[0, s, TILE - 2 + r : TILE - 1 + r, :]
    copies[2].wait()
    for s in range(count):
        for r in range(2):
            head_ref[r, s : s + 1, :] = buf[1, s, r : r + 1, :]
    copies[0].wait()


def edges(f):
    count, rows, cols = f.shape
    pair = jax.ShapeDtypeStruct((2, rows, cols), F32)
    strip = jax.ShapeDtypeStruct((2, count, cols), F32)
    return pl.pallas_call(
        edge_kernel,
        out_shape=(pair, strip, strip),
        in_specs=[ANY],
        out_specs=(VMEM, VMEM, VMEM),
        scratch_shapes=[pltpu.VMEM((2, count, TILE, cols), F32), pltpu.SemaphoreType.DMA((3,))],
        name="edges",
    )(f)


def interior_kernel(f_ref, part_ref):
    count, rows, cols = f_ref.shape
    tiles = rows // TILE
    row = iota((TILE, cols), 0)
    part_ref[...] = jnp.zeros_like(part_ref)

    def drift_sum(s, _):
        total = jnp.zeros((TILE, LANES), F32)
        for k in range(tiles):
            c = f_ref[s, pl.ds(TILE * k, TILE), :]
            up = f_ref[s, pl.ds(TILE * k - 1, TILE), :] if k > 0 else pltpu.roll(c, 1, 0)
            dn = f_ref[s, pl.ds(TILE * k + 1, TILE), :] if k < tiles - 1 else pltpu.roll(c, TILE - 1, 0)
            drift = up + dn + sides(c) - 3.0 * c - c * c * c
            if k == 0:
                drift = jnp.where(row == 0, 0.0, drift)
            if k == tiles - 1:
                drift = jnp.where(row == TILE - 1, 0.0, drift)
            total += lanes_sum(drift * drift)
        part_ref[pl.ds(s, 1), :] = jnp.sum(total, axis=0, keepdims=True)
        return 0

    def tangent_sum(s, _):
        total = jnp.zeros((TILE, LANES), F32)
        for k in range(tiles):
            tangent = f_ref[s + 1, pl.ds(TILE * k, TILE), :] - f_ref[s - 1, pl.ds(TILE * k, TILE), :]
            total += lanes_sum(tangent * tangent)
        part_ref[pl.ds(count + s + 1, 1), :] = jnp.sum(total, axis=0, keepdims=True)
        return 0

    lax.fori_loop(0, count, drift_sum, 0)
    lax.fori_loop(1, count - 1, tangent_sum, 0)


def interior(f):
    count, rows, cols = f.shape
    return pl.pallas_call(
        interior_kernel,
        out_shape=jax.ShapeDtypeStruct((2 * count + TILE, LANES), F32),
        in_specs=[VMEM],
        out_specs=VMEM,
        cost_estimate=pl.CostEstimate(flops=20 * count * rows * cols, transcendentals=0, bytes_accessed=4 * count * rows * cols),
        name="interior",
    )(f)


def chunk_kernel(m, n, chunk, f_ref, below_ref, above_ref, tail_ref, head_ref, start_ref, end_ref, part_ref, out_ref):
    count, rows, cols = f_ref.shape
    tiles = rows // TILE
    path = lax.axis_index("path")
    space = lax.axis_index("space")
    first = path == 0
    last = path == m - 1

    r0, r1 = tail_ref[0], tail_ref[1]
    r2, r3 = head_ref[0], head_ref[1]
    drift_a = r0 + r2 + sides(r1) - 3.0 * r1 - r1 * r1 * r1
    drift_b = r1 + r3 + sides(r2) - 3.0 * r2 - r2 * r2 * r2
    drift = part_ref[0:count, :] + lanes_sum(drift_a * drift_a) + lanes_sum(drift_b * drift_b)

    totals = [jnp.zeros((TILE, LANES), F32) for _ in range(3)]
    for k in range(tiles):
        at = pl.ds(TILE * k, TILE)
        prior = jnp.where(first, start_ref[at, :], below_ref[1, at, :])
        tangents = (
            f_ref[0, at, :] - below_ref[0, at, :],
            f_ref[1, at, :] - prior,
            jnp.where(last, end_ref[at, :] - f_ref[count - 2, at, :], 0.0),
        )
        totals = [a + lanes_sum(t * t) for a, t in zip(totals, tangents)]
    sums = [jnp.sum(a, axis=0, keepdims=True) for a in totals]
    sub = iota((TILE, LANES), 0)
    tan_a = part_ref[count : count + TILE, :]
    tan_a = jnp.where(sub == 0, sums[0], jnp.where(sub == 1, sums[1], tan_a))

    lane = iota((TILE, LANES), 1)
    spread = jnp.where(lane == sub, jnp.sum(drift, axis=1, keepdims=True), 0.0)
    spread += jnp.where(lane == sub + count, jnp.sum(tan_a, axis=1, keepdims=True), 0.0)
    line = jnp.sum(spread, axis=0, keepdims=True)
    tan_last = jnp.sum(sums[2], axis=1, keepdims=True)
    line += jnp.where(lane[0:1] == 2 * count, tan_last, 0.0)

    for j in range(m * n):
        out_ref[chunk * j : chunk * j + SUMS, :] = line
    right = lax.rem(space + 1, n) * m
    left = lax.rem(space + n - 1, n) * m

    def put(base, source):
        for i in range(cols // LANES):
            out_ref[pl.ds(base * chunk + SUMS + i, 1), :] = source[:, i * LANES : (i + 1) * LANES]

    @pl.when(jnp.logical_not(first))
    def _():
        put(right + path - 1, f_ref[0, rows - 1 : rows, :])
        put(left + path - 1, f_ref[0, 0:1, :])

    @pl.when(jnp.logical_not(last))
    def _():
        put(right + path + 1, f_ref[count - 1, rows - 1 : rows, :])
        put(left + path + 1, f_ref[count - 1, 0:1, :])

    @pl.when(first)
    def _():
        put(right + path, start_ref[rows - 1 : rows, :])
        put(left + path, start_ref[0:1, :])

    @pl.when(last)
    def _():
        put(right + path, end_ref[rows - 1 : rows, :])
        put(left + path, end_ref[0:1, :])


def chunks(m, n, f, below, tail_in, head, start, end, part):
    chunk = SUMS + f.shape[2] // LANES
    return pl.pallas_call(
        functools.partial(chunk_kernel, m, n, chunk),
        out_shape=jax.ShapeDtypeStruct((m * n * chunk, LANES), F32),
        in_specs=[VMEM] * 8,
        out_specs=VMEM,
        name="chunks",
    )(f, below, below, tail_in, head, start, end, part)


def final_kernel(
    m, n, chunk, got_ref, f_ref, below_ref, above_ref, tail_ref, head_ref, start_ref, end_ref,
    ratio_ref, res_out, grad_out, field, resid, scale, rowbuf, sem,
):
    count, rows, cols = f_ref.shape
    tiles = rows // TILE
    path = lax.axis_index("path")
    space = lax.axis_index("space")
    first = path == 0
    last = path == m - 1
    path_lo = jnp.where(first, path, path - 1)
    path_hi = jnp.where(last, path, path + 1)

    def gathered(p):
        total = got_ref[pl.ds(p * chunk, 1), :]
        for i in range(1, n):
            total += got_ref[pl.ds((i * m + p) * chunk, 1), :]
        return jnp.broadcast_to(total, (TILE, LANES))

    mine = gathered(path)
    lower = gathered(path_lo)
    upper = gathered(path_hi)
    lane = iota((TILE, LANES), 1)
    sub = iota((TILE, LANES), 0)

    def shift(x, k):
        return pltpu.roll(x, k % LANES, 1)

    drift_sq = jnp.where(lane == 0, shift(lower, 1 - count), jnp.where(lane <= count, shift(mine, 1), shift(upper, count + 1)))
    at_end = shift(mine, -count) + jnp.where(last, 0.0, upper)
    tangent_sq = jnp.where(lane < count, shift(mine, -count), jnp.where(lane == count, at_end, upper))
    ratio = jnp.sqrt(drift_sq + EPS) / jnp.sqrt(tangent_sq + EPS)
    ratio = jnp.where((lane == 0) & first, 0.0, ratio)
    ratio = jnp.where((lane == count + 1) & last, 0.0, ratio)
    ratio_ref[...] = shift(ratio, -1)[0, 0:count]
    for s in range(count + 2):
        splat = jnp.sum(jnp.where(lane == s, ratio, 0.0), axis=1, keepdims=True)
        scale[s] = jnp.broadcast_to(splat, (TILE, LANES))
    column = jnp.sum(jnp.where(lane == sub + 1, ratio, 0.0), axis=1, keepdims=True)

    for k in range(tiles):
        src = pl.ds(TILE * k, TILE)
        dst = pl.ds(TILE * (k + 1), TILE)
        field[0, dst, :] = below_ref[0, src, :]
        field[1, dst, :] = jnp.where(first, start_ref[src, :], below_ref[1, src, :])
        field[count + 2, dst, :] = jnp.where(last, end_ref[src, :], above_ref[0, src, :])
        field[count + 3, dst, :] = above_ref[1, src, :]

    def copy_in(s, _):
        for k in range(tiles):
            field[s + 2, pl.ds(TILE * (k + 1), TILE), :] = f_ref[s, pl.ds(TILE * k, TILE), :]
        field[s + 2, pl.ds(TILE - 1, 1), :] = tail_ref[1, pl.ds(s, 1), :]
        field[s + 2, pl.ds(TILE + rows, 1), :] = head_ref[0, pl.ds(s, 1), :]
        return 0

    lax.fori_loop(0, count, copy_in, 0)

    def corner(slot, at, source):
        for i in range(cols // LANES):
            value = got_ref[pl.ds(source * chunk + SUMS + i, 1), :]
            field[slot, pl.ds(at, 1), i * LANES : (i + 1) * LANES] = value

    prev = lax.rem(space + n - 1, n) * m
    nxt = lax.rem(space + 1, n) * m
    corner(1, TILE - 1, prev + path_lo)
    corner(1, TILE + rows, nxt + path_lo)
    corner(count + 2, TILE - 1, prev + path_hi)
    corner(count + 2, TILE + rows, nxt + path_hi)

    def edge_residual(outer, mid, inner, at):
        below = field[1, at : at + 1, :]
        above = field[count + 2, at : at + 1, :]
        subs = iota(mid.shape, 0)
        ahead = jnp.where(subs == count - 1, above, pltpu.roll(mid, count - 1, 0))
        behind = jnp.where(subs == 0, below, pltpu.roll(mid, 1, 0))
        drift = outer + inner + sides(mid) - 3.0 * mid - mid * mid * mid
        return column * (ahead - behind) - drift

    for s in range(count):
        rowbuf[0, s : s + 1, :] = f_ref[s, 0:1, :]
        rowbuf[1, s : s + 1, :] = f_ref[s, rows - 1 : rows, :]
    top = edge_residual(tail_ref[0], tail_ref[1], rowbuf[0], TILE - 1)
    bottom = edge_residual(head_ref[1], head_ref[0], rowbuf[1], TILE + rows)
    for s in range(count):
        resid[s + 1, TILE - 1 : TILE, :] = top[s : s + 1, :]
        resid[s + 1, TILE + rows : TILE + rows + 1, :] = bottom[s : s + 1, :]

    def widen(x):
        return jnp.concatenate([x] * (cols // LANES), axis=1)

    def residual_of(t, _):
        r = widen(scale[t])
        for k in range(tiles):
            base = TILE * (k + 1)
            c = field[t + 1, pl.ds(base, TILE), :]
            drift = field[t + 1, pl.ds(base - 1, TILE), :] + field[t + 1, pl.ds(base + 1, TILE), :] + sides(c) - 3.0 * c - c * c * c
            tangent = field[t + 2, pl.ds(base, TILE), :] - field[t, pl.ds(base, TILE), :]
            resid[t, pl.ds(base, TILE), :] = r * tangent - drift
        return 0

    lax.fori_loop(0, count + 2, residual_of, 0)
    res_copy = pltpu.make_async_copy(resid.at[pl.ds(1, count), pl.ds(TILE, rows)], res_out, sem.at[0])
    res_copy.start()

    def gradient_of(s, _):
        lo = widen(scale[s])
        hi = widen(scale[s + 2])
        for k in range(tiles):
            base = TILE * (k + 1)
            c = field[s + 2, pl.ds(base, TILE), :]
            r = resid[s + 1, pl.ds(base, TILE), :]
            lap = resid[s + 1, pl.ds(base - 1, TILE), :] + resid[s + 1, pl.ds(base + 1, TILE), :] + sides(r)
            out = lo * resid[s, pl.ds(base, TILE), :] - hi * resid[s + 2, pl.ds(base, TILE), :]
            field[s, pl.ds(base, TILE), :] = out - (lap - (3.0 + 3.0 * c * c) * r)
        return 0

    lax.fori_loop(0, count, gradient_of, 0)
    grad_copy = pltpu.make_async_copy(field.at[pl.ds(0, count), pl.ds(TILE, rows)], grad_out, sem.at[1])
    grad_copy.start()
    res_copy.wait()
    grad_copy.wait()


def final(m, n, got, f, below, above, tail_in, head_in, start, end):
    count, rows, cols = f.shape
    chunk = SUMS + cols // LANES
    big = jax.ShapeDtypeStruct(f.shape, F32)
    return pl.pallas_call(
        functools.partial(final_kernel, m, n, chunk),
        out_shape=(jax.ShapeDtypeStruct((count,), F32), big, big),
        in_specs=[VMEM] * 8,
        out_specs=(VMEM, ANY, ANY),
        scratch_shapes=[
            pltpu.VMEM((count + 4, rows + 2 * TILE, cols), F32),
            pltpu.VMEM((count + 2, rows + 2 * TILE, cols), F32),
            pltpu.VMEM((count + 2, TILE, LANES), F32),
            pltpu.VMEM((2, count, cols), F32),
            pltpu.SemaphoreType.DMA((2,)),
        ],
        name="final",
    )(got, f, below, above, tail_in, head_in, start, end)


def body(m, n, f, start, end):
    count = f.shape[0]
    up, tail, head = edges(f)
    tail_in = lax.ppermute(tail, "space", [(i, (i + 1) % n) for i in range(n)])
    below = lax.ppermute(up, "path", [(i, i + 1) for i in range(m - 1)])
    part = interior(f)
    send = chunks(m, n, f, below, tail_in, head, start, end, part)
    got = lax.all_to_all(send, ("space", "path"), 0, 0, tiled=True)
    down, head_out, send = lax.optimization_barrier((f[0:2], head, send))
    above = lax.ppermute(down, "path", [(i + 1, i) for i in range(m - 1)])
    head_in = lax.ppermute(head_out, "space", [((i + 1) % n, i) for i in range(n)])
    return final(m, n, got, f, below, above, tail_in, head_in, start, end)


def solution(mesh):
    m, n = mesh.shape["path"], mesh.shape["space"]
    in_specs = (P("path", "space", None), P("space", None), P("space", None))
    out_specs = (P("path"), P("path", "space", None), P("path", "space", None))
    return jax.shard_map(
        functools.partial(body, m, n), mesh=mesh, in_specs=in_specs, out_specs=out_specs, check_vma=False
    )
```

```python
import functools

import jax
import jax.numpy as jnp
from jax import lax
from jax.experimental import pallas as pl
from jax.experimental.pallas import tpu as pltpu
from jax.sharding import PartitionSpec as P

F32 = jnp.float32
LANES = 128
TILE = 8
EPS = 1e-06
VMEM = pl.BlockSpec(memory_space=pltpu.VMEM)
ANY = pl.BlockSpec(memory_space=pl.ANY)
PARAMS = pltpu.CompilerParams(vmem_limit_bytes=16 * 2**20)


def lanes_sum(x):
    parts = [x[:, i : i + LANES] for i in range(0, x.shape[1], LANES)]
    while len(parts) > 1:
        parts = [a + b for a, b in zip(parts[::2], parts[1::2])] + parts[len(parts) & ~1 :]
    return parts[0]


def sides(x):
    cols = x.shape[1]
    return pltpu.roll(x, 1, 1) + pltpu.roll(x, cols - 1, 1)


def iota(shape, dim):
    return lax.broadcasted_iota(jnp.int32, shape, dim)


def edge_kernel(f_ref, up_ref, down_ref, tail_ref, head_ref):
    count, rows, _ = f_ref.shape
    for s in range(count):
        for r in range(2):
            tail_ref[r, s : s + 1, :] = f_ref[s, rows - 2 + r : rows - 1 + r, :]
            head_ref[r, s : s + 1, :] = f_ref[s, r : r + 1, :]
    for s in range(2):
        up_ref[s] = f_ref[count - 2 + s]
        down_ref[s] = f_ref[s]


def edges(f):
    count, rows, cols = f.shape
    pair = jax.ShapeDtypeStruct((2, rows, cols), F32)
    strip = jax.ShapeDtypeStruct((2, count, cols), F32)
    return pl.pallas_call(
        edge_kernel,
        out_shape=(pair, pair, strip, strip),
        in_specs=[VMEM],
        out_specs=(VMEM, VMEM, VMEM, VMEM),
        compiler_params=PARAMS,
        name="edges",
    )(f)


def interior_kernel(f_ref, part_ref):
    count, rows, cols = f_ref.shape
    tiles = rows // TILE
    row = iota((TILE, cols), 0)
    part_ref[...] = jnp.zeros_like(part_ref)

    def drift_sum(s, _):
        total = jnp.zeros((TILE, LANES), F32)
        for k in range(tiles):
            c = f_ref[s, pl.ds(TILE * k, TILE), :]
            up = f_ref[s, pl.ds(TILE * k - 1, TILE), :] if k > 0 else pltpu.roll(c, 1, 0)
            dn = f_ref[s, pl.ds(TILE * k + 1, TILE), :] if k < tiles - 1 else pltpu.roll(c, TILE - 1, 0)
            drift = up + dn + sides(c) - 3.0 * c - c * c * c
            if k == 0:
                drift = jnp.where(row == 0, 0.0, drift)
            if k == tiles - 1:
                drift = jnp.where(row == TILE - 1, 0.0, drift)
            total += lanes_sum(drift * drift)
        part_ref[pl.ds(s, 1), :] = jnp.sum(total, axis=0, keepdims=True)
        return 0

    def tangent_sum(s, _):
        total = jnp.zeros((TILE, LANES), F32)
        for k in range(tiles):
            tangent = f_ref[s + 1, pl.ds(TILE * k, TILE), :] - f_ref[s - 1, pl.ds(TILE * k, TILE), :]
            total += lanes_sum(tangent * tangent)
        part_ref[pl.ds(count + s + 1, 1), :] = jnp.sum(total, axis=0, keepdims=True)
        return 0

    lax.fori_loop(0, count, drift_sum, 0)
    lax.fori_loop(1, count - 1, tangent_sum, 0)


def interior(f):
    count, rows, cols = f.shape
    return pl.pallas_call(
        interior_kernel,
        out_shape=jax.ShapeDtypeStruct((2 * count + TILE, LANES), F32),
        in_specs=[VMEM],
        out_specs=VMEM,
        cost_estimate=pl.CostEstimate(flops=20 * count * rows * cols, transcendentals=0, bytes_accessed=4 * count * rows * cols),
        compiler_params=PARAMS,
        name="interior",
    )(f)


def chunk_kernel(m, n, f_ref, below_ref, above_ref, tail_ref, head_ref, start_ref, end_ref, part_ref, out_ref):
    count, rows, cols = f_ref.shape
    tiles = rows // TILE
    path = lax.axis_index("path")
    space = lax.axis_index("space")
    first = path == 0
    last = path == m - 1

    r0, r1 = tail_ref[0], tail_ref[1]
    r2, r3 = head_ref[0], head_ref[1]
    drift_a = r0 + r2 + sides(r1) - 3.0 * r1 - r1 * r1 * r1
    drift_b = r1 + r3 + sides(r2) - 3.0 * r2 - r2 * r2 * r2
    drift = part_ref[0:count, :] + lanes_sum(drift_a * drift_a) + lanes_sum(drift_b * drift_b)

    totals = [jnp.zeros((TILE, LANES), F32) for _ in range(3)]
    for k in range(tiles):
        at = pl.ds(TILE * k, TILE)
        prior = jnp.where(first, start_ref[at, :], below_ref[1, at, :])
        tangents = (
            f_ref[0, at, :] - below_ref[0, at, :],
            f_ref[1, at, :] - prior,
            jnp.where(last, end_ref[at, :] - f_ref[count - 2, at, :], 0.0),
        )
        totals = [a + lanes_sum(t * t) for a, t in zip(totals, tangents)]
    sums = [jnp.sum(a, axis=0, keepdims=True) for a in totals]
    sub = iota((TILE, LANES), 0)
    tan_a = part_ref[count : count + TILE, :]
    tan_a = jnp.where(sub == 0, sums[0], jnp.where(sub == 1, sums[1], tan_a))

    lane = iota((TILE, LANES), 1)
    spread = jnp.where(lane == sub, jnp.sum(drift, axis=1, keepdims=True), 0.0)
    spread += jnp.where(lane == sub + count, jnp.sum(tan_a, axis=1, keepdims=True), 0.0)
    line = jnp.sum(spread, axis=0, keepdims=True)
    tan_last = jnp.sum(sums[2], axis=1, keepdims=True)
    line += jnp.where(lane[0:1] == 2 * count, tan_last, 0.0)

    for j in range(m * n):
        out_ref[j, :, 0:LANES] = line
    right = lax.rem(space + 1, n) * m
    left = lax.rem(space + n - 1, n) * m

    def put(base, source):
        out_ref[base, :, LANES:] = source

    @pl.when(jnp.logical_not(first))
    def _():
        put(right + path - 1, f_ref[0, rows - 1 : rows, :])
        put(left + path - 1, f_ref[0, 0:1, :])

    @pl.when(jnp.logical_not(last))
    def _():
        put(right + path + 1, f_ref[count - 1, rows - 1 : rows, :])
        put(left + path + 1, f_ref[count - 1, 0:1, :])

    @pl.when(first)
    def _():
        put(right + path, start_ref[rows - 1 : rows, :])
        put(left + path, start_ref[0:1, :])

    @pl.when(last)
    def _():
        put(right + path, end_ref[rows - 1 : rows, :])
        put(left + path, end_ref[0:1, :])


def chunks(m, n, f, below, tail_in, head, start, end, part):
    return pl.pallas_call(
        functools.partial(chunk_kernel, m, n),
        out_shape=jax.ShapeDtypeStruct((m * n, 1, LANES + f.shape[2]), F32),
        in_specs=[VMEM] * 8,
        out_specs=VMEM,
        compiler_params=PARAMS,
        name="chunks",
    )(f, below, below, tail_in, head, start, end, part)


def final_kernel(
    m, n, got_ref, f_ref, below_ref, above_ref, tail_ref, head_ref, start_ref, end_ref,
    ratio_ref, res_out, grad_out, field, resid, scale, rowbuf, sem,
):
    count, rows, cols = f_ref.shape
    tiles = rows // TILE
    path = lax.axis_index("path")
    space = lax.axis_index("space")
    first = path == 0
    last = path == m - 1
    path_lo = jnp.where(first, path, path - 1)
    path_hi = jnp.where(last, path, path + 1)

    def gathered(p):
        total = got_ref[p, :, 0:LANES]
        for i in range(1, n):
            total += got_ref[i * m + p, :, 0:LANES]
        return jnp.broadcast_to(total, (TILE, LANES))

    mine = gathered(path)
    lower = gathered(path_lo)
    upper = gathered(path_hi)
    lane = iota((TILE, LANES), 1)
    sub = iota((TILE, LANES), 0)

    def shift(x, k):
        return pltpu.roll(x, k % LANES, 1)

    drift_sq = jnp.where(lane == 0, shift(lower, 1 - count), jnp.where(lane <= count, shift(mine, 1), shift(upper, count + 1)))
    at_end = shift(mine, -count) + jnp.where(last, 0.0, upper)
    tangent_sq = jnp.where(lane < count, shift(mine, -count), jnp.where(lane == count, at_end, upper))
    ratio = jnp.sqrt(drift_sq + EPS) / jnp.sqrt(tangent_sq + EPS)
    ratio = jnp.where((lane == 0) & first, 0.0, ratio)
    ratio = jnp.where((lane == count + 1) & last, 0.0, ratio)
    ratio_ref[...] = shift(ratio, -1)[0, 0:count]
    for s in range(count + 2):
        splat = jnp.sum(jnp.where(lane == s, ratio, 0.0), axis=1, keepdims=True)
        scale[s] = jnp.broadcast_to(splat, (TILE, LANES))
    column = jnp.sum(jnp.where(lane == sub + 1, ratio, 0.0), axis=1, keepdims=True)

    for k in range(tiles):
        src = pl.ds(TILE * k, TILE)
        dst = pl.ds(TILE * (k + 1), TILE)
        field[0, dst, :] = below_ref[0, src, :]
        field[1, dst, :] = jnp.where(first, start_ref[src, :], below_ref[1, src, :])
        field[count + 2, dst, :] = jnp.where(last, end_ref[src, :], above_ref[0, src, :])
        field[count + 3, dst, :] = above_ref[1, src, :]

    def copy_in(s, _):
        for k in range(tiles):
            field[s + 2, pl.ds(TILE * (k + 1), TILE), :] = f_ref[s, pl.ds(TILE * k, TILE), :]
        field[s + 2, pl.ds(TILE - 1, 1), :] = tail_ref[1, pl.ds(s, 1), :]
        field[s + 2, pl.ds(TILE + rows, 1), :] = head_ref[0, pl.ds(s, 1), :]
        return 0

    lax.fori_loop(0, count, copy_in, 0)

    def corner(slot, at, source):
        field[slot, pl.ds(at, 1), :] = got_ref[source, :, LANES:]

    prev = lax.rem(space + n - 1, n) * m
    nxt = lax.rem(space + 1, n) * m
    corner(1, TILE - 1, prev + path_lo)
    corner(1, TILE + rows, nxt + path_lo)
    corner(count + 2, TILE - 1, prev + path_hi)
    corner(count + 2, TILE + rows, nxt + path_hi)

    def edge_residual(outer, mid, inner, at):
        below = field[1, at : at + 1, :]
        above = field[count + 2, at : at + 1, :]
        subs = iota(mid.shape, 0)
        ahead = jnp.where(subs == count - 1, above, pltpu.roll(mid, count - 1, 0))
        behind = jnp.where(subs == 0, below, pltpu.roll(mid, 1, 0))
        drift = outer + inner + sides(mid) - 3.0 * mid - mid * mid * mid
        return column * (ahead - behind) - drift

    for s in range(count):
        rowbuf[0, s : s + 1, :] = f_ref[s, 0:1, :]
        rowbuf[1, s : s + 1, :] = f_ref[s, rows - 1 : rows, :]
    top = edge_residual(tail_ref[0], tail_ref[1], rowbuf[0], TILE - 1)
    bottom = edge_residual(head_ref[1], head_ref[0], rowbuf[1], TILE + rows)
    for s in range(count):
        resid[s + 1, TILE - 1 : TILE, :] = top[s : s + 1, :]
        resid[s + 1, TILE + rows : TILE + rows + 1, :] = bottom[s : s + 1, :]

    def widen(x):
        return jnp.concatenate([x] * (cols // LANES), axis=1)

    def residual_of(t, _):
        r = widen(scale[t])
        for k in range(tiles):
            base = TILE * (k + 1)
            c = field[t + 1, pl.ds(base, TILE), :]
            drift = field[t + 1, pl.ds(base - 1, TILE), :] + field[t + 1, pl.ds(base + 1, TILE), :] + sides(c) - 3.0 * c - c * c * c
            tangent = field[t + 2, pl.ds(base, TILE), :] - field[t, pl.ds(base, TILE), :]
            resid[t, pl.ds(base, TILE), :] = r * tangent - drift
        return 0

    lax.fori_loop(0, count + 2, residual_of, 0)
    res_copy = pltpu.make_async_copy(resid.at[pl.ds(1, count), pl.ds(TILE, rows)], res_out, sem.at[0])
    res_copy.start()

    def gradient_of(s, _):
        lo = widen(scale[s])
        hi = widen(scale[s + 2])
        for k in range(tiles):
            base = TILE * (k + 1)
            c = field[s + 2, pl.ds(base, TILE), :]
            r = resid[s + 1, pl.ds(base, TILE), :]
            lap = resid[s + 1, pl.ds(base - 1, TILE), :] + resid[s + 1, pl.ds(base + 1, TILE), :] + sides(r)
            out = lo * resid[s, pl.ds(base, TILE), :] - hi * resid[s + 2, pl.ds(base, TILE), :]
            field[s, pl.ds(base, TILE), :] = out - (lap - (3.0 + 3.0 * c * c) * r)
        return 0

    lax.fori_loop(0, count, gradient_of, 0)
    grad_copy = pltpu.make_async_copy(field.at[pl.ds(0, count), pl.ds(TILE, rows)], grad_out, sem.at[1])
    grad_copy.start()
    res_copy.wait()
    grad_copy.wait()


def final(m, n, got, f, below, above, tail_in, head_in, start, end):
    count, rows, cols = f.shape
    big = jax.ShapeDtypeStruct(f.shape, F32)
    return pl.pallas_call(
        functools.partial(final_kernel, m, n),
        out_shape=(jax.ShapeDtypeStruct((count,), F32), big, big),
        in_specs=[VMEM] * 8,
        out_specs=(VMEM, ANY, ANY),
        scratch_shapes=[
            pltpu.VMEM((count + 4, rows + 2 * TILE, cols), F32),
            pltpu.VMEM((count + 2, rows + 2 * TILE, cols), F32),
            pltpu.VMEM((count + 2, TILE, LANES), F32),
            pltpu.VMEM((2, count, cols), F32),
            pltpu.SemaphoreType.DMA((2,)),
        ],
        compiler_params=PARAMS,
        name="final",
    )(got, f, below, above, tail_in, head_in, start, end)


def body(m, n, f, start, end):
    count = f.shape[0]
    up, down, tail, head = edges(f)
    tail_in = lax.ppermute(tail, "space", [(i, (i + 1) % n) for i in range(n)])
    below = lax.ppermute(up, "path", [(i, i + 1) for i in range(m - 1)])
    part = interior(f)
    send = chunks(m, n, f, below, tail_in, head, start, end, part)
    got = lax.all_to_all(send, ("space", "path"), 0, 0, tiled=True)
    down, head_out, send = lax.optimization_barrier((down, head, send))
    above = lax.ppermute(down, "path", [(i + 1, i) for i in range(m - 1)])
    head_in = lax.ppermute(head_out, "space", [((i + 1) % n, i) for i in range(n)])
    return final(m, n, got, f, below, above, tail_in, head_in, start, end)


def solution(mesh):
    m, n = mesh.shape["path"], mesh.shape["space"]
    in_specs = (P("path", "space", None), P("space", None), P("space", None))
    out_specs = (P("path"), P("path", "space", None), P("path", "space", None))
    return jax.shard_map(
        functools.partial(body, m, n), mesh=mesh, in_specs=in_specs, out_specs=out_specs, check_vma=False
    )
```

```python
import functools

import jax
import jax.numpy as jnp
from jax import lax
from jax.experimental import pallas as pl
from jax.experimental.pallas import tpu as pltpu
from jax.sharding import PartitionSpec as P

F32 = jnp.float32
LANES = 128
TILE = 8
EPS = 1e-06
VMEM = pl.BlockSpec(memory_space=pltpu.VMEM)
ANY = pl.BlockSpec(memory_space=pl.ANY)
PARAMS = pltpu.CompilerParams(vmem_limit_bytes=16 * 2**20)


def lanes_sum(x):
    parts = [x[:, i : i + LANES] for i in range(0, x.shape[1], LANES)]
    while len(parts) > 1:
        parts = [a + b for a, b in zip(parts[::2], parts[1::2])] + parts[len(parts) & ~1 :]
    return parts[0]


def sides(x):
    cols = x.shape[1]
    return pltpu.roll(x, 1, 1) + pltpu.roll(x, cols - 1, 1)


def iota(shape, dim):
    return lax.broadcasted_iota(jnp.int32, shape, dim)


def edge_kernel(f_ref, up_ref, down_ref, tail_ref, head_ref):
    count, rows, _ = f_ref.shape
    for s in range(count):
        for r in range(2):
            tail_ref[r, s : s + 1, :] = f_ref[s, rows - 2 + r : rows - 1 + r, :]
            head_ref[r, s : s + 1, :] = f_ref[s, r : r + 1, :]
    for s in range(2):
        up_ref[s] = f_ref[count - 2 + s]
        down_ref[s] = f_ref[s]


def edges(f):
    count, rows, cols = f.shape
    pair = jax.ShapeDtypeStruct((2, rows, cols), F32)
    strip = jax.ShapeDtypeStruct((2, count, cols), F32)
    return pl.pallas_call(
        edge_kernel,
        out_shape=(pair, pair, strip, strip),
        in_specs=[VMEM],
        out_specs=(VMEM, VMEM, VMEM, VMEM),
        compiler_params=PARAMS,
        name="edges",
    )(f)


def interior_kernel(f_ref, part_ref, drift_ref, rim_ref):
    count, rows, cols = f_ref.shape
    tiles = rows // TILE
    row = iota((TILE, cols), 0)
    part_ref[...] = jnp.zeros_like(part_ref)

    def drift_sum(s, _):
        total = jnp.zeros((TILE, LANES), F32)
        for k in range(tiles):
            c = f_ref[s, pl.ds(TILE * k, TILE), :]
            above = f_ref[s, pl.ds(TILE * k - 1, 1), :] if k > 0 else 0.0
            under = f_ref[s, pl.ds(TILE * (k + 1), 1), :] if k < tiles - 1 else 0.0
            up = jnp.where(row == 0, above, pltpu.roll(c, 1, 0))
            dn = jnp.where(row == TILE - 1, under, pltpu.roll(c, TILE - 1, 0))
            drift = up + dn + sides(c) - 3.0 * c - c * c * c
            drift_ref[s, pl.ds(TILE * k, TILE), :] = drift
            if k == 0:
                rim_ref[0, pl.ds(s, 1), :] = drift[0:1]
                drift = jnp.where(row == 0, 0.0, drift)
            if k == tiles - 1:
                rim_ref[1, pl.ds(s, 1), :] = drift[TILE - 1 : TILE]
                drift = jnp.where(row == TILE - 1, 0.0, drift)
            total += lanes_sum(drift * drift)
        part_ref[pl.ds(s, 1), :] = jnp.sum(total, axis=0, keepdims=True)
        return 0

    def tangent_sum(s, _):
        total = jnp.zeros((TILE, LANES), F32)
        for k in range(tiles):
            tangent = f_ref[s + 1, pl.ds(TILE * k, TILE), :] - f_ref[s - 1, pl.ds(TILE * k, TILE), :]
            total += lanes_sum(tangent * tangent)
        part_ref[pl.ds(count + s + 1, 1), :] = jnp.sum(total, axis=0, keepdims=True)
        return 0

    lax.fori_loop(0, count, drift_sum, 0)
    lax.fori_loop(1, count - 1, tangent_sum, 0)


def interior(f):
    count, rows, cols = f.shape
    return pl.pallas_call(
        interior_kernel,
        out_shape=(
            jax.ShapeDtypeStruct((2 * count + TILE, LANES), F32),
            jax.ShapeDtypeStruct(f.shape, F32),
            jax.ShapeDtypeStruct((2, count, cols), F32),
        ),
        in_specs=[VMEM],
        out_specs=[VMEM] * 3,
        cost_estimate=pl.CostEstimate(flops=20 * count * rows * cols, transcendentals=0, bytes_accessed=8 * count * rows * cols),
        compiler_params=PARAMS,
        name="interior",
    )(f)


def chunk_kernel(m, n, f_ref, below_ref, tail_ref, head_ref, start_ref, end_ref, part_ref, rim_ref, out_ref):
    count, rows, cols = f_ref.shape
    tiles = rows // TILE
    path = lax.axis_index("path")
    space = lax.axis_index("space")
    first = path == 0
    last = path == m - 1

    drift_a = rim_ref[0] + tail_ref[1]
    drift_b = rim_ref[1] + head_ref[0]
    drift = part_ref[0:count, :] + lanes_sum(drift_a * drift_a) + lanes_sum(drift_b * drift_b)

    totals = [jnp.zeros((TILE, LANES), F32) for _ in range(3)]
    for k in range(tiles):
        at = pl.ds(TILE * k, TILE)
        prior = jnp.where(first, start_ref[at, :], below_ref[1, at, :])
        tangents = (
            f_ref[0, at, :] - below_ref[0, at, :],
            f_ref[1, at, :] - prior,
            jnp.where(last, end_ref[at, :] - f_ref[count - 2, at, :], 0.0),
        )
        totals = [a + lanes_sum(t * t) for a, t in zip(totals, tangents)]
    sums = [jnp.sum(a, axis=0, keepdims=True) for a in totals]
    sub = iota((TILE, LANES), 0)
    tan_a = part_ref[count : count + TILE, :]
    tan_a = jnp.where(sub == 0, sums[0], jnp.where(sub == 1, sums[1], tan_a))

    lane = iota((TILE, LANES), 1)
    spread = jnp.where(lane == sub, jnp.sum(drift, axis=1, keepdims=True), 0.0)
    spread += jnp.where(lane == sub + count, jnp.sum(tan_a, axis=1, keepdims=True), 0.0)
    line = jnp.sum(spread, axis=0, keepdims=True)
    tan_last = jnp.sum(sums[2], axis=1, keepdims=True)
    line += jnp.where(lane[0:1] == 2 * count, tan_last, 0.0)

    for j in range(m * n):
        out_ref[j, :, 0:LANES] = line
    right = lax.rem(space + 1, n) * m
    left = lax.rem(space + n - 1, n) * m

    def put(base, source):
        out_ref[base, :, LANES:] = source

    @pl.when(jnp.logical_not(first))
    def _():
        put(right + path - 1, f_ref[0, rows - 1 : rows, :])
        put(left + path - 1, f_ref[0, 0:1, :])

    @pl.when(jnp.logical_not(last))
    def _():
        put(right + path + 1, f_ref[count - 1, rows - 1 : rows, :])
        put(left + path + 1, f_ref[count - 1, 0:1, :])

    @pl.when(first)
    def _():
        put(right + path, start_ref[rows - 1 : rows, :])
        put(left + path, start_ref[0:1, :])

    @pl.when(last)
    def _():
        put(right + path, end_ref[rows - 1 : rows, :])
        put(left + path, end_ref[0:1, :])


def chunks(m, n, f, below, tail_in, head_in, start, end, part, rim):
    return pl.pallas_call(
        functools.partial(chunk_kernel, m, n),
        out_shape=jax.ShapeDtypeStruct((m * n, 1, LANES + f.shape[2]), F32),
        in_specs=[VMEM] * 8,
        out_specs=VMEM,
        compiler_params=PARAMS,
        name="chunks",
    )(f, below, tail_in, head_in, start, end, part, rim)


def final_kernel(
    m, n, got_ref, f_ref, drift_ref, below_ref, above_ref, tail_ref, head_ref, start_ref, end_ref,
    ratio_ref, res_out, grad_out, resid, grad, outer, rim, sem,
):
    count, rows, cols = f_ref.shape
    tiles = rows // TILE
    path = lax.axis_index("path")
    space = lax.axis_index("space")
    first = path == 0
    last = path == m - 1
    path_lo = jnp.where(first, path, path - 1)
    path_hi = jnp.where(last, path, path + 1)

    def gathered(p):
        total = got_ref[p, :, 0:LANES]
        for i in range(1, n):
            total += got_ref[i * m + p, :, 0:LANES]
        return jnp.broadcast_to(total, (TILE, LANES))

    mine = gathered(path)
    lower = gathered(path_lo)
    upper = gathered(path_hi)
    lane = iota((TILE, LANES), 1)
    sub = iota((TILE, LANES), 0)

    def shift(x, k):
        return pltpu.roll(x, k % LANES, 1)

    drift_sq = jnp.where(lane == 0, shift(lower, 1 - count), jnp.where(lane <= count, shift(mine, 1), shift(upper, count + 1)))
    at_end = shift(mine, -count) + jnp.where(last, 0.0, upper)
    tangent_sq = jnp.where(lane < count, shift(mine, -count), jnp.where(lane == count, at_end, upper))
    ratio = jnp.sqrt(drift_sq + EPS) / jnp.sqrt(tangent_sq + EPS)
    ratio = jnp.where((lane == 0) & first, 0.0, ratio)
    ratio = jnp.where((lane == count + 1) & last, 0.0, ratio)
    ratio_ref[...] = shift(ratio, -1)[0, 0:count]

    def splat(t):
        return jnp.broadcast_to(jnp.sum(jnp.where(lane == t, ratio, 0.0), axis=1, keepdims=True), (TILE, LANES))

    def widen(x):
        return jnp.concatenate([x] * (cols // LANES), axis=1)

    scale = [widen(splat(t)) for t in range(count + 2)]
    column = jnp.sum(jnp.where(lane == sub + 1, ratio, 0.0), axis=1, keepdims=True)
    row = iota((TILE, cols), 0)
    prev = lax.rem(space + n - 1, n) * m
    nxt = lax.rem(space + 1, n) * m

    def at(k):
        return pl.ds(TILE * k, TILE)

    for k in range(tiles):
        outer[0, at(k), :] = jnp.where(first, start_ref[at(k), :], below_ref[1, at(k), :])
        outer[1, at(k), :] = jnp.where(last, end_ref[at(k), :], above_ref[0, at(k), :])

    def value(s, k):
        where = {-2: (below_ref, 0), -1: (outer, 0), count: (outer, 1), count + 1: (above_ref, 1)}
        ref, slot = where.get(s, (f_ref, s))
        return ref[slot, at(k), :]

    for s in range(count):
        rim[0, s : s + 1, :] = f_ref[s, 0:1, :]
        rim[1, s : s + 1, :] = f_ref[s, rows - 1 : rows, :]
    for far, mid, near, base, place in (
        (tail_ref[0], tail_ref[1], rim[0], prev, TILE - 1),
        (head_ref[1], head_ref[0], rim[1], nxt, TILE + rows),
    ):
        low = got_ref[base + path_lo, :, LANES:]
        high = got_ref[base + path_hi, :, LANES:]
        ahead = jnp.where(row == count - 1, high, pltpu.roll(mid, count - 1, 0))
        behind = jnp.where(row == 0, low, pltpu.roll(mid, 1, 0))
        edge = column * (ahead - behind) - (far + near + sides(mid) - 3.0 * mid - mid * mid * mid)
        for s in range(count):
            resid[s + 1, place : place + 1, :] = edge[s : s + 1, :]

    def residual_of(s):
        if s in (-1, count):
            slot, q = (0, path_lo) if s < 0 else (1, path_hi)
            top, bottom = got_ref[prev + q, :, LANES:], got_ref[nxt + q, :, LANES:]
        else:
            top, bottom = tail_ref[1, s : s + 1, :], head_ref[0, s : s + 1, :]
        for k in range(tiles):
            if s in (-1, count):
                c = outer[slot, at(k), :]
                above = outer[slot, TILE * k - 1 : TILE * k, :] if k > 0 else top
                under = outer[slot, TILE * (k + 1) : TILE * (k + 1) + 1, :] if k < tiles - 1 else bottom
                up = jnp.where(row == 0, above, pltpu.roll(c, 1, 0))
                dn = jnp.where(row == TILE - 1, under, pltpu.roll(c, TILE - 1, 0))
                drift = up + dn + sides(c) - 3.0 * c - c * c * c
            else:
                drift = drift_ref[s, at(k), :]
                if k == 0:
                    drift += jnp.where(row == 0, top, 0.0)
                if k == tiles - 1:
                    drift += jnp.where(row == TILE - 1, bottom, 0.0)
            resid[s + 1, at(k + 1), :] = scale[s + 1] * (value(s + 1, k) - value(s - 1, k)) - drift

    def gradient_of(s):
        for k in range(tiles):
            base = TILE * (k + 1)
            c = f_ref[s, pl.ds(TILE * k, TILE), :]
            r = resid[s + 1, pl.ds(base, TILE), :]
            around = resid[s + 1, pl.ds(base - 1, TILE), :] + resid[s + 1, pl.ds(base + 1, TILE), :] + sides(r)
            out = scale[s] * resid[s, pl.ds(base, TILE), :] - scale[s + 2] * resid[s + 2, pl.ds(base, TILE), :]
            grad[s, pl.ds(TILE * k, TILE), :] = out - (around - (3.0 + 3.0 * c * c) * r)

    copies = []

    def send(src, dst, slot):
        copy = pltpu.make_async_copy(src, dst, slot)
        copy.start()
        copies.append(copy)

    residual_of(-1)
    residual_of(0)
    for s in range(count):
        residual_of(s + 1)
        send(resid.at[s + 1, pl.ds(TILE, rows)], res_out.at[s], sem.at[0, s])
        gradient_of(s)
        send(grad.at[s], grad_out.at[s], sem.at[1, s])
    for copy in copies:
        copy.wait()


def final(m, n, got, f, drift, below, above, tail_in, head_in, start, end):
    count, rows, cols = f.shape
    big = jax.ShapeDtypeStruct(f.shape, F32)
    return pl.pallas_call(
        functools.partial(final_kernel, m, n),
        out_shape=(jax.ShapeDtypeStruct((count,), F32), big, big),
        in_specs=[VMEM] * 9,
        out_specs=(VMEM, ANY, ANY),
        scratch_shapes=[
            pltpu.VMEM((count + 2, rows + 2 * TILE, cols), F32),
            pltpu.VMEM(f.shape, F32),
            pltpu.VMEM((2, rows, cols), F32),
            pltpu.VMEM((2, count, cols), F32),
            pltpu.SemaphoreType.DMA((2, count)),
        ],
        compiler_params=PARAMS,
        name="final",
    )(got, f, drift, below, above, tail_in, head_in, start, end)


def ring(x, n, step):
    return lax.ppermute(x, "space", [(i, (i + step) % n) for i in range(n)])


def body(m, n, f, start, end):
    up, down, tail, head = edges(f)
    tail_in = ring(tail, n, 1)
    below = lax.ppermute(up, "path", [(i, i + 1) for i in range(m - 1)])
    head_in = ring(head, n, -1)
    above = lax.ppermute(down, "path", [(i + 1, i) for i in range(m - 1)])
    part, drift, rim = interior(f)
    send = chunks(m, n, f, below, tail_in, head_in, start, end, part, rim)
    got = lax.all_to_all(send, ("space", "path"), 0, 0, tiled=True)
    return final(m, n, got, f, drift, below, above, tail_in, head_in, start, end)


def solution(mesh):
    m, n = mesh.shape["path"], mesh.shape["space"]
    in_specs = (P("path", "space", None), P("space", None), P("space", None))
    out_specs = (P("path"), P("path", "space", None), P("path", "space", None))
    return jax.shard_map(
        functools.partial(body, m, n), mesh=mesh, in_specs=in_specs, out_specs=out_specs, check_vma=False
    )
```

```python
import functools

import jax
import jax.numpy as jnp
from jax import lax
from jax.experimental import pallas as pl
from jax.experimental.pallas import tpu as pltpu
from jax.sharding import PartitionSpec as P

F32 = jnp.float32
LANES = 128
TILE = 8
EPS = 1e-06
VMEM = pl.BlockSpec(memory_space=pltpu.VMEM)
ANY = pl.BlockSpec(memory_space=pl.ANY)
PARAMS = pltpu.CompilerParams(vmem_limit_bytes=16 * 2**20)


def lanes_sum(x):
    parts = [x[:, i : i + LANES] for i in range(0, x.shape[1], LANES)]
    while len(parts) > 1:
        parts = [a + b for a, b in zip(parts[::2], parts[1::2])] + parts[len(parts) & ~1 :]
    return parts[0]


def sides(x):
    cols = x.shape[1]
    return pltpu.roll(x, 1, 1) + pltpu.roll(x, cols - 1, 1)


def iota(shape, dim):
    return lax.broadcasted_iota(jnp.int32, shape, dim)


def edge_kernel(f_ref, up_ref, down_ref, tail_ref, head_ref):
    count, rows, _ = f_ref.shape
    for s in range(count):
        for r in range(2):
            tail_ref[r, s : s + 1, :] = f_ref[s, rows - 2 + r : rows - 1 + r, :]
            head_ref[r, s : s + 1, :] = f_ref[s, r : r + 1, :]
    for s in range(2):
        up_ref[s] = f_ref[count - 2 + s]
        down_ref[s] = f_ref[s]


def edges(f):
    count, rows, cols = f.shape
    pair = jax.ShapeDtypeStruct((2, rows, cols), F32)
    strip = jax.ShapeDtypeStruct((2, count, cols), F32)
    return pl.pallas_call(
        edge_kernel,
        out_shape=(pair, pair, strip, strip),
        in_specs=[VMEM],
        out_specs=(VMEM, VMEM, VMEM, VMEM),
        compiler_params=PARAMS,
        name="edges",
    )(f)


def interior_kernel(f_ref, part_ref, drift_ref, rim_ref):
    count, rows, cols = f_ref.shape
    tiles = rows // TILE
    row = iota((TILE, cols), 0)
    part_ref[...] = jnp.zeros_like(part_ref)

    def drift_sum(s, _):
        total = jnp.zeros((TILE, LANES), F32)
        for k in range(tiles):
            c = f_ref[s, pl.ds(TILE * k, TILE), :]
            above = f_ref[s, pl.ds(TILE * k - 1, 1), :] if k > 0 else 0.0
            under = f_ref[s, pl.ds(TILE * (k + 1), 1), :] if k < tiles - 1 else 0.0
            up = jnp.where(row == 0, above, pltpu.roll(c, 1, 0))
            dn = jnp.where(row == TILE - 1, under, pltpu.roll(c, TILE - 1, 0))
            drift = up + dn + sides(c) - 3.0 * c - c * c * c
            drift_ref[s, pl.ds(TILE * k, TILE), :] = drift
            if k == 0:
                rim_ref[0, pl.ds(s, 1), :] = drift[0:1]
                drift = jnp.where(row == 0, 0.0, drift)
            if k == tiles - 1:
                rim_ref[1, pl.ds(s, 1), :] = drift[TILE - 1 : TILE]
                drift = jnp.where(row == TILE - 1, 0.0, drift)
            total += lanes_sum(drift * drift)
        part_ref[pl.ds(s, 1), :] = jnp.sum(total, axis=0, keepdims=True)
        return 0

    def tangent_sum(s, _):
        total = jnp.zeros((TILE, LANES), F32)
        for k in range(tiles):
            tangent = f_ref[s + 1, pl.ds(TILE * k, TILE), :] - f_ref[s - 1, pl.ds(TILE * k, TILE), :]
            total += lanes_sum(tangent * tangent)
        part_ref[pl.ds(count + s, 1), :] = jnp.sum(total, axis=0, keepdims=True)
        return 0

    lax.fori_loop(0, count, drift_sum, 0)
    lax.fori_loop(1, count - 1, tangent_sum, 0)


def interior(f):
    count, rows, cols = f.shape
    return pl.pallas_call(
        interior_kernel,
        out_shape=(
            jax.ShapeDtypeStruct((2 * count, LANES), F32),
            jax.ShapeDtypeStruct(f.shape, F32),
            jax.ShapeDtypeStruct((2, count, cols), F32),
        ),
        in_specs=[VMEM],
        out_specs=[VMEM] * 3,
        cost_estimate=pl.CostEstimate(flops=20 * count * rows * cols, transcendentals=0, bytes_accessed=8 * count * rows * cols),
        compiler_params=PARAMS,
        name="interior",
    )(f)


def chunk_kernel(m, n, f_ref, below_ref, above_ref, tail_ref, head_ref, start_ref, end_ref, part_ref, rim_ref, out_ref):
    count, rows, cols = f_ref.shape
    tiles = rows // TILE
    path = lax.axis_index("path")
    space = lax.axis_index("space")
    first = path == 0
    last = path == m - 1

    drift_a = rim_ref[0] + tail_ref[1]
    drift_b = rim_ref[1] + head_ref[0]
    drift = part_ref[0:count, :] + lanes_sum(drift_a * drift_a) + lanes_sum(drift_b * drift_b)

    totals = [jnp.zeros((TILE, LANES), F32) for _ in range(2)]
    for k in range(tiles):
        at = pl.ds(TILE * k, TILE)
        prior = jnp.where(first, start_ref[at, :], below_ref[1, at, :])
        after = jnp.where(last, end_ref[at, :], above_ref[0, at, :])
        tangents = (f_ref[1, at, :] - prior, after - f_ref[count - 2, at, :])
        totals = [a + lanes_sum(t * t) for a, t in zip(totals, tangents)]
    head_sum, tail_sum = [jnp.sum(a, axis=0, keepdims=True) for a in totals]
    sub = iota((TILE, LANES), 0)
    tangent = part_ref[count : 2 * count, :]
    tangent = jnp.where(sub == 0, head_sum, jnp.where(sub == count - 1, tail_sum, tangent))

    lane = iota((TILE, LANES), 1)
    spread = jnp.where(lane == sub, jnp.sum(drift, axis=1, keepdims=True), 0.0)
    spread += jnp.where(lane == sub + count, jnp.sum(tangent, axis=1, keepdims=True), 0.0)
    line = jnp.sum(spread, axis=0, keepdims=True)

    for j in range(m * n):
        out_ref[j, :, 0:LANES] = line
    right = lax.rem(space + 1, n) * m
    left = lax.rem(space + n - 1, n) * m

    def put(base, source):
        out_ref[base, :, LANES:] = source

    @pl.when(jnp.logical_not(first))
    def _():
        put(right + path - 1, f_ref[0, rows - 1 : rows, :])
        put(left + path - 1, f_ref[0, 0:1, :])

    @pl.when(jnp.logical_not(last))
    def _():
        put(right + path + 1, f_ref[count - 1, rows - 1 : rows, :])
        put(left + path + 1, f_ref[count - 1, 0:1, :])

    @pl.when(first)
    def _():
        put(right + path, start_ref[rows - 1 : rows, :])
        put(left + path, start_ref[0:1, :])

    @pl.when(last)
    def _():
        put(right + path, end_ref[rows - 1 : rows, :])
        put(left + path, end_ref[0:1, :])


def chunks(m, n, f, below, above, tail_in, head_in, start, end, part, rim):
    return pl.pallas_call(
        functools.partial(chunk_kernel, m, n),
        out_shape=jax.ShapeDtypeStruct((m * n, 1, LANES + f.shape[2]), F32),
        in_specs=[VMEM] * 9,
        out_specs=VMEM,
        compiler_params=PARAMS,
        name="chunks",
    )(f, below, above, tail_in, head_in, start, end, part, rim)


def final_kernel(
    m, n, got_ref, f_ref, drift_ref, below_ref, above_ref, tail_ref, head_ref, start_ref, end_ref,
    ratio_ref, res_out, grad_out, resid, grad, outer, rim, sem,
):
    count, rows, cols = f_ref.shape
    tiles = rows // TILE
    path = lax.axis_index("path")
    space = lax.axis_index("space")
    first = path == 0
    last = path == m - 1
    path_lo = jnp.where(first, path, path - 1)
    path_hi = jnp.where(last, path, path + 1)

    def gathered(p):
        total = got_ref[p, :, 0:LANES]
        for i in range(1, n):
            total += got_ref[i * m + p, :, 0:LANES]
        return jnp.broadcast_to(total, (TILE, LANES))

    mine = gathered(path)
    lower = gathered(path_lo)
    upper = gathered(path_hi)
    lane = iota((TILE, LANES), 1)
    sub = iota((TILE, LANES), 0)

    def shift(x, k):
        return pltpu.roll(x, k % LANES, 1)

    def ratios(x):
        return jnp.sqrt(x + EPS) / jnp.sqrt(shift(x, -count) + EPS)

    low = jnp.where(first, 0.0, shift(ratios(lower), 1 - count))
    high = jnp.where(last, 0.0, shift(ratios(upper), count + 1))
    own = ratios(mine)
    ratio_ref[...] = own[0, 0:count]
    ratio = jnp.where(lane == 0, low, jnp.where(lane == count + 1, high, shift(own, 1)))

    def splat(t):
        return jnp.broadcast_to(jnp.sum(jnp.where(lane == t, ratio, 0.0), axis=1, keepdims=True), (TILE, LANES))

    def widen(x):
        return jnp.concatenate([x] * (cols // LANES), axis=1)

    scale = [widen(splat(t)) for t in range(count + 2)]
    column = jnp.sum(jnp.where(lane == sub + 1, ratio, 0.0), axis=1, keepdims=True)
    row = iota((TILE, cols), 0)
    prev = lax.rem(space + n - 1, n) * m
    nxt = lax.rem(space + 1, n) * m

    def at(k):
        return pl.ds(TILE * k, TILE)

    for k in range(tiles):
        outer[0, at(k), :] = jnp.where(first, start_ref[at(k), :], below_ref[1, at(k), :])
        outer[1, at(k), :] = jnp.where(last, end_ref[at(k), :], above_ref[0, at(k), :])

    def value(s, k):
        where = {-2: (below_ref, 0), -1: (outer, 0), count: (outer, 1), count + 1: (above_ref, 1)}
        ref, slot = where.get(s, (f_ref, s))
        return ref[slot, at(k), :]

    for s in range(count):
        rim[0, s : s + 1, :] = f_ref[s, 0:1, :]
        rim[1, s : s + 1, :] = f_ref[s, rows - 1 : rows, :]
    for far, mid, near, base, place in (
        (tail_ref[0], tail_ref[1], rim[0], prev, TILE - 1),
        (head_ref[1], head_ref[0], rim[1], nxt, TILE + rows),
    ):
        low = got_ref[base + path_lo, :, LANES:]
        high = got_ref[base + path_hi, :, LANES:]
        ahead = jnp.where(row == count - 1, high, pltpu.roll(mid, count - 1, 0))
        behind = jnp.where(row == 0, low, pltpu.roll(mid, 1, 0))
        edge = column * (ahead - behind) - (far + near + sides(mid) - 3.0 * mid - mid * mid * mid)
        for s in range(count):
            resid[s + 1, place : place + 1, :] = edge[s : s + 1, :]

    def residual_of(s):
        if s in (-1, count):
            slot, q = (0, path_lo) if s < 0 else (1, path_hi)
            top, bottom = got_ref[prev + q, :, LANES:], got_ref[nxt + q, :, LANES:]
        else:
            top, bottom = tail_ref[1, s : s + 1, :], head_ref[0, s : s + 1, :]
        for k in range(tiles):
            if s in (-1, count):
                c = outer[slot, at(k), :]
                above = outer[slot, TILE * k - 1 : TILE * k, :] if k > 0 else top
                under = outer[slot, TILE * (k + 1) : TILE * (k + 1) + 1, :] if k < tiles - 1 else bottom
                up = jnp.where(row == 0, above, pltpu.roll(c, 1, 0))
                dn = jnp.where(row == TILE - 1, under, pltpu.roll(c, TILE - 1, 0))
                drift = up + dn + sides(c) - 3.0 * c - c * c * c
            else:
                drift = drift_ref[s, at(k), :]
                if k == 0:
                    drift += jnp.where(row == 0, top, 0.0)
                if k == tiles - 1:
                    drift += jnp.where(row == TILE - 1, bottom, 0.0)
            resid[s + 1, at(k + 1), :] = scale[s + 1] * (value(s + 1, k) - value(s - 1, k)) - drift

    def gradient_of(s):
        for k in range(tiles):
            base = TILE * (k + 1)
            c = f_ref[s, pl.ds(TILE * k, TILE), :]
            r = resid[s + 1, pl.ds(base, TILE), :]
            around = resid[s + 1, pl.ds(base - 1, TILE), :] + resid[s + 1, pl.ds(base + 1, TILE), :] + sides(r)
            out = scale[s] * resid[s, pl.ds(base, TILE), :] - scale[s + 2] * resid[s + 2, pl.ds(base, TILE), :]
            grad[s, pl.ds(TILE * k, TILE), :] = out - (around - (3.0 + 3.0 * c * c) * r)

    copies = []

    def send(src, dst, slot):
        copy = pltpu.make_async_copy(src, dst, slot)
        copy.start()
        copies.append(copy)

    residual_of(-1)
    residual_of(0)
    for s in range(count):
        residual_of(s + 1)
        send(resid.at[s + 1, pl.ds(TILE, rows)], res_out.at[s], sem.at[0, s])
        gradient_of(s)
        send(grad.at[s], grad_out.at[s], sem.at[1, s])
    for copy in copies:
        copy.wait()


def final(m, n, got, f, drift, below, above, tail_in, head_in, start, end):
    count, rows, cols = f.shape
    big = jax.ShapeDtypeStruct(f.shape, F32)
    return pl.pallas_call(
        functools.partial(final_kernel, m, n),
        out_shape=(jax.ShapeDtypeStruct((count,), F32), big, big),
        in_specs=[VMEM] * 9,
        out_specs=(VMEM, ANY, ANY),
        scratch_shapes=[
            pltpu.VMEM((count + 2, rows + 2 * TILE, cols), F32),
            pltpu.VMEM(f.shape, F32),
            pltpu.VMEM((2, rows, cols), F32),
            pltpu.VMEM((2, count, cols), F32),
            pltpu.SemaphoreType.DMA((2, count)),
        ],
        compiler_params=PARAMS,
        name="final",
    )(got, f, drift, below, above, tail_in, head_in, start, end)


def ring(x, n, step):
    return lax.ppermute(x, "space", [(i, (i + step) % n) for i in range(n)])


def body(m, n, f, start, end):
    up, down, tail, head = edges(f)
    tail_in = ring(tail, n, 1)
    below = lax.ppermute(up, "path", [(i, i + 1) for i in range(m - 1)])
    head_in = ring(head, n, -1)
    above = lax.ppermute(down, "path", [(i + 1, i) for i in range(m - 1)])
    part, drift, rim = interior(f)
    send = chunks(m, n, f, below, above, tail_in, head_in, start, end, part, rim)
    got = lax.all_to_all(send, ("space", "path"), 0, 0, tiled=True)
    return final(m, n, got, f, drift, below, above, tail_in, head_in, start, end)


def solution(mesh):
    m, n = mesh.shape["path"], mesh.shape["space"]
    in_specs = (P("path", "space", None), P("space", None), P("space", None))
    out_specs = (P("path"), P("path", "space", None), P("path", "space", None))
    return jax.shard_map(
        functools.partial(body, m, n), mesh=mesh, in_specs=in_specs, out_specs=out_specs, check_vma=False
    )
```

```python
import functools

import jax
import jax.numpy as jnp
from jax import lax
from jax.experimental import pallas as pl
from jax.experimental.pallas import tpu as pltpu
from jax.sharding import PartitionSpec as P

F32 = jnp.float32
LANES = 128
TILE = 8
EPS = 1e-06
VMEM = pl.BlockSpec(memory_space=pltpu.VMEM)
ANY = pl.BlockSpec(memory_space=pl.ANY)
PARAMS = pltpu.CompilerParams(vmem_limit_bytes=16 * 2**20)


def lanes_sum(x):
    parts = [x[:, i : i + LANES] for i in range(0, x.shape[1], LANES)]
    while len(parts) > 1:
        parts = [a + b for a, b in zip(parts[::2], parts[1::2])] + parts[len(parts) & ~1 :]
    return parts[0]


def sides(x):
    cols = x.shape[1]
    return pltpu.roll(x, 1, 1) + pltpu.roll(x, cols - 1, 1)


def iota(shape, dim):
    return lax.broadcasted_iota(jnp.int32, shape, dim)


def odd(axis):
    return lax.rem(lax.axis_index(axis), 2) == 1


def pick(flag, x, y):
    return jnp.where(flag, x, y)


def edge_kernel(f_ref, start_ref, end_ref, far_ref, near_strip_ref, far_strip_ref, tiles, sem):
    count, rows, _ = f_ref.shape
    flag = odd("space")
    copies = []
    for i, at in enumerate((pl.ds(0, TILE), pl.ds(rows - TILE, TILE))):
        copies.append(pltpu.make_async_copy(f_ref.at[:, at], tiles.at[i, pl.ds(0, count)], sem.at[3 * i]))
        copies.append(pltpu.make_async_copy(start_ref.at[at], tiles.at[i, count], sem.at[3 * i + 1]))
        copies.append(pltpu.make_async_copy(end_ref.at[at], tiles.at[i, count + 1], sem.at[3 * i + 2]))
    base = pick(odd("path"), count - 2, 0)
    copies.append(pltpu.make_async_copy(f_ref.at[pl.ds(base, 2)], far_ref, sem.at[6]))
    for copy in copies:
        copy.start()
    for copy in copies[:-1]:
        copy.wait()
    for ref, low in ((near_strip_ref, flag), (far_strip_ref, jnp.logical_not(flag))):
        side = pick(low, 0, 1)
        at = pick(low, 0, TILE - 2)
        face = pick(low, 0, TILE - 1)
        ref[2] = jnp.zeros_like(ref[2])
        for i in range(2):
            ref[2, i : i + 1, :] = tiles[side, count + i, pl.ds(face, 1), :]
        for s in range(count):
            for r in range(2):
                ref[r, s : s + 1, :] = tiles[side, s, pl.ds(at + r, 1), :]
    copies[-1].wait()


def edges(f, start, end):
    count, rows, cols = f.shape
    strip = jax.ShapeDtypeStruct((3, count, cols), F32)
    return pl.pallas_call(
        edge_kernel,
        out_shape=(jax.ShapeDtypeStruct((2, rows, cols), F32), strip, strip),
        in_specs=[pl.BlockSpec(memory_space=pltpu.MemorySpace.HBM)] * 3,
        out_specs=[VMEM] * 3,
        scratch_shapes=[pltpu.VMEM((2, count + 2, TILE, cols), F32), pltpu.SemaphoreType.DMA((7,))],
        compiler_params=PARAMS,
        name="edges",
    )(f, start, end)


class Halo:
    def __init__(self, m, near_ref, far_ref, near_strip_ref, far_strip_ref, start_ref, end_ref):
        self.path, self.space = odd("path"), odd("space")
        self.first = lax.axis_index("path") == 0
        self.last = lax.axis_index("path") == m - 1
        self.near, self.far = near_ref, far_ref
        self.strips = near_strip_ref, far_strip_ref
        self.start, self.end = start_ref, end_ref

    def below(self, i, at):
        got = pick(self.path, self.near[i, at, :], self.far[i, at, :])
        return pick(self.first, self.start[at, :], got) if i else got

    def above(self, i, at):
        got = pick(self.path, self.far[i, at, :], self.near[i, at, :])
        return got if i else pick(self.last, self.end[at, :], got)

    def tail(self, *at):
        return pick(self.space, self.strips[0][at], self.strips[1][at])

    def head(self, *at):
        return pick(self.space, self.strips[1][at], self.strips[0][at])


def interior_kernel(f_ref, part_ref, drift_ref, rim_ref, near_ref):
    count, rows, cols = f_ref.shape
    tiles = rows // TILE
    row = iota((TILE, cols), 0)
    part_ref[...] = jnp.zeros_like(part_ref)
    base = pick(odd("path"), 0, count - 2)
    for s in range(2):
        near_ref[s] = f_ref[base + s]

    def drift_sum(s, _):
        total = jnp.zeros((TILE, LANES), F32)
        for k in range(tiles):
            c = f_ref[s, pl.ds(TILE * k, TILE), :]
            above = f_ref[s, pl.ds(TILE * k - 1, 1), :] if k > 0 else 0.0
            under = f_ref[s, pl.ds(TILE * (k + 1), 1), :] if k < tiles - 1 else 0.0
            up = jnp.where(row == 0, above, pltpu.roll(c, 1, 0))
            dn = jnp.where(row == TILE - 1, under, pltpu.roll(c, TILE - 1, 0))
            drift = up + dn + sides(c) - 3.0 * c - c * c * c
            drift_ref[s, pl.ds(TILE * k, TILE), :] = drift
            if k == 0:
                rim_ref[0, pl.ds(s, 1), :] = drift[0:1]
                drift = jnp.where(row == 0, 0.0, drift)
            if k == tiles - 1:
                rim_ref[1, pl.ds(s, 1), :] = drift[TILE - 1 : TILE]
                drift = jnp.where(row == TILE - 1, 0.0, drift)
            total += lanes_sum(drift * drift)
        part_ref[pl.ds(s, 1), :] = jnp.sum(total, axis=0, keepdims=True)
        return 0

    def tangent_sum(s, _):
        total = jnp.zeros((TILE, LANES), F32)
        for k in range(tiles):
            tangent = f_ref[s + 1, pl.ds(TILE * k, TILE), :] - f_ref[s - 1, pl.ds(TILE * k, TILE), :]
            total += lanes_sum(tangent * tangent)
        part_ref[pl.ds(count + s, 1), :] = jnp.sum(total, axis=0, keepdims=True)
        return 0

    lax.fori_loop(0, count, drift_sum, 0)
    lax.fori_loop(1, count - 1, tangent_sum, 0)


def interior(f):
    count, rows, cols = f.shape
    return pl.pallas_call(
        interior_kernel,
        out_shape=(
            jax.ShapeDtypeStruct((2 * count, LANES), F32),
            jax.ShapeDtypeStruct(f.shape, F32),
            jax.ShapeDtypeStruct((2, count, cols), F32),
            jax.ShapeDtypeStruct((2, rows, cols), F32),
        ),
        in_specs=[VMEM],
        out_specs=[VMEM] * 4,
        cost_estimate=pl.CostEstimate(flops=20 * count * rows * cols, transcendentals=0, bytes_accessed=8 * count * rows * cols),
        compiler_params=PARAMS,
        name="interior",
    )(f)


def chunk_kernel(m, n, f_ref, part_ref, rim_ref, *refs):
    halo_refs, (out_ref, near_corner_ref, far_corner_ref) = refs[:6], refs[6:]
    halo = Halo(m, *halo_refs)
    count, rows, cols = f_ref.shape
    tiles = rows // TILE

    for ref, low in ((near_corner_ref, halo.path), (far_corner_ref, jnp.logical_not(halo.path))):
        s = pl.ds(pick(low, 0, count - 1), 1)
        ref[0:1, :] = halo.tail(1, s)
        ref[1:2, :] = halo.head(0, s)

    drift_a = rim_ref[0] + halo.tail(1)
    drift_b = rim_ref[1] + halo.head(0)
    drift = part_ref[0:count, :] + lanes_sum(drift_a * drift_a) + lanes_sum(drift_b * drift_b)

    totals = [jnp.zeros((TILE, LANES), F32) for _ in range(2)]
    for k in range(tiles):
        at = pl.ds(TILE * k, TILE)
        tangents = (f_ref[1, at, :] - halo.below(1, at), halo.above(0, at) - f_ref[count - 2, at, :])
        totals = [a + lanes_sum(t * t) for a, t in zip(totals, tangents)]
    head_sum, tail_sum = [jnp.sum(a, axis=0, keepdims=True) for a in totals]
    sub = iota((TILE, LANES), 0)
    tangent = part_ref[count : 2 * count, :]
    tangent = jnp.where(sub == 0, head_sum, jnp.where(sub == count - 1, tail_sum, tangent))

    lane = iota((TILE, LANES), 1)
    spread = jnp.where(lane == sub, jnp.sum(drift, axis=1, keepdims=True), 0.0)
    spread += jnp.where(lane == sub + count, jnp.sum(tangent, axis=1, keepdims=True), 0.0)
    line = jnp.sum(spread, axis=0, keepdims=True)

    for j in range(m * n):
        out_ref[j] = line


def chunks(m, n, f, part, rim, halo):
    cols = f.shape[2]
    corner = jax.ShapeDtypeStruct((2, cols), F32)
    return pl.pallas_call(
        functools.partial(chunk_kernel, m, n),
        out_shape=(jax.ShapeDtypeStruct((m * n, 1, LANES), F32), corner, corner),
        in_specs=[VMEM] * 9,
        out_specs=[VMEM] * 3,
        compiler_params=PARAMS,
        name="chunks",
    )(f, part, rim, *halo)


def final_kernel(m, n, got_ref, near_corner_ref, far_corner_ref, f_ref, drift_ref, *refs):
    halo_refs, (ratio_ref, res_out, grad_out, resid, grad, outer, rim, sem) = refs[:6], refs[6:]
    halo = Halo(m, *halo_refs)
    count, rows, cols = f_ref.shape
    tiles = rows // TILE
    path = lax.axis_index("path")
    first, last = halo.first, halo.last
    path_lo = jnp.where(first, path, path - 1)
    path_hi = jnp.where(last, path, path + 1)

    def gathered(p):
        total = got_ref[p]
        for i in range(1, n):
            total += got_ref[i * m + p]
        return jnp.broadcast_to(total, (TILE, LANES))

    mine = gathered(path)
    lower = gathered(path_lo)
    upper = gathered(path_hi)
    lane = iota((TILE, LANES), 1)
    sub = iota((TILE, LANES), 0)

    def shift(x, k):
        return pltpu.roll(x, k % LANES, 1)

    def ratios(x):
        return jnp.sqrt(x + EPS) / jnp.sqrt(shift(x, -count) + EPS)

    low = jnp.where(first, 0.0, shift(ratios(lower), 1 - count))
    high = jnp.where(last, 0.0, shift(ratios(upper), count + 1))
    own = ratios(mine)
    ratio_ref[...] = own[0, 0:count]
    ratio = jnp.where(lane == 0, low, jnp.where(lane == count + 1, high, shift(own, 1)))

    def splat(t):
        return jnp.broadcast_to(jnp.sum(jnp.where(lane == t, ratio, 0.0), axis=1, keepdims=True), (TILE, LANES))

    def widen(x):
        return jnp.concatenate([x] * (cols // LANES), axis=1)

    scale = [widen(splat(t)) for t in range(count + 2)]
    column = jnp.sum(jnp.where(lane == sub + 1, ratio, 0.0), axis=1, keepdims=True)
    row = iota((TILE, cols), 0)
    fixed = halo.tail(2), halo.head(2)
    corners = []
    for i in range(2):
        near, far = near_corner_ref[i : i + 1, :], far_corner_ref[i : i + 1, :]
        low = pick(first, fixed[i][0:1], pick(halo.path, near, far))
        high = pick(last, fixed[i][1:2], pick(halo.path, far, near))
        corners.append((low, high))

    def at(k):
        return pl.ds(TILE * k, TILE)

    for k in range(tiles):
        outer[0, at(k), :] = halo.below(1, at(k))
        outer[1, at(k), :] = halo.above(0, at(k))

    def value(s, k):
        if s == -2:
            return halo.below(0, at(k))
        if s == count + 1:
            return halo.above(1, at(k))
        ref, slot = {-1: (outer, 0), count: (outer, 1)}.get(s, (f_ref, s))
        return ref[slot, at(k), :]

    for s in range(count):
        rim[0, s : s + 1, :] = f_ref[s, 0:1, :]
        rim[1, s : s + 1, :] = f_ref[s, rows - 1 : rows, :]
    for far, mid, near, (low, high), place in (
        (halo.tail(0), halo.tail(1), rim[0], corners[0], TILE - 1),
        (halo.head(1), halo.head(0), rim[1], corners[1], TILE + rows),
    ):
        ahead = jnp.where(row == count - 1, high, pltpu.roll(mid, count - 1, 0))
        behind = jnp.where(row == 0, low, pltpu.roll(mid, 1, 0))
        edge = column * (ahead - behind) - (far + near + sides(mid) - 3.0 * mid - mid * mid * mid)
        for s in range(count):
            resid[s + 1, place : place + 1, :] = edge[s : s + 1, :]

    def residual_of(s):
        if s in (-1, count):
            slot = 0 if s < 0 else 1
            top, bottom = corners[0][slot], corners[1][slot]
        else:
            top, bottom = halo.tail(1, pl.ds(s, 1)), halo.head(0, pl.ds(s, 1))
        for k in range(tiles):
            if s in (-1, count):
                c = outer[slot, at(k), :]
                above = outer[slot, TILE * k - 1 : TILE * k, :] if k > 0 else top
                under = outer[slot, TILE * (k + 1) : TILE * (k + 1) + 1, :] if k < tiles - 1 else bottom
                up = jnp.where(row == 0, above, pltpu.roll(c, 1, 0))
                dn = jnp.where(row == TILE - 1, under, pltpu.roll(c, TILE - 1, 0))
                drift = up + dn + sides(c) - 3.0 * c - c * c * c
            else:
                drift = drift_ref[s, at(k), :]
                if k == 0:
                    drift += jnp.where(row == 0, top, 0.0)
                if k == tiles - 1:
                    drift += jnp.where(row == TILE - 1, bottom, 0.0)
            resid[s + 1, at(k + 1), :] = scale[s + 1] * (value(s + 1, k) - value(s - 1, k)) - drift

    def gradient_of(s):
        for k in range(tiles):
            base = TILE * (k + 1)
            c = f_ref[s, pl.ds(TILE * k, TILE), :]
            r = resid[s + 1, pl.ds(base, TILE), :]
            around = resid[s + 1, pl.ds(base - 1, TILE), :] + resid[s + 1, pl.ds(base + 1, TILE), :] + sides(r)
            out = scale[s] * resid[s, pl.ds(base, TILE), :] - scale[s + 2] * resid[s + 2, pl.ds(base, TILE), :]
            grad[s, pl.ds(TILE * k, TILE), :] = out - (around - (3.0 + 3.0 * c * c) * r)

    copies = []

    def send(src, dst, slot):
        copy = pltpu.make_async_copy(src, dst, slot)
        copy.start()
        copies.append(copy)

    residual_of(-1)
    residual_of(0)
    for s in range(count):
        residual_of(s + 1)
        send(resid.at[s + 1, pl.ds(TILE, rows)], res_out.at[s], sem.at[0, s])
        gradient_of(s)
        send(grad.at[s], grad_out.at[s], sem.at[1, s])
    for copy in copies:
        copy.wait()


def final(m, n, got, corners, f, drift, halo):
    count, rows, cols = f.shape
    big = jax.ShapeDtypeStruct(f.shape, F32)
    return pl.pallas_call(
        functools.partial(final_kernel, m, n),
        out_shape=(jax.ShapeDtypeStruct((count,), F32), big, big),
        in_specs=[VMEM] * 11,
        out_specs=(VMEM, ANY, ANY),
        scratch_shapes=[
            pltpu.VMEM((count + 2, rows + 2 * TILE, cols), F32),
            pltpu.VMEM(f.shape, F32),
            pltpu.VMEM((2, rows, cols), F32),
            pltpu.VMEM((2, count, cols), F32),
            pltpu.SemaphoreType.DMA((2, count)),
        ],
        compiler_params=PARAMS,
        name="final",
    )(got, *corners, f, drift, *halo)


def swap(x, axis, kind, wrap):
    size = lax.axis_size(axis)
    pairs = [(i, i ^ 1) for i in range(size)]
    if kind == 1:
        pairs = [((i + 1) % size, (j + 1) % size) for i, j in pairs]
        pairs = [(i, j) for i, j in pairs if wrap or abs(i - j) == 1]
    return lax.ppermute(x, axis, pairs)


def body(m, n, f, start, end):
    far, near_strip, far_strip = edges(f, start, end)
    far = swap(far, "path", 1, False)
    far_strip = swap(far_strip, "space", 1, True)
    near_strip = swap(near_strip, "space", 0, True)
    part, drift, rim, near = interior(f)
    near = swap(near, "path", 0, False)
    halo = near, far, near_strip, far_strip, start, end
    send, near_corner, far_corner = chunks(m, n, f, part, rim, halo)
    got = lax.all_to_all(send, ("space", "path"), 0, 0, tiled=True)
    corners = swap(near_corner, "path", 0, False), swap(far_corner, "path", 1, False)
    return final(m, n, got, corners, f, drift, halo)


def solution(mesh):
    m, n = mesh.shape["path"], mesh.shape["space"]
    in_specs = (P("path", "space", None), P("space", None), P("space", None))
    out_specs = (P("path"), P("path", "space", None), P("path", "space", None))
    return jax.shard_map(
        functools.partial(body, m, n), mesh=mesh, in_specs=in_specs, out_specs=out_specs, check_vma=False
    )
```

```python
import functools

import jax
import jax.numpy as jnp
from jax import lax
from jax.experimental import pallas as pl
from jax.experimental.pallas import tpu as pltpu
from jax.sharding import PartitionSpec as P

F32 = jnp.float32
LANES = 128
TILE = 8
EPS = 1e-06
VMEM = pl.BlockSpec(memory_space=pltpu.VMEM)
ANY = pl.BlockSpec(memory_space=pl.ANY)
EDGE_VMEM = 66_200_000
PARAMS = pltpu.CompilerParams(vmem_limit_bytes=16 * 2**20)


def lanes_sum(x):
    parts = [x[:, i : i + LANES] for i in range(0, x.shape[1], LANES)]
    while len(parts) > 1:
        parts = [a + b for a, b in zip(parts[::2], parts[1::2])] + parts[len(parts) & ~1 :]
    return parts[0]


def sides(x):
    cols = x.shape[1]
    return pltpu.roll(x, 1, 1) + pltpu.roll(x, cols - 1, 1)


def iota(shape, dim):
    return lax.broadcasted_iota(jnp.int32, shape, dim)


def odd(axis):
    return lax.rem(lax.axis_index(axis), 2) == 1


def edge_kernel(f_ref, start_ref, end_ref, up_ref, down_ref, tail_ref, head_ref, tiles, sem):
    count, rows, _ = f_ref.shape
    sides_at = pl.ds(rows - TILE, TILE), pl.ds(0, TILE)
    copies = [pltpu.make_async_copy(f_ref.at[pl.ds(count - 2, 2)], up_ref, sem.at[0])]
    for i, at in enumerate(sides_at):
        copies.append(pltpu.make_async_copy(f_ref.at[:, at], tiles.at[i, pl.ds(0, count)], sem.at[3 * i + 1]))
        copies.append(pltpu.make_async_copy(start_ref.at[at], tiles.at[i, count], sem.at[3 * i + 2]))
        copies.append(pltpu.make_async_copy(end_ref.at[at], tiles.at[i, count + 1], sem.at[3 * i + 3]))
    copies.append(pltpu.make_async_copy(f_ref.at[pl.ds(0, 2)], down_ref, sem.at[7]))
    for copy in copies:
        copy.start()
    for copy in copies[1:7]:
        copy.wait()
    for i, (ref, at, face) in enumerate(((tail_ref, TILE - 2, TILE - 1), (head_ref, 0, 0))):
        ref[2] = jnp.zeros_like(ref[2])
        for j in range(2):
            ref[2, j : j + 1, :] = tiles[i, count + j, face : face + 1, :]
        for s in range(count):
            for r in range(2):
                ref[r, s : s + 1, :] = tiles[i, s, at + r : at + r + 1, :]
    copies[0].wait()
    copies[7].wait()


def edges(f, start, end):
    count, rows, cols = f.shape
    pair = jax.ShapeDtypeStruct((2, rows, cols), F32)
    strip = jax.ShapeDtypeStruct((3, count, cols), F32)
    return pl.pallas_call(
        edge_kernel,
        out_shape=(pair, pair, strip, strip),
        in_specs=[ANY] * 3,
        out_specs=[VMEM] * 4,
        scratch_shapes=[pltpu.VMEM((2, count + 2, TILE, cols), F32), pltpu.SemaphoreType.DMA((8,))],
        compiler_params=pltpu.CompilerParams(vmem_limit_bytes=EDGE_VMEM),
        name="edges",
    )(f, start, end)


def interior_kernel(f_ref, part_ref, drift_ref, rim_ref):
    count, rows, cols = f_ref.shape
    tiles = rows // TILE
    row = iota((TILE, cols), 0)
    part_ref[...] = jnp.zeros_like(part_ref)

    def drift_sum(s, _):
        total = jnp.zeros((TILE, LANES), F32)
        for k in range(tiles):
            c = f_ref[s, pl.ds(TILE * k, TILE), :]
            above = f_ref[s, pl.ds(TILE * k - 1, 1), :] if k > 0 else 0.0
            under = f_ref[s, pl.ds(TILE * (k + 1), 1), :] if k < tiles - 1 else 0.0
            up = jnp.where(row == 0, above, pltpu.roll(c, 1, 0))
            dn = jnp.where(row == TILE - 1, under, pltpu.roll(c, TILE - 1, 0))
            drift = up + dn + sides(c) - 3.0 * c - c * c * c
            drift_ref[s, pl.ds(TILE * k, TILE), :] = drift
            if k == 0:
                rim_ref[0, pl.ds(s, 1), :] = drift[0:1]
                drift = jnp.where(row == 0, 0.0, drift)
            if k == tiles - 1:
                rim_ref[1, pl.ds(s, 1), :] = drift[TILE - 1 : TILE]
                drift = jnp.where(row == TILE - 1, 0.0, drift)
            total += lanes_sum(drift * drift)
        part_ref[pl.ds(s, 1), :] = jnp.sum(total, axis=0, keepdims=True)
        return 0

    def tangent_sum(s, _):
        total = jnp.zeros((TILE, LANES), F32)
        for k in range(tiles):
            tangent = f_ref[s + 1, pl.ds(TILE * k, TILE), :] - f_ref[s - 1, pl.ds(TILE * k, TILE), :]
            total += lanes_sum(tangent * tangent)
        part_ref[pl.ds(count + s + 1, 1), :] = jnp.sum(total, axis=0, keepdims=True)
        return 0

    lax.fori_loop(0, count, drift_sum, 0)
    lax.fori_loop(1, count - 1, tangent_sum, 0)


def interior(f):
    count, rows, cols = f.shape
    return pl.pallas_call(
        interior_kernel,
        out_shape=(
            jax.ShapeDtypeStruct((2 * count + TILE, LANES), F32),
            jax.ShapeDtypeStruct(f.shape, F32),
            jax.ShapeDtypeStruct((2, count, cols), F32),
        ),
        in_specs=[VMEM],
        out_specs=[VMEM] * 3,
        cost_estimate=pl.CostEstimate(flops=20 * count * rows * cols, transcendentals=0, bytes_accessed=8 * count * rows * cols),
        compiler_params=PARAMS,
        name="interior",
    )(f)


def chunk_kernel(
    m, n, f_ref, below_ref, tail_ref, head_ref, start_ref, end_ref, part_ref, rim_ref,
    out_ref, near_corner_ref, far_corner_ref,
):
    count, rows, cols = f_ref.shape
    tiles = rows // TILE
    path = lax.axis_index("path")
    first = path == 0
    last = path == m - 1

    flag = odd("path")
    for ref, low in ((near_corner_ref, flag), (far_corner_ref, jnp.logical_not(flag))):
        s = pl.ds(jnp.where(low, 0, count - 1), 1)
        ref[0:1, :] = tail_ref[1, s, :]
        ref[1:2, :] = head_ref[0, s, :]

    drift_a = rim_ref[0] + tail_ref[1]
    drift_b = rim_ref[1] + head_ref[0]
    drift = part_ref[0:count, :] + lanes_sum(drift_a * drift_a) + lanes_sum(drift_b * drift_b)

    totals = [jnp.zeros((TILE, LANES), F32) for _ in range(3)]
    for k in range(tiles):
        at = pl.ds(TILE * k, TILE)
        prior = jnp.where(first, start_ref[at, :], below_ref[1, at, :])
        tangents = (
            f_ref[0, at, :] - below_ref[0, at, :],
            f_ref[1, at, :] - prior,
            jnp.where(last, end_ref[at, :] - f_ref[count - 2, at, :], 0.0),
        )
        totals = [a + lanes_sum(t * t) for a, t in zip(totals, tangents)]
    sums = [jnp.sum(a, axis=0, keepdims=True) for a in totals]
    sub = iota((TILE, LANES), 0)
    tan_a = part_ref[count : count + TILE, :]
    tan_a = jnp.where(sub == 0, sums[0], jnp.where(sub == 1, sums[1], tan_a))

    lane = iota((TILE, LANES), 1)
    spread = jnp.where(lane == sub, jnp.sum(drift, axis=1, keepdims=True), 0.0)
    spread += jnp.where(lane == sub + count, jnp.sum(tan_a, axis=1, keepdims=True), 0.0)
    line = jnp.sum(spread, axis=0, keepdims=True)
    tan_last = jnp.sum(sums[2], axis=1, keepdims=True)
    line += jnp.where(lane[0:1] == 2 * count, tan_last, 0.0)

    for j in range(m * n):
        out_ref[j] = line


def chunks(m, n, f, below, tail_in, head_in, start, end, part, rim):
    corner = jax.ShapeDtypeStruct((2, f.shape[2]), F32)
    return pl.pallas_call(
        functools.partial(chunk_kernel, m, n),
        out_shape=(jax.ShapeDtypeStruct((m * n, 1, LANES), F32), corner, corner),
        in_specs=[VMEM] * 8,
        out_specs=[VMEM] * 3,
        compiler_params=PARAMS,
        name="chunks",
    )(f, below, tail_in, head_in, start, end, part, rim)


def final_kernel(
    m, n, got_ref, near_corner_ref, far_corner_ref, f_ref, drift_ref, below_ref, above_ref, tail_ref, head_ref, start_ref, end_ref,
    ratio_ref, res_out, grad_out, resid, grad, outer, rim, sem,
):
    count, rows, cols = f_ref.shape
    tiles = rows // TILE
    path = lax.axis_index("path")
    first = path == 0
    last = path == m - 1
    path_lo = jnp.where(first, path, path - 1)
    path_hi = jnp.where(last, path, path + 1)

    def gathered(p):
        total = got_ref[p]
        for i in range(1, n):
            total += got_ref[i * m + p]
        return jnp.broadcast_to(total, (TILE, LANES))

    mine = gathered(path)
    lower = gathered(path_lo)
    upper = gathered(path_hi)
    lane = iota((TILE, LANES), 1)
    sub = iota((TILE, LANES), 0)

    def shift(x, k):
        return pltpu.roll(x, k % LANES, 1)

    drift_sq = jnp.where(lane == 0, shift(lower, 1 - count), jnp.where(lane <= count, shift(mine, 1), shift(upper, count + 1)))
    at_end = shift(mine, -count) + jnp.where(last, 0.0, upper)
    tangent_sq = jnp.where(lane < count, shift(mine, -count), jnp.where(lane == count, at_end, upper))
    ratio = jnp.sqrt(drift_sq + EPS) / jnp.sqrt(tangent_sq + EPS)
    ratio = jnp.where((lane == 0) & first, 0.0, ratio)
    ratio = jnp.where((lane == count + 1) & last, 0.0, ratio)
    ratio_ref[...] = shift(ratio, -1)[0, 0:count]

    def splat(t):
        return jnp.broadcast_to(jnp.sum(jnp.where(lane == t, ratio, 0.0), axis=1, keepdims=True), (TILE, LANES))

    def widen(x):
        return jnp.concatenate([x] * (cols // LANES), axis=1)

    scale = [widen(splat(t)) for t in range(count + 2)]
    column = jnp.sum(jnp.where(lane == sub + 1, ratio, 0.0), axis=1, keepdims=True)
    row = iota((TILE, cols), 0)
    flag = odd("path")
    corners = []
    for i, fixed in enumerate((tail_ref, head_ref)):
        near, far = near_corner_ref[i : i + 1, :], far_corner_ref[i : i + 1, :]
        low = jnp.where(first, fixed[2, 0:1, :], jnp.where(flag, near, far))
        high = jnp.where(last, fixed[2, 1:2, :], jnp.where(flag, far, near))
        corners.append((low, high))

    def at(k):
        return pl.ds(TILE * k, TILE)

    for k in range(tiles):
        outer[0, at(k), :] = jnp.where(first, start_ref[at(k), :], below_ref[1, at(k), :])
        outer[1, at(k), :] = jnp.where(last, end_ref[at(k), :], above_ref[0, at(k), :])

    def value(s, k):
        where = {-2: (below_ref, 0), -1: (outer, 0), count: (outer, 1), count + 1: (above_ref, 1)}
        ref, slot = where.get(s, (f_ref, s))
        return ref[slot, at(k), :]

    for s in range(count):
        rim[0, s : s + 1, :] = f_ref[s, 0:1, :]
        rim[1, s : s + 1, :] = f_ref[s, rows - 1 : rows, :]
    for far, mid, near, (low, high), place in (
        (tail_ref[0], tail_ref[1], rim[0], corners[0], TILE - 1),
        (head_ref[1], head_ref[0], rim[1], corners[1], TILE + rows),
    ):
        ahead = jnp.where(row == count - 1, high, pltpu.roll(mid, count - 1, 0))
        behind = jnp.where(row == 0, low, pltpu.roll(mid, 1, 0))
        edge = column * (ahead - behind) - (far + near + sides(mid) - 3.0 * mid - mid * mid * mid)
        for s in range(count):
            resid[s + 1, place : place + 1, :] = edge[s : s + 1, :]

    def residual_of(s):
        if s in (-1, count):
            slot = 0 if s < 0 else 1
            top, bottom = corners[0][slot], corners[1][slot]
        else:
            top, bottom = tail_ref[1, s : s + 1, :], head_ref[0, s : s + 1, :]
        for k in range(tiles):
            if s in (-1, count):
                c = outer[slot, at(k), :]
                above = outer[slot, TILE * k - 1 : TILE * k, :] if k > 0 else top
                under = outer[slot, TILE * (k + 1) : TILE * (k + 1) + 1, :] if k < tiles - 1 else bottom
                up = jnp.where(row == 0, above, pltpu.roll(c, 1, 0))
                dn = jnp.where(row == TILE - 1, under, pltpu.roll(c, TILE - 1, 0))
                drift = up + dn + sides(c) - 3.0 * c - c * c * c
            else:
                drift = drift_ref[s, at(k), :]
                if k == 0:
                    drift += jnp.where(row == 0, top, 0.0)
                if k == tiles - 1:
                    drift += jnp.where(row == TILE - 1, bottom, 0.0)
            resid[s + 1, at(k + 1), :] = scale[s + 1] * (value(s + 1, k) - value(s - 1, k)) - drift

    def gradient_of(s):
        for k in range(tiles):
            base = TILE * (k + 1)
            c = f_ref[s, pl.ds(TILE * k, TILE), :]
            r = resid[s + 1, pl.ds(base, TILE), :]
            around = resid[s + 1, pl.ds(base - 1, TILE), :] + resid[s + 1, pl.ds(base + 1, TILE), :] + sides(r)
            out = scale[s] * resid[s, pl.ds(base, TILE), :] - scale[s + 2] * resid[s + 2, pl.ds(base, TILE), :]
            grad[s, pl.ds(TILE * k, TILE), :] = out - (around - (3.0 + 3.0 * c * c) * r)

    copies = []

    def send(src, dst, slot):
        copy = pltpu.make_async_copy(src, dst, slot)
        copy.start()
        copies.append(copy)

    residual_of(-1)
    residual_of(0)
    for s in range(count):
        residual_of(s + 1)
        send(resid.at[s + 1, pl.ds(TILE, rows)], res_out.at[s], sem.at[0, s])
        gradient_of(s)
        send(grad.at[s], grad_out.at[s], sem.at[1, s])
    for copy in copies:
        copy.wait()


def final(m, n, got, corners, f, drift, below, above, tail_in, head_in, start, end):
    count, rows, cols = f.shape
    big = jax.ShapeDtypeStruct(f.shape, F32)
    return pl.pallas_call(
        functools.partial(final_kernel, m, n),
        out_shape=(jax.ShapeDtypeStruct((count,), F32), big, big),
        in_specs=[VMEM] * 11,
        out_specs=(VMEM, ANY, ANY),
        scratch_shapes=[
            pltpu.VMEM((count + 2, rows + 2 * TILE, cols), F32),
            pltpu.VMEM(f.shape, F32),
            pltpu.VMEM((2, rows, cols), F32),
            pltpu.VMEM((2, count, cols), F32),
            pltpu.SemaphoreType.DMA((2, count)),
        ],
        compiler_params=PARAMS,
        name="final",
    )(got, *corners, f, drift, below, above, tail_in, head_in, start, end)


def ring(x, axis, step):
    size = lax.axis_size(axis)
    return lax.ppermute(x, axis, [(i, (i + step) % size) for i in range(size)])


def swap(x, axis, kind):
    size = lax.axis_size(axis)
    return lax.ppermute(x, axis, [((i + kind) % size, ((i ^ 1) + kind) % size) for i in range(size)])


def body(m, n, f, start, end):
    up, down, tail, head = edges(f, start, end)
    tail_in = ring(tail, "space", 1)
    below = ring(up, "path", 1)
    head_in = ring(head, "space", -1)
    above = ring(down, "path", -1)
    part, drift, rim = interior(f)
    send, near_corner, far_corner = chunks(m, n, f, below, tail_in, head_in, start, end, part, rim)
    got = lax.all_to_all(send, ("space", "path"), 0, 0, tiled=True)
    corners = swap(near_corner, "path", 0), swap(far_corner, "path", 1)
    return final(m, n, got, corners, f, drift, below, above, tail_in, head_in, start, end)


def solution(mesh):
    m, n = mesh.shape["path"], mesh.shape["space"]
    in_specs = (P("path", "space", None), P("space", None), P("space", None))
    out_specs = (P("path"), P("path", "space", None), P("path", "space", None))
    return jax.shard_map(
        functools.partial(body, m, n), mesh=mesh, in_specs=in_specs, out_specs=out_specs, check_vma=False
    )
```

```python
import functools

import jax
import jax.numpy as jnp
from jax import lax
from jax.experimental import pallas as pl
from jax.experimental.pallas import tpu as pltpu
from jax.sharding import PartitionSpec as P

F32 = jnp.float32
LANES = 128
TILE = 8
EPS = 1e-06
VMEM = pl.BlockSpec(memory_space=pltpu.VMEM)
ANY = pl.BlockSpec(memory_space=pl.ANY)
FAR_TILES = 4
PARAMS = pltpu.CompilerParams(vmem_limit_bytes=16 * 2**20)


def lanes_sum(x):
    parts = [x[:, i : i + LANES] for i in range(0, x.shape[1], LANES)]
    while len(parts) > 1:
        parts = [a + b for a, b in zip(parts[::2], parts[1::2])] + parts[len(parts) & ~1 :]
    return parts[0]


def sides(x):
    cols = x.shape[1]
    return pltpu.roll(x, 1, 1) + pltpu.roll(x, cols - 1, 1)


def iota(shape, dim):
    return lax.broadcasted_iota(jnp.int32, shape, dim)


def odd(axis):
    return lax.rem(lax.axis_index(axis), 2) == 1


def pick(flag, x, y):
    return jnp.where(flag, x, y)


def slices_kernel(f_ref, near_ref, far_ref):
    count = f_ref.shape[0]
    flag = odd("path")
    base = pick(flag, 0, count - 2)
    for s in range(2):
        near_ref[s] = f_ref[base + s]
    far_ref[...] = f_ref[pick(flag, count - 1, 0)]


def strips_kernel(f_ref, start_ref, end_ref, near_ref, far_ref):
    count, rows, _ = f_ref.shape
    flag = odd("space")
    for ref, low in ((near_ref, flag), (far_ref, jnp.logical_not(flag))):
        at = pick(low, 0, rows - 2)
        face = pl.ds(pick(low, 0, rows - 1), 1)
        ref[2:] = jnp.zeros_like(ref[2:])
        ref[2, 0:1, :] = start_ref[face, :]
        ref[2, 1:2, :] = end_ref[face, :]
        for s in range(count):
            for r in range(2):
                ref[r, s : s + 1, :] = f_ref[s, pl.ds(at + r, 1), :]


def slices(f):
    count, rows, cols = f.shape
    return pl.pallas_call(
        slices_kernel,
        out_shape=(jax.ShapeDtypeStruct((2, rows, cols), F32), jax.ShapeDtypeStruct((rows, cols), F32)),
        in_specs=[VMEM],
        out_specs=[VMEM] * 2,
        compiler_params=PARAMS,
        name="slices",
    )(f)


def strips(f, start, end):
    count, rows, cols = f.shape
    return pl.pallas_call(
        strips_kernel,
        out_shape=tuple(jax.ShapeDtypeStruct((k, count, cols), F32) for k in (3, FAR_TILES)),
        in_specs=[VMEM] * 3,
        out_specs=[VMEM] * 2,
        compiler_params=PARAMS,
        name="strips",
    )(f, start, end)


class Halo:
    def __init__(self, m, near_ref, far_ref, near_strip_ref, far_strip_ref, start_ref, end_ref, far_b_ref=None):
        self.path, self.space = odd("path"), odd("space")
        self.first = lax.axis_index("path") == 0
        self.last = lax.axis_index("path") == m - 1
        self.near, self.far, self.far_b = near_ref, far_ref, far_b_ref
        self.strips = near_strip_ref, far_strip_ref
        self.start, self.end = start_ref, end_ref

    def below(self, at):
        return pick(self.first, self.start[at, :], pick(self.path, self.near[1, at, :], self.far[at, :]))

    def above(self, at):
        return pick(self.last, self.end[at, :], pick(self.path, self.far[at, :], self.near[0, at, :]))

    def below_2(self, at):
        return pick(self.path, self.near[0, at, :], self.far_b[at, :])

    def above_2(self, at):
        return pick(self.path, self.far_b[at, :], self.near[1, at, :])

    def tail(self, *at):
        return pick(self.space, self.strips[0][at], self.strips[1][at])

    def head(self, *at):
        return pick(self.space, self.strips[1][at], self.strips[0][at])


def interior_kernel(f_ref, part_ref, drift_ref, rim_ref):
    count, rows, cols = f_ref.shape
    tiles = rows // TILE
    row = iota((TILE, cols), 0)
    part_ref[...] = jnp.zeros_like(part_ref)

    def drift_sum(s, _):
        total = jnp.zeros((TILE, LANES), F32)
        for k in range(tiles):
            c = f_ref[s, pl.ds(TILE * k, TILE), :]
            above = f_ref[s, pl.ds(TILE * k - 1, 1), :] if k > 0 else 0.0
            under = f_ref[s, pl.ds(TILE * (k + 1), 1), :] if k < tiles - 1 else 0.0
            up = jnp.where(row == 0, above, pltpu.roll(c, 1, 0))
            dn = jnp.where(row == TILE - 1, under, pltpu.roll(c, TILE - 1, 0))
            drift = up + dn + sides(c) - 3.0 * c - c * c * c
            drift_ref[s, pl.ds(TILE * k, TILE), :] = drift
            if k == 0:
                rim_ref[0, pl.ds(s, 1), :] = drift[0:1]
                drift = jnp.where(row == 0, 0.0, drift)
            if k == tiles - 1:
                rim_ref[1, pl.ds(s, 1), :] = drift[TILE - 1 : TILE]
                drift = jnp.where(row == TILE - 1, 0.0, drift)
            total += lanes_sum(drift * drift)
        part_ref[pl.ds(s, 1), :] = jnp.sum(total, axis=0, keepdims=True)
        return 0

    def tangent_sum(s, _):
        total = jnp.zeros((TILE, LANES), F32)
        for k in range(tiles):
            tangent = f_ref[s + 1, pl.ds(TILE * k, TILE), :] - f_ref[s - 1, pl.ds(TILE * k, TILE), :]
            total += lanes_sum(tangent * tangent)
        part_ref[pl.ds(count + s, 1), :] = jnp.sum(total, axis=0, keepdims=True)
        return 0

    lax.fori_loop(0, count, drift_sum, 0)
    lax.fori_loop(1, count - 1, tangent_sum, 0)


def interior(f):
    count, rows, cols = f.shape
    return pl.pallas_call(
        interior_kernel,
        out_shape=(
            jax.ShapeDtypeStruct((2 * count, LANES), F32),
            jax.ShapeDtypeStruct(f.shape, F32),
            jax.ShapeDtypeStruct((2, count, cols), F32),
        ),
        in_specs=[VMEM],
        out_specs=[VMEM] * 3,
        cost_estimate=pl.CostEstimate(flops=20 * count * rows * cols, transcendentals=0, bytes_accessed=8 * count * rows * cols),
        compiler_params=PARAMS,
        name="interior",
    )(f)


def chunk_kernel(m, n, f_ref, part_ref, rim_ref, *refs):
    halo_refs, (out_ref, near_corner_ref, far_b_ref) = refs[:6], refs[6:]
    halo = Halo(m, *halo_refs)
    count, rows, cols = f_ref.shape
    tiles = rows // TILE

    for ref, low, at in ((near_corner_ref, halo.path, 0), (far_b_ref, jnp.logical_not(halo.path), rows)):
        s = pl.ds(pick(low, 0, count - 1), 1)
        ref[at : at + 1, :] = halo.tail(1, s)
        ref[at + 1 : at + 2, :] = halo.head(0, s)
    far_b_ref[0:rows, :] = f_ref[pick(halo.path, count - 2, 1)]
    far_b_ref[rows + 2 :, :] = jnp.zeros((TILE - 2, cols), F32)

    drift_a = rim_ref[0] + halo.tail(1)
    drift_b = rim_ref[1] + halo.head(0)
    drift = part_ref[0:count, :] + lanes_sum(drift_a * drift_a) + lanes_sum(drift_b * drift_b)

    totals = [jnp.zeros((TILE, LANES), F32) for _ in range(2)]
    for k in range(tiles):
        at = pl.ds(TILE * k, TILE)
        tangents = (f_ref[1, at, :] - halo.below(at), halo.above(at) - f_ref[count - 2, at, :])
        totals = [a + lanes_sum(t * t) for a, t in zip(totals, tangents)]
    head_sum, tail_sum = [jnp.sum(a, axis=0, keepdims=True) for a in totals]
    sub = iota((TILE, LANES), 0)
    tangent = part_ref[count : 2 * count, :]
    tangent = jnp.where(sub == 0, head_sum, jnp.where(sub == count - 1, tail_sum, tangent))

    lane = iota((TILE, LANES), 1)
    spread = jnp.where(lane == sub, jnp.sum(drift, axis=1, keepdims=True), 0.0)
    spread += jnp.where(lane == sub + count, jnp.sum(tangent, axis=1, keepdims=True), 0.0)
    line = jnp.sum(spread, axis=0, keepdims=True)

    for j in range(m * n):
        out_ref[j] = line


def chunks(m, n, f, part, rim, halo):
    _, rows, cols = f.shape
    return pl.pallas_call(
        functools.partial(chunk_kernel, m, n),
        out_shape=(
            jax.ShapeDtypeStruct((m * n, 1, LANES), F32),
            jax.ShapeDtypeStruct((2, cols), F32),
            jax.ShapeDtypeStruct((rows + TILE, cols), F32),
        ),
        in_specs=[VMEM] * 9,
        out_specs=[VMEM] * 3,
        compiler_params=PARAMS,
        name="chunks",
    )(f, part, rim, *halo)


def final_kernel(m, n, got_ref, near_corner_ref, far_b_ref, f_ref, drift_ref, *refs):
    halo_refs, (ratio_ref, res_out, grad_out, resid, grad, outer, rim, sem) = refs[:6], refs[6:]
    halo = Halo(m, *halo_refs, far_b_ref)
    count, rows, cols = f_ref.shape
    tiles = rows // TILE
    path = lax.axis_index("path")
    first, last = halo.first, halo.last
    path_lo = jnp.where(first, path, path - 1)
    path_hi = jnp.where(last, path, path + 1)

    def gathered(p):
        total = got_ref[p]
        for i in range(1, n):
            total += got_ref[i * m + p]
        return jnp.broadcast_to(total, (TILE, LANES))

    mine = gathered(path)
    lower = gathered(path_lo)
    upper = gathered(path_hi)
    lane = iota((TILE, LANES), 1)
    sub = iota((TILE, LANES), 0)

    def shift(x, k):
        return pltpu.roll(x, k % LANES, 1)

    def ratios(x):
        return jnp.sqrt(x + EPS) / jnp.sqrt(shift(x, -count) + EPS)

    low = jnp.where(first, 0.0, shift(ratios(lower), 1 - count))
    high = jnp.where(last, 0.0, shift(ratios(upper), count + 1))
    own = ratios(mine)
    ratio_ref[...] = own[0, 0:count]
    ratio = jnp.where(lane == 0, low, jnp.where(lane == count + 1, high, shift(own, 1)))

    def splat(t):
        return jnp.broadcast_to(jnp.sum(jnp.where(lane == t, ratio, 0.0), axis=1, keepdims=True), (TILE, LANES))

    def widen(x):
        return jnp.concatenate([x] * (cols // LANES), axis=1)

    scale = [widen(splat(t)) for t in range(count + 2)]
    column = jnp.sum(jnp.where(lane == sub + 1, ratio, 0.0), axis=1, keepdims=True)
    row = iota((TILE, cols), 0)
    fixed = halo.tail(2), halo.head(2)
    corners = []
    for i in range(2):
        near, far = near_corner_ref[i : i + 1, :], far_b_ref[rows + i : rows + i + 1, :]
        low = pick(first, fixed[i][0:1], pick(halo.path, near, far))
        high = pick(last, fixed[i][1:2], pick(halo.path, far, near))
        corners.append((low, high))

    def at(k):
        return pl.ds(TILE * k, TILE)

    for k in range(tiles):
        outer[0, at(k), :] = halo.below(at(k))
        outer[1, at(k), :] = halo.above(at(k))

    def value(s, k):
        if s == -2:
            return halo.below_2(at(k))
        if s == count + 1:
            return halo.above_2(at(k))
        ref, slot = {-1: (outer, 0), count: (outer, 1)}.get(s, (f_ref, s))
        return ref[slot, at(k), :]

    for s in range(count):
        rim[0, s : s + 1, :] = f_ref[s, 0:1, :]
        rim[1, s : s + 1, :] = f_ref[s, rows - 1 : rows, :]
    for far, mid, near, (low, high), place in (
        (halo.tail(0), halo.tail(1), rim[0], corners[0], TILE - 1),
        (halo.head(1), halo.head(0), rim[1], corners[1], TILE + rows),
    ):
        ahead = jnp.where(row == count - 1, high, pltpu.roll(mid, count - 1, 0))
        behind = jnp.where(row == 0, low, pltpu.roll(mid, 1, 0))
        edge = column * (ahead - behind) - (far + near + sides(mid) - 3.0 * mid - mid * mid * mid)
        for s in range(count):
            resid[s + 1, place : place + 1, :] = edge[s : s + 1, :]

    def residual_of(s):
        if s in (-1, count):
            slot = 0 if s < 0 else 1
            top, bottom = corners[0][slot], corners[1][slot]
        else:
            top, bottom = halo.tail(1, pl.ds(s, 1)), halo.head(0, pl.ds(s, 1))
        for k in range(tiles):
            if s in (-1, count):
                c = outer[slot, at(k), :]
                above = outer[slot, TILE * k - 1 : TILE * k, :] if k > 0 else top
                under = outer[slot, TILE * (k + 1) : TILE * (k + 1) + 1, :] if k < tiles - 1 else bottom
                up = jnp.where(row == 0, above, pltpu.roll(c, 1, 0))
                dn = jnp.where(row == TILE - 1, under, pltpu.roll(c, TILE - 1, 0))
                drift = up + dn + sides(c) - 3.0 * c - c * c * c
            else:
                drift = drift_ref[s, at(k), :]
                if k == 0:
                    drift += jnp.where(row == 0, top, 0.0)
                if k == tiles - 1:
                    drift += jnp.where(row == TILE - 1, bottom, 0.0)
            resid[s + 1, at(k + 1), :] = scale[s + 1] * (value(s + 1, k) - value(s - 1, k)) - drift

    def gradient_of(s):
        for k in range(tiles):
            base = TILE * (k + 1)
            c = f_ref[s, pl.ds(TILE * k, TILE), :]
            r = resid[s + 1, pl.ds(base, TILE), :]
            around = resid[s + 1, pl.ds(base - 1, TILE), :] + resid[s + 1, pl.ds(base + 1, TILE), :] + sides(r)
            out = scale[s] * resid[s, pl.ds(base, TILE), :] - scale[s + 2] * resid[s + 2, pl.ds(base, TILE), :]
            grad[s, pl.ds(TILE * k, TILE), :] = out - (around - (3.0 + 3.0 * c * c) * r)

    copies = []

    def send(src, dst, slot):
        copy = pltpu.make_async_copy(src, dst, slot)
        copy.start()
        copies.append(copy)

    residual_of(-1)
    residual_of(0)
    for s in range(count):
        residual_of(s + 1)
        send(resid.at[s + 1, pl.ds(TILE, rows)], res_out.at[s], sem.at[0, s])
        gradient_of(s)
        send(grad.at[s], grad_out.at[s], sem.at[1, s])
    for copy in copies:
        copy.wait()


def final(m, n, got, corners, f, drift, halo):
    count, rows, cols = f.shape
    big = jax.ShapeDtypeStruct(f.shape, F32)
    return pl.pallas_call(
        functools.partial(final_kernel, m, n),
        out_shape=(jax.ShapeDtypeStruct((count,), F32), big, big),
        in_specs=[VMEM] * 11,
        out_specs=(VMEM, ANY, ANY),
        scratch_shapes=[
            pltpu.VMEM((count + 2, rows + 2 * TILE, cols), F32),
            pltpu.VMEM(f.shape, F32),
            pltpu.VMEM((2, rows, cols), F32),
            pltpu.VMEM((2, count, cols), F32),
            pltpu.SemaphoreType.DMA((2, count)),
        ],
        compiler_params=PARAMS,
        name="final",
    )(got, *corners, f, drift, *halo)


def swap(x, axis, kind):
    size = lax.axis_size(axis)
    return lax.ppermute(x, axis, [((i + kind) % size, ((i ^ 1) + kind) % size) for i in range(size)])


def body(m, n, f, start, end):
    near, far = slices(f)
    near_strip, far_strip = strips(f, start, end)
    near = swap(near, "path", 0)
    far = swap(far, "path", 1)
    near_strip = swap(near_strip, "space", 0)
    far_strip = swap(far_strip, "space", 1)
    part, drift, rim = interior(f)
    halo = near, far, near_strip, far_strip, start, end
    send, near_corner, far_b = chunks(m, n, f, part, rim, halo)
    got = lax.all_to_all(send, ("space", "path"), 0, 0, tiled=True)
    later = swap(near_corner, "path", 0), swap(far_b, "path", 1)
    return final(m, n, got, later, f, drift, halo)


def solution(mesh):
    m, n = mesh.shape["path"], mesh.shape["space"]
    in_specs = (P("path", "space", None), P("space", None), P("space", None))
    out_specs = (P("path"), P("path", "space", None), P("path", "space", None))
    return jax.shard_map(
        functools.partial(body, m, n), mesh=mesh, in_specs=in_specs, out_specs=out_specs, check_vma=False
    )
```

```python
import functools

import jax
import jax.numpy as jnp
from jax import lax
from jax.experimental import pallas as pl
from jax.experimental.pallas import tpu as pltpu
from jax.sharding import PartitionSpec as P

F32 = jnp.float32
LANES = 128
TILE = 8
EPS = 1e-06
VMEM = pl.BlockSpec(memory_space=pltpu.VMEM)
ANY = pl.BlockSpec(memory_space=pl.ANY)
PARAMS = pltpu.CompilerParams(vmem_limit_bytes=16 * 2**20)


def lanes_sum(x):
    parts = [x[:, i : i + LANES] for i in range(0, x.shape[1], LANES)]
    while len(parts) > 1:
        parts = [a + b for a, b in zip(parts[::2], parts[1::2])] + parts[len(parts) & ~1 :]
    return parts[0]


def sides(x):
    cols = x.shape[1]
    return pltpu.roll(x, 1, 1) + pltpu.roll(x, cols - 1, 1)


def iota(shape, dim):
    return lax.broadcasted_iota(jnp.int32, shape, dim)


def odd(axis):
    return lax.rem(lax.axis_index(axis), 2) == 1


def pick(flag, x, y):
    return jnp.where(flag, x, y)


def slices_kernel(f_ref, near_ref, far_ref):
    count = f_ref.shape[0]
    flag = odd("path")
    for ref, low in ((far_ref, jnp.logical_not(flag)), (near_ref, flag)):
        base = pick(low, 0, count - 2)
        for s in range(2):
            ref[s] = f_ref[base + s]


def strips_kernel(f_ref, start_ref, end_ref, near_ref, far_ref):
    count, rows, _ = f_ref.shape
    flag = odd("space")
    for ref, low in ((near_ref, flag), (far_ref, jnp.logical_not(flag))):
        at = pick(low, 0, rows - 2)
        face = pl.ds(pick(low, 0, rows - 1), 1)
        ref[count:] = jnp.zeros_like(ref[count:])
        ref[count, 0:1, :] = start_ref[face, :]
        ref[count, 1:2, :] = end_ref[face, :]
        for s in range(count):
            for r in range(2):
                ref[s, r : r + 1, :] = f_ref[s, pl.ds(at + r, 1), :]


def slices(f):
    count, rows, cols = f.shape
    return pl.pallas_call(
        slices_kernel,
        out_shape=(jax.ShapeDtypeStruct((2, rows, cols), F32),) * 2,
        in_specs=[VMEM],
        out_specs=[VMEM] * 2,
        compiler_params=PARAMS,
        name="slices",
    )(f)


def strips(f, start, end):
    count, rows, cols = f.shape
    return pl.pallas_call(
        strips_kernel,
        out_shape=tuple(jax.ShapeDtypeStruct((count + k, 2, cols), F32) for k in (1, 2)),
        in_specs=[VMEM] * 3,
        out_specs=[VMEM] * 2,
        compiler_params=PARAMS,
        name="strips",
    )(f, start, end)


class Halo:
    def __init__(self, m, near_ref, far_ref, start_ref, end_ref):
        self.odd = odd("path")
        self.first = lax.axis_index("path") == 0
        self.last = lax.axis_index("path") == m - 1
        self.near, self.far = near_ref, far_ref
        self.start, self.end = start_ref, end_ref

    def below(self, at):
        return pick(self.first, self.start[at, :], pick(self.odd, self.near[1, at, :], self.far[1, at, :]))

    def above(self, at):
        return pick(self.last, self.end[at, :], pick(self.odd, self.far[0, at, :], self.near[0, at, :]))

    def below_2(self, at):
        return pick(self.odd, self.near[0, at, :], self.far[0, at, :])

    def above_2(self, at):
        return pick(self.odd, self.far[1, at, :], self.near[1, at, :])


def interior_kernel(f_ref, part_ref, drift_ref, rim_ref):
    count, rows, cols = f_ref.shape
    tiles = rows // TILE
    row = iota((TILE, cols), 0)
    part_ref[...] = jnp.zeros_like(part_ref)

    def drift_sum(s, _):
        total = jnp.zeros((TILE, LANES), F32)
        for k in range(tiles):
            c = f_ref[s, pl.ds(TILE * k, TILE), :]
            above = f_ref[s, pl.ds(TILE * k - 1, 1), :] if k > 0 else 0.0
            under = f_ref[s, pl.ds(TILE * (k + 1), 1), :] if k < tiles - 1 else 0.0
            up = jnp.where(row == 0, above, pltpu.roll(c, 1, 0))
            dn = jnp.where(row == TILE - 1, under, pltpu.roll(c, TILE - 1, 0))
            drift = up + dn + sides(c) - 3.0 * c - c * c * c
            drift_ref[s, pl.ds(TILE * k, TILE), :] = drift
            if k == 0:
                rim_ref[0, pl.ds(s, 1), :] = drift[0:1]
                drift = jnp.where(row == 0, 0.0, drift)
            if k == tiles - 1:
                rim_ref[1, pl.ds(s, 1), :] = drift[TILE - 1 : TILE]
                drift = jnp.where(row == TILE - 1, 0.0, drift)
            total += lanes_sum(drift * drift)
        part_ref[pl.ds(s, 1), :] = jnp.sum(total, axis=0, keepdims=True)
        return 0

    def tangent_sum(s, _):
        total = jnp.zeros((TILE, LANES), F32)
        for k in range(tiles):
            tangent = f_ref[s + 1, pl.ds(TILE * k, TILE), :] - f_ref[s - 1, pl.ds(TILE * k, TILE), :]
            total += lanes_sum(tangent * tangent)
        part_ref[pl.ds(count + s, 1), :] = jnp.sum(total, axis=0, keepdims=True)
        return 0

    lax.fori_loop(0, count, drift_sum, 0)
    lax.fori_loop(1, count - 1, tangent_sum, 0)


def interior(f):
    count, rows, cols = f.shape
    return pl.pallas_call(
        interior_kernel,
        out_shape=(
            jax.ShapeDtypeStruct((2 * count, LANES), F32),
            jax.ShapeDtypeStruct(f.shape, F32),
            jax.ShapeDtypeStruct((2, count, cols), F32),
        ),
        in_specs=[VMEM],
        out_specs=[VMEM] * 3,
        cost_estimate=pl.CostEstimate(flops=20 * count * rows * cols, transcendentals=0, bytes_accessed=8 * count * rows * cols),
        compiler_params=PARAMS,
        name="interior",
    )(f)


def chunk_kernel(
    m, n, f_ref, part_ref, rim_ref, near_ref, far_ref, start_ref, end_ref, near_strip_ref, far_strip_ref,
    out_ref, near_corner_ref, far_corner_ref, tail_ref, head_ref, face_ref,
):
    halo = Halo(m, near_ref, far_ref, start_ref, end_ref)
    count, rows, cols = f_ref.shape
    tiles = rows // TILE

    flag = odd("space")
    for i, (ref, x_ref, y_ref) in enumerate(((tail_ref, near_strip_ref, far_strip_ref), (head_ref, far_strip_ref, near_strip_ref))):
        for s in range(count):
            both = pick(flag, x_ref[s], y_ref[s])
            for r in range(2):
                ref[r, s : s + 1, :] = both[r : r + 1]
        face_ref[2 * i : 2 * i + 2, :] = pick(flag, x_ref[count], y_ref[count])
    for ref, low in ((near_corner_ref, halo.odd), (far_corner_ref, jnp.logical_not(halo.odd))):
        s = pl.ds(pick(low, 0, count - 1), 1)
        ref[0:1, :] = tail_ref[1, s, :]
        ref[1:2, :] = head_ref[0, s, :]

    drift_a = rim_ref[0] + tail_ref[1]
    drift_b = rim_ref[1] + head_ref[0]
    drift = part_ref[0:count, :] + lanes_sum(drift_a * drift_a) + lanes_sum(drift_b * drift_b)

    totals = [jnp.zeros((TILE, LANES), F32) for _ in range(2)]
    for k in range(tiles):
        at = pl.ds(TILE * k, TILE)
        tangents = (f_ref[1, at, :] - halo.below(at), halo.above(at) - f_ref[count - 2, at, :])
        totals = [a + lanes_sum(t * t) for a, t in zip(totals, tangents)]
    head_sum, tail_sum = [jnp.sum(a, axis=0, keepdims=True) for a in totals]
    sub = iota((TILE, LANES), 0)
    tangent = part_ref[count : 2 * count, :]
    tangent = jnp.where(sub == 0, head_sum, jnp.where(sub == count - 1, tail_sum, tangent))

    lane = iota((TILE, LANES), 1)
    spread = jnp.where(lane == sub, jnp.sum(drift, axis=1, keepdims=True), 0.0)
    spread += jnp.where(lane == sub + count, jnp.sum(tangent, axis=1, keepdims=True), 0.0)
    line = jnp.sum(spread, axis=0, keepdims=True)

    for j in range(m * n):
        out_ref[j] = line


def chunks(m, n, f, part, rim, near, far, start, end, near_strip, far_strip):
    count, rows, cols = f.shape
    corner = jax.ShapeDtypeStruct((2, cols), F32)
    strip = jax.ShapeDtypeStruct((2, count, cols), F32)
    return pl.pallas_call(
        functools.partial(chunk_kernel, m, n),
        out_shape=(
            jax.ShapeDtypeStruct((m * n, 1, LANES), F32),
            corner,
            corner,
            strip,
            strip,
            jax.ShapeDtypeStruct((4, cols), F32),
        ),
        in_specs=[VMEM] * 9,
        out_specs=[VMEM] * 6,
        compiler_params=PARAMS,
        name="chunks",
    )(f, part, rim, near, far, start, end, near_strip, far_strip)


def final_kernel(
    m, n, got_ref, near_corner_ref, far_corner_ref, f_ref, drift_ref, near_ref, far_ref, start_ref, end_ref,
    tail_ref, head_ref, face_ref, ratio_ref, res_out, grad_out, resid, grad, outer, rim, sem,
):
    halo = Halo(m, near_ref, far_ref, start_ref, end_ref)
    count, rows, cols = f_ref.shape
    tiles = rows // TILE
    path = lax.axis_index("path")
    first, last = halo.first, halo.last
    path_lo = jnp.where(first, path, path - 1)
    path_hi = jnp.where(last, path, path + 1)

    def gathered(p):
        total = got_ref[p]
        for i in range(1, n):
            total += got_ref[i * m + p]
        return jnp.broadcast_to(total, (TILE, LANES))

    mine = gathered(path)
    lower = gathered(path_lo)
    upper = gathered(path_hi)
    lane = iota((TILE, LANES), 1)
    sub = iota((TILE, LANES), 0)

    def shift(x, k):
        return pltpu.roll(x, k % LANES, 1)

    def ratios(x):
        return jnp.sqrt(x + EPS) / jnp.sqrt(shift(x, -count) + EPS)

    low = jnp.where(first, 0.0, shift(ratios(lower), 1 - count))
    high = jnp.where(last, 0.0, shift(ratios(upper), count + 1))
    own = ratios(mine)
    ratio_ref[...] = own[0, 0:count]
    ratio = jnp.where(lane == 0, low, jnp.where(lane == count + 1, high, shift(own, 1)))

    def splat(t):
        return jnp.broadcast_to(jnp.sum(jnp.where(lane == t, ratio, 0.0), axis=1, keepdims=True), (TILE, LANES))

    def widen(x):
        return jnp.concatenate([x] * (cols // LANES), axis=1)

    scale = [widen(splat(t)) for t in range(count + 2)]
    column = jnp.sum(jnp.where(lane == sub + 1, ratio, 0.0), axis=1, keepdims=True)
    row = iota((TILE, cols), 0)
    corners = []
    for i in range(2):
        near, far = near_corner_ref[i : i + 1, :], far_corner_ref[i : i + 1, :]
        low = pick(first, face_ref[2 * i : 2 * i + 1, :], pick(halo.odd, near, far))
        high = pick(last, face_ref[2 * i + 1 : 2 * i + 2, :], pick(halo.odd, far, near))
        corners.append((low, high))

    def at(k):
        return pl.ds(TILE * k, TILE)

    for k in range(tiles):
        outer[0, at(k), :] = halo.below(at(k))
        outer[1, at(k), :] = halo.above(at(k))

    def value(s, k):
        if s == -2:
            return halo.below_2(at(k))
        if s == count + 1:
            return halo.above_2(at(k))
        ref, slot = {-1: (outer, 0), count: (outer, 1)}.get(s, (f_ref, s))
        return ref[slot, at(k), :]

    for s in range(count):
        rim[0, s : s + 1, :] = f_ref[s, 0:1, :]
        rim[1, s : s + 1, :] = f_ref[s, rows - 1 : rows, :]
    for far, mid, near, (low, high), place in (
        (tail_ref[0], tail_ref[1], rim[0], corners[0], TILE - 1),
        (head_ref[1], head_ref[0], rim[1], corners[1], TILE + rows),
    ):
        ahead = jnp.where(row == count - 1, high, pltpu.roll(mid, count - 1, 0))
        behind = jnp.where(row == 0, low, pltpu.roll(mid, 1, 0))
        edge = column * (ahead - behind) - (far + near + sides(mid) - 3.0 * mid - mid * mid * mid)
        for s in range(count):
            resid[s + 1, place : place + 1, :] = edge[s : s + 1, :]

    def residual_of(s):
        if s in (-1, count):
            slot = 0 if s < 0 else 1
            top, bottom = corners[0][slot], corners[1][slot]
        else:
            top, bottom = tail_ref[1, s : s + 1, :], head_ref[0, s : s + 1, :]
        for k in range(tiles):
            if s in (-1, count):
                c = outer[slot, at(k), :]
                above = outer[slot, TILE * k - 1 : TILE * k, :] if k > 0 else top
                under = outer[slot, TILE * (k + 1) : TILE * (k + 1) + 1, :] if k < tiles - 1 else bottom
                up = jnp.where(row == 0, above, pltpu.roll(c, 1, 0))
                dn = jnp.where(row == TILE - 1, under, pltpu.roll(c, TILE - 1, 0))
                drift = up + dn + sides(c) - 3.0 * c - c * c * c
            else:
                drift = drift_ref[s, at(k), :]
                if k == 0:
                    drift += jnp.where(row == 0, top, 0.0)
                if k == tiles - 1:
                    drift += jnp.where(row == TILE - 1, bottom, 0.0)
            resid[s + 1, at(k + 1), :] = scale[s + 1] * (value(s + 1, k) - value(s - 1, k)) - drift

    def gradient_of(s):
        for k in range(tiles):
            base = TILE * (k + 1)
            c = f_ref[s, pl.ds(TILE * k, TILE), :]
            r = resid[s + 1, pl.ds(base, TILE), :]
            around = resid[s + 1, pl.ds(base - 1, TILE), :] + resid[s + 1, pl.ds(base + 1, TILE), :] + sides(r)
            out = scale[s] * resid[s, pl.ds(base, TILE), :] - scale[s + 2] * resid[s + 2, pl.ds(base, TILE), :]
            grad[s, pl.ds(TILE * k, TILE), :] = out - (around - (3.0 + 3.0 * c * c) * r)

    copies = []

    def send(src, dst, slot):
        copy = pltpu.make_async_copy(src, dst, slot)
        copy.start()
        copies.append(copy)

    residual_of(-1)
    residual_of(0)
    for s in range(count):
        residual_of(s + 1)
        send(resid.at[s + 1, pl.ds(TILE, rows)], res_out.at[s], sem.at[0, s])
        gradient_of(s)
        send(grad.at[s], grad_out.at[s], sem.at[1, s])
    for copy in copies:
        copy.wait()


def final(m, n, got, corners, f, drift, slabs, strips):
    count, rows, cols = f.shape
    big = jax.ShapeDtypeStruct(f.shape, F32)
    return pl.pallas_call(
        functools.partial(final_kernel, m, n),
        out_shape=(jax.ShapeDtypeStruct((count,), F32), big, big),
        in_specs=[VMEM] * 12,
        out_specs=(VMEM, ANY, ANY),
        scratch_shapes=[
            pltpu.VMEM((count + 2, rows + 2 * TILE, cols), F32),
            pltpu.VMEM(f.shape, F32),
            pltpu.VMEM((2, rows, cols), F32),
            pltpu.VMEM((2, count, cols), F32),
            pltpu.SemaphoreType.DMA((2, count)),
        ],
        compiler_params=PARAMS,
        name="final",
    )(got, *corners, f, drift, *slabs, *strips)


def swap(x, axis, kind):
    size = lax.axis_size(axis)
    return lax.ppermute(x, axis, [((i + kind) % size, ((i ^ 1) + kind) % size) for i in range(size)])


def body(m, n, f, start, end):
    near, far = slices(f)
    near_strip, far_strip = strips(f, start, end)
    far = swap(far, "path", 1)
    near = swap(near, "path", 0)
    far_strip = swap(far_strip, "space", 1)
    near_strip = swap(near_strip, "space", 0)
    part, drift, rim = interior(f)
    slabs = near, far, start, end
    send, near_corner, far_corner, *sorted_strips = chunks(m, n, f, part, rim, *slabs, near_strip, far_strip)
    got = lax.all_to_all(send, ("space", "path"), 0, 0, tiled=True)
    corners = swap(near_corner, "path", 0), swap(far_corner, "path", 1)
    return final(m, n, got, corners, f, drift, slabs, sorted_strips)


def solution(mesh):
    m, n = mesh.shape["path"], mesh.shape["space"]
    in_specs = (P("path", "space", None), P("space", None), P("space", None))
    out_specs = (P("path"), P("path", "space", None), P("path", "space", None))
    return jax.shard_map(
        functools.partial(body, m, n), mesh=mesh, in_specs=in_specs, out_specs=out_specs, check_vma=False
    )
```

```python
import functools

import jax
import jax.numpy as jnp
from jax import lax
from jax.experimental import pallas as pl
from jax.experimental.pallas import tpu as pltpu
from jax.sharding import PartitionSpec as P

F32 = jnp.float32
LANES = 128
TILE = 8
EPS = 1e-06
VMEM = pl.BlockSpec(memory_space=pltpu.VMEM)
ANY = pl.BlockSpec(memory_space=pl.ANY)
PIECES = 4
PARAMS = pltpu.CompilerParams(vmem_limit_bytes=16 * 2**20)


def lanes_sum(x):
    parts = [x[:, i : i + LANES] for i in range(0, x.shape[1], LANES)]
    while len(parts) > 1:
        parts = [a + b for a, b in zip(parts[::2], parts[1::2])] + parts[len(parts) & ~1 :]
    return parts[0]


def sides(x):
    cols = x.shape[1]
    return pltpu.roll(x, 1, 1) + pltpu.roll(x, cols - 1, 1)


def iota(shape, dim):
    return lax.broadcasted_iota(jnp.int32, shape, dim)


def odd(axis):
    return lax.rem(lax.axis_index(axis), 2) == 1


def pick(flag, x, y):
    return jnp.where(flag, x, y)


def slices_kernel(f_ref, near_ref, far_ref):
    count = f_ref.shape[0]
    flag = odd("path")
    for ref, low in ((far_ref, jnp.logical_not(flag)), (near_ref, flag)):
        base = pick(low, 0, count - 2)
        for s in range(2):
            ref[s] = f_ref[base + s]


def strips_kernel(f_ref, start_ref, end_ref, near_ref, far_ref):
    count, rows, _ = f_ref.shape
    flag = odd("space")
    for ref, low in ((near_ref, flag), (far_ref, jnp.logical_not(flag))):
        at = pick(low, 0, rows - 2)
        face = pl.ds(pick(low, 0, rows - 1), 1)
        ref[count:] = jnp.zeros_like(ref[count:])
        ref[count, 0:1, :] = start_ref[face, :]
        ref[count, 1:2, :] = end_ref[face, :]
        for s in range(count):
            for r in range(2):
                ref[s, r : r + 1, :] = f_ref[s, pl.ds(at + r, 1), :]


def slices(f):
    count, rows, cols = f.shape
    return pl.pallas_call(
        slices_kernel,
        out_shape=(jax.ShapeDtypeStruct((2, rows, cols), F32),) * 2,
        in_specs=[VMEM],
        out_specs=[VMEM] * 2,
        compiler_params=PARAMS,
        name="slices",
    )(f)


def strips(f, start, end):
    count, rows, cols = f.shape
    return pl.pallas_call(
        strips_kernel,
        out_shape=tuple(jax.ShapeDtypeStruct((count + k, 2, cols), F32) for k in (1, 2)),
        in_specs=[VMEM] * 3,
        out_specs=[VMEM] * 2,
        compiler_params=PARAMS,
        name="strips",
    )(f, start, end)


class Halo:
    def __init__(self, m, near_ref, far_ref, start_ref, end_ref):
        self.odd = odd("path")
        self.first = lax.axis_index("path") == 0
        self.last = lax.axis_index("path") == m - 1
        self.near, self.far = near_ref, far_ref
        self.start, self.end = start_ref, end_ref

    def below(self, at):
        return pick(self.first, self.start[at, :], pick(self.odd, self.near[1, at, :], self.far[1, at, :]))

    def above(self, at):
        return pick(self.last, self.end[at, :], pick(self.odd, self.far[0, at, :], self.near[0, at, :]))

    def below_2(self, at):
        return pick(self.odd, self.near[0, at, :], self.far[0, at, :])

    def above_2(self, at):
        return pick(self.odd, self.far[1, at, :], self.near[1, at, :])


def interior_kernel(f_ref, part_ref, drift_ref, rim_ref):
    count, rows, cols = f_ref.shape
    tiles = rows // TILE
    row = iota((TILE, cols), 0)
    part_ref[...] = jnp.zeros_like(part_ref)

    def drift_sum(s, _):
        total = jnp.zeros((TILE, LANES), F32)
        for k in range(tiles):
            c = f_ref[s, pl.ds(TILE * k, TILE), :]
            above = f_ref[s, pl.ds(TILE * k - 1, 1), :] if k > 0 else 0.0
            under = f_ref[s, pl.ds(TILE * (k + 1), 1), :] if k < tiles - 1 else 0.0
            up = jnp.where(row == 0, above, pltpu.roll(c, 1, 0))
            dn = jnp.where(row == TILE - 1, under, pltpu.roll(c, TILE - 1, 0))
            drift = up + dn + sides(c) - 3.0 * c - c * c * c
            drift_ref[s, pl.ds(TILE * k, TILE), :] = drift
            if k == 0:
                rim_ref[0, pl.ds(s, 1), :] = drift[0:1]
                drift = jnp.where(row == 0, 0.0, drift)
            if k == tiles - 1:
                rim_ref[1, pl.ds(s, 1), :] = drift[TILE - 1 : TILE]
                drift = jnp.where(row == TILE - 1, 0.0, drift)
            total += lanes_sum(drift * drift)
        part_ref[pl.ds(s, 1), :] = jnp.sum(total, axis=0, keepdims=True)
        return 0

    def tangent_sum(s, _):
        total = jnp.zeros((TILE, LANES), F32)
        for k in range(tiles):
            tangent = f_ref[s + 1, pl.ds(TILE * k, TILE), :] - f_ref[s - 1, pl.ds(TILE * k, TILE), :]
            total += lanes_sum(tangent * tangent)
        part_ref[pl.ds(count + s, 1), :] = jnp.sum(total, axis=0, keepdims=True)
        return 0

    lax.fori_loop(0, count, drift_sum, 0)
    lax.fori_loop(1, count - 1, tangent_sum, 0)


def interior(f):
    count, rows, cols = f.shape
    return pl.pallas_call(
        interior_kernel,
        out_shape=(
            jax.ShapeDtypeStruct((2 * count, LANES), F32),
            jax.ShapeDtypeStruct(f.shape, F32),
            jax.ShapeDtypeStruct((2, count, cols), F32),
        ),
        in_specs=[VMEM],
        out_specs=[VMEM] * 3,
        cost_estimate=pl.CostEstimate(flops=20 * count * rows * cols, transcendentals=0, bytes_accessed=8 * count * rows * cols),
        compiler_params=PARAMS,
        name="interior",
    )(f)


def chunk_kernel(
    m, n, f_ref, part_ref, rim_ref, near_ref, far_ref, start_ref, end_ref, near_strip_ref, far_strip_ref,
    out_ref, near_corner_ref, far_corner_ref, tail_ref, head_ref, face_ref, lines, sem,
):
    halo = Halo(m, near_ref, far_ref, start_ref, end_ref)
    count, rows, cols = f_ref.shape
    tiles = rows // TILE

    flag = odd("space")
    strips = (tail_ref, near_strip_ref, far_strip_ref), (head_ref, far_strip_ref, near_strip_ref)

    def sort(i, r):
        ref, x_ref, y_ref = strips[i]
        for s in range(count):
            ref[r, s : s + 1, :] = pick(flag, x_ref[s, r : r + 1, :], y_ref[s, r : r + 1, :])

    sort(0, 1)
    sort(1, 0)

    drift_a = rim_ref[0] + tail_ref[1]
    drift_b = rim_ref[1] + head_ref[0]
    drift = part_ref[0:count, :] + lanes_sum(drift_a * drift_a) + lanes_sum(drift_b * drift_b)

    totals = [jnp.zeros((TILE, LANES), F32) for _ in range(2)]
    for k in range(tiles):
        at = pl.ds(TILE * k, TILE)
        tangents = (f_ref[1, at, :] - halo.below(at), halo.above(at) - f_ref[count - 2, at, :])
        totals = [a + lanes_sum(t * t) for a, t in zip(totals, tangents)]
    head_sum, tail_sum = [jnp.sum(a, axis=0, keepdims=True) for a in totals]
    sub = iota((TILE, LANES), 0)
    tangent = part_ref[count : 2 * count, :]
    tangent = jnp.where(sub == 0, head_sum, jnp.where(sub == count - 1, tail_sum, tangent))

    lane = iota((TILE, LANES), 1)
    spread = jnp.where(lane == sub, jnp.sum(drift, axis=1, keepdims=True), 0.0)
    spread += jnp.where(lane == sub + count, jnp.sum(tangent, axis=1, keepdims=True), 0.0)
    line = jnp.sum(spread, axis=0, keepdims=True)

    for j in range(m * n):
        lines[j] = line
    copy = pltpu.make_async_copy(lines, out_ref, sem)
    copy.start()

    sort(0, 0)
    sort(1, 1)
    for i, (_, x_ref, y_ref) in enumerate(strips):
        face_ref[2 * i : 2 * i + 2, :] = pick(flag, x_ref[count], y_ref[count])
    for ref, low in ((near_corner_ref, halo.odd), (far_corner_ref, jnp.logical_not(halo.odd))):
        s = pl.ds(pick(low, 0, count - 1), 1)
        ref[0:1, :] = tail_ref[1, s, :]
        ref[1:2, :] = head_ref[0, s, :]
    copy.wait()


def chunks(m, n, f, part, rim, near, far, start, end, near_strip, far_strip):
    count, rows, cols = f.shape
    corner = jax.ShapeDtypeStruct((2, cols), F32)
    strip = jax.ShapeDtypeStruct((2, count, cols), F32)
    return pl.pallas_call(
        functools.partial(chunk_kernel, m, n),
        out_shape=(
            jax.ShapeDtypeStruct((m * n, 1, LANES), F32),
            corner,
            corner,
            strip,
            strip,
            jax.ShapeDtypeStruct((4, cols), F32),
        ),
        in_specs=[VMEM] * 9,
        out_specs=[ANY] + [VMEM] * 5,
        scratch_shapes=[pltpu.VMEM((m * n, 1, LANES), F32), pltpu.SemaphoreType.DMA],
        compiler_params=PARAMS,
        name="chunks",
    )(f, part, rim, near, far, start, end, near_strip, far_strip)


def final_kernel(
    m, n, got_ref, near_corner_ref, far_corner_ref, f_ref, drift_ref, near_ref, far_ref, start_ref, end_ref,
    tail_ref, head_ref, face_ref, ratio_out, res_out, grad_out, ratio_ref, resid, grad, outer, rim, sem,
):
    halo = Halo(m, near_ref, far_ref, start_ref, end_ref)
    count, rows, cols = f_ref.shape
    tiles = rows // TILE
    path = lax.axis_index("path")
    first, last = halo.first, halo.last
    path_lo = jnp.where(first, path, path - 1)
    path_hi = jnp.where(last, path, path + 1)

    def gathered(p):
        total = got_ref[p]
        for i in range(1, n):
            total += got_ref[i * m + p]
        return jnp.broadcast_to(total, (TILE, LANES))

    mine = gathered(path)
    lower = gathered(path_lo)
    upper = gathered(path_hi)
    lane = iota((TILE, LANES), 1)
    sub = iota((TILE, LANES), 0)

    def shift(x, k):
        return pltpu.roll(x, k % LANES, 1)

    def ratios(x):
        return jnp.sqrt(x + EPS) / jnp.sqrt(shift(x, -count) + EPS)

    low = jnp.where(first, 0.0, shift(ratios(lower), 1 - count))
    high = jnp.where(last, 0.0, shift(ratios(upper), count + 1))
    own = ratios(mine)
    ratio_ref[...] = own[0, 0:count]
    copies = [pltpu.make_async_copy(ratio_ref, ratio_out, sem.at[2, 0])]
    copies[0].start()
    ratio = jnp.where(lane == 0, low, jnp.where(lane == count + 1, high, shift(own, 1)))

    def splat(t):
        return jnp.broadcast_to(jnp.sum(jnp.where(lane == t, ratio, 0.0), axis=1, keepdims=True), (TILE, LANES))

    def widen(x):
        return jnp.concatenate([x] * (cols // LANES), axis=1)

    scale = [widen(splat(t)) for t in range(count + 2)]
    column = jnp.sum(jnp.where(lane == sub + 1, ratio, 0.0), axis=1, keepdims=True)
    row = iota((TILE, cols), 0)
    corners = []
    for i in range(2):
        near, far = near_corner_ref[i : i + 1, :], far_corner_ref[i : i + 1, :]
        low = pick(first, face_ref[2 * i : 2 * i + 1, :], pick(halo.odd, near, far))
        high = pick(last, face_ref[2 * i + 1 : 2 * i + 2, :], pick(halo.odd, far, near))
        corners.append((low, high))

    def at(k):
        return pl.ds(TILE * k, TILE)

    def value(s, k):
        if s < 0:
            return halo.below(at(k)) if s == -1 else halo.below_2(at(k))
        if s >= count:
            return halo.above(at(k)) if s == count else halo.above_2(at(k))
        return f_ref[s, at(k), :]

    def residual_of(s):
        for k in range(tiles):
            if 0 <= s < count:
                drift = drift_ref[s, at(k), :]
                if k == 0:
                    drift += jnp.where(row == 0, tail_ref[1, s : s + 1, :], 0.0)
                if k == tiles - 1:
                    drift += jnp.where(row == TILE - 1, head_ref[0, s : s + 1, :], 0.0)
            else:
                slot = 0 if s < 0 else 1
                c = outer[slot, at(k), :]
                above = outer[slot, TILE * k - 1 : TILE * k, :] if k > 0 else corners[0][slot]
                under = outer[slot, TILE * (k + 1) : TILE * (k + 1) + 1, :] if k < tiles - 1 else corners[1][slot]
                up = jnp.where(row == 0, above, pltpu.roll(c, 1, 0))
                dn = jnp.where(row == TILE - 1, under, pltpu.roll(c, TILE - 1, 0))
                drift = up + dn + sides(c) - 3.0 * c - c * c * c
            resid[s + 1, at(k + 1), :] = scale[s + 1] * (value(s + 1, k) - value(s - 1, k)) - drift

    def send(src, dst, slot):
        copy = pltpu.make_async_copy(src, dst, slot)
        copy.start()
        copies.append(copy)

    pieces = PIECES if count % PIECES == 0 else 1
    step = count // pieces
    for i in range(pieces):
        for s in range(i * step, (i + 1) * step):
            residual_of(s)
        span = pl.ds(i * step, step)
        send(resid.at[pl.ds(i * step + 1, step), pl.ds(TILE, rows)], res_out.at[span], sem.at[0, i])

    for k in range(tiles):
        outer[0, at(k), :] = halo.below(at(k))
        outer[1, at(k), :] = halo.above(at(k))
    residual_of(-1)
    residual_of(count)

    for s in range(count):
        rim[0, s : s + 1, :] = f_ref[s, 0:1, :]
        rim[1, s : s + 1, :] = f_ref[s, rows - 1 : rows, :]
    for far, mid, near, (low, high), place in (
        (tail_ref[0], tail_ref[1], rim[0], corners[0], TILE - 1),
        (head_ref[1], head_ref[0], rim[1], corners[1], TILE + rows),
    ):
        ahead = jnp.where(row == count - 1, high, pltpu.roll(mid, count - 1, 0))
        behind = jnp.where(row == 0, low, pltpu.roll(mid, 1, 0))
        edge = column * (ahead - behind) - (far + near + sides(mid) - 3.0 * mid - mid * mid * mid)
        for s in range(count):
            resid[s + 1, place : place + 1, :] = edge[s : s + 1, :]

    def gradient_of(s):
        r = [resid[s + 1, at(k + 1), :] for k in range(tiles)]
        down = [resid[s + 1, TILE - 1 : TILE, :]] + [pltpu.roll(x, 1, 0) for x in r]
        up = [pltpu.roll(x, TILE - 1, 0) for x in r] + [resid[s + 1, TILE + rows : TILE + rows + 1, :]]
        for k in range(tiles):
            c = f_ref[s, at(k), :]
            around = jnp.where(row == 0, down[k], down[k + 1]) + jnp.where(row == TILE - 1, up[k + 1], up[k]) + sides(r[k])
            out = scale[s] * resid[s, at(k + 1), :] - scale[s + 2] * resid[s + 2, at(k + 1), :]
            grad[s, at(k), :] = out - (around - (3.0 + 3.0 * c * c) * r[k])

    for i in range(pieces):
        for s in range(i * step, (i + 1) * step):
            gradient_of(s)
        span = pl.ds(i * step, step)
        send(grad.at[span], grad_out.at[span], sem.at[1, i])
    for copy in copies:
        copy.wait()


def final(m, n, got, corners, f, drift, slabs, strips):
    count, rows, cols = f.shape
    big = jax.ShapeDtypeStruct(f.shape, F32)
    return pl.pallas_call(
        functools.partial(final_kernel, m, n),
        out_shape=(jax.ShapeDtypeStruct((count,), F32), big, big),
        in_specs=[VMEM] * 12,
        out_specs=(ANY, ANY, ANY),
        scratch_shapes=[
            pltpu.VMEM((count,), F32),
            pltpu.VMEM((count + 2, rows + 2 * TILE, cols), F32),
            pltpu.VMEM(f.shape, F32),
            pltpu.VMEM((2, rows, cols), F32),
            pltpu.VMEM((2, count, cols), F32),
            pltpu.SemaphoreType.DMA((3, PIECES)),
        ],
        compiler_params=PARAMS,
        name="final",
    )(got, *corners, f, drift, *slabs, *strips)


def swap(x, axis, kind):
    size = lax.axis_size(axis)
    return lax.ppermute(x, axis, [((i + kind) % size, ((i ^ 1) + kind) % size) for i in range(size)])


def body(m, n, f, start, end):
    near, far = slices(f)
    near_strip, far_strip = strips(f, start, end)
    far = swap(far, "path", 1)
    near = swap(near, "path", 0)
    far_strip = swap(far_strip, "space", 1)
    near_strip = swap(near_strip, "space", 0)
    part, drift, rim = interior(f)
    slabs = near, far, start, end
    send, near_corner, far_corner, *sorted_strips = chunks(m, n, f, part, rim, *slabs, near_strip, far_strip)
    got = lax.all_to_all(send, ("space", "path"), 0, 0, tiled=True)
    corners = swap(near_corner, "path", 0), swap(far_corner, "path", 1)
    return final(m, n, got, corners, f, drift, slabs, sorted_strips)


def solution(mesh):
    m, n = mesh.shape["path"], mesh.shape["space"]
    in_specs = (P("path", "space", None), P("space", None), P("space", None))
    out_specs = (P("path"), P("path", "space", None), P("path", "space", None))
    return jax.shard_map(
        functools.partial(body, m, n), mesh=mesh, in_specs=in_specs, out_specs=out_specs, check_vma=False
    )
```

```python
import functools

import jax
import jax.numpy as jnp
from jax import lax
from jax.experimental import pallas as pl
from jax.experimental.pallas import tpu as pltpu
from jax.sharding import PartitionSpec as P

F32 = jnp.float32
LANES = 128
TILE = 8
EPS = 1e-06
VMEM = pl.BlockSpec(memory_space=pltpu.VMEM)
ANY = pl.BlockSpec(memory_space=pl.ANY)
PIECES = 4
WIDTH = 384
PARAMS = pltpu.CompilerParams(vmem_limit_bytes=16 * 2**20)


def lanes_sum(x):
    parts = [x[:, i : i + LANES] for i in range(0, x.shape[1], LANES)]
    while len(parts) > 1:
        parts = [a + b for a, b in zip(parts[::2], parts[1::2])] + parts[len(parts) & ~1 :]
    return parts[0]


def sides(x):
    cols = x.shape[1]
    return pltpu.roll(x, 1, 1) + pltpu.roll(x, cols - 1, 1)


def iota(shape, dim):
    return lax.broadcasted_iota(jnp.int32, shape, dim)


def odd(axis):
    return lax.rem(lax.axis_index(axis), 2) == 1


def pick(flag, x, y):
    return jnp.where(flag, x, y)


def slices_kernel(f_ref, near_ref, far_ref):
    count = f_ref.shape[0]
    flag = odd("path")
    for ref, low in ((far_ref, jnp.logical_not(flag)), (near_ref, flag)):
        base = pick(low, 0, count - 2)
        for s in range(2):
            ref[s] = f_ref[base + s]


def tail_kernel(f_ref, start_ref, end_ref, tail_ref):
    count, rows, _ = f_ref.shape
    tail_ref[count, 0:1, :] = start_ref[rows - 1 :, :]
    tail_ref[count, 1:2, :] = end_ref[rows - 1 :, :]
    for s in range(count):
        tail_ref[s] = f_ref[s, rows - 2 :, :]


def slices(f):
    count, rows, cols = f.shape
    return pl.pallas_call(
        slices_kernel,
        out_shape=(jax.ShapeDtypeStruct((2, rows, cols), F32),) * 2,
        in_specs=[VMEM],
        out_specs=[VMEM] * 2,
        compiler_params=PARAMS,
        name="slices",
    )(f)


def tail_rows(f, start, end):
    count, rows, cols = f.shape
    return pl.pallas_call(
        tail_kernel,
        out_shape=jax.ShapeDtypeStruct((count + 1, 2, cols), F32),
        in_specs=[VMEM] * 3,
        out_specs=VMEM,
        compiler_params=PARAMS,
        name="tail_rows",
    )(f, start, end)


class Halo:
    def __init__(self, m, near_ref, far_ref, start_ref, end_ref):
        self.odd = odd("path")
        self.first = lax.axis_index("path") == 0
        self.last = lax.axis_index("path") == m - 1
        self.near, self.far = near_ref, far_ref
        self.start, self.end = start_ref, end_ref

    def below(self, at):
        return pick(self.first, self.start[at, :], pick(self.odd, self.near[1, at, :], self.far[1, at, :]))

    def above(self, at):
        return pick(self.last, self.end[at, :], pick(self.odd, self.far[0, at, :], self.near[0, at, :]))

    def below_2(self, at):
        return pick(self.odd, self.near[0, at, :], self.far[0, at, :])

    def above_2(self, at):
        return pick(self.odd, self.far[1, at, :], self.near[1, at, :])


def interior_kernel(f_ref, part_ref, drift_ref, rim_ref):
    count, rows, cols = f_ref.shape
    tiles = rows // TILE
    row = iota((TILE, cols), 0)
    part_ref[...] = jnp.zeros_like(part_ref)

    def drift_sum(s, _):
        total = jnp.zeros((TILE, LANES), F32)
        for k in range(tiles):
            c = f_ref[s, pl.ds(TILE * k, TILE), :]
            above = f_ref[s, pl.ds(TILE * k - 1, 1), :] if k > 0 else 0.0
            under = f_ref[s, pl.ds(TILE * (k + 1), 1), :] if k < tiles - 1 else 0.0
            up = jnp.where(row == 0, above, pltpu.roll(c, 1, 0))
            dn = jnp.where(row == TILE - 1, under, pltpu.roll(c, TILE - 1, 0))
            drift = up + dn + sides(c) - 3.0 * c - c * c * c
            drift_ref[s, pl.ds(TILE * k, TILE), :] = drift
            if k == 0:
                rim_ref[0, pl.ds(s, 1), :] = drift[0:1]
                rim_ref[1, pl.ds(s, 1), :] = c[0:1]
                drift = jnp.where(row == 0, 0.0, drift)
            if k == tiles - 1:
                drift = jnp.where(row == TILE - 1, 0.0, drift)
            total += lanes_sum(drift * drift)
        part_ref[pl.ds(s, 1), :] = jnp.sum(total, axis=0, keepdims=True)
        return 0

    def tangent_sum(s, _):
        total = jnp.zeros((TILE, LANES), F32)
        for k in range(tiles):
            tangent = f_ref[s + 1, pl.ds(TILE * k, TILE), :] - f_ref[s - 1, pl.ds(TILE * k, TILE), :]
            total += lanes_sum(tangent * tangent)
        part_ref[pl.ds(count + s, 1), :] = jnp.sum(total, axis=0, keepdims=True)
        return 0

    lax.fori_loop(0, count, drift_sum, 0)
    lax.fori_loop(1, count - 1, tangent_sum, 0)


def interior(f):
    count, rows, cols = f.shape
    return pl.pallas_call(
        interior_kernel,
        out_shape=(
            jax.ShapeDtypeStruct((2 * count, LANES), F32),
            jax.ShapeDtypeStruct(f.shape, F32),
            jax.ShapeDtypeStruct((2, count, cols), F32),
        ),
        in_specs=[VMEM],
        out_specs=[VMEM] * 3,
        cost_estimate=pl.CostEstimate(flops=20 * count * rows * cols, transcendentals=0, bytes_accessed=8 * count * rows * cols),
        compiler_params=PARAMS,
        name="interior",
    )(f)


def chunk_kernel(
    m, n, f_ref, part_ref, rim_ref, near_ref, far_ref, start_ref, end_ref, strip_ref,
    out_ref, near_corner_ref, far_corner_ref, tail_ref, head_ref, lines, sem,
):
    halo = Halo(m, near_ref, far_ref, start_ref, end_ref)
    count, rows, cols = f_ref.shape
    tiles = rows // TILE

    for s in range(count):
        for r in range(2):
            tail_ref[r, s : s + 1, :] = strip_ref[s, r : r + 1, :]
    r0, r1 = tail_ref[0], tail_ref[1]

    drift_a = r0 + rim_ref[1] + sides(r1) - 3.0 * r1 - r1 * r1 * r1
    drift_b = rim_ref[0] + r1
    drift = part_ref[0:count, :] + lanes_sum(drift_a * drift_a) + lanes_sum(drift_b * drift_b)

    totals = [jnp.zeros((TILE, LANES), F32) for _ in range(2)]
    for k in range(tiles):
        at = pl.ds(TILE * k, TILE)
        tangents = (f_ref[1, at, :] - halo.below(at), halo.above(at) - f_ref[count - 2, at, :])
        totals = [a + lanes_sum(t * t) for a, t in zip(totals, tangents)]
    head_sum, tail_sum = [jnp.sum(a, axis=0, keepdims=True) for a in totals]
    sub = iota((TILE, LANES), 0)
    tangent = part_ref[count : 2 * count, :]
    tangent = jnp.where(sub == 0, head_sum, jnp.where(sub == count - 1, tail_sum, tangent))

    lane = iota((TILE, LANES), 1)
    spread = jnp.where(lane == sub, jnp.sum(drift, axis=1, keepdims=True), 0.0)
    spread += jnp.where(lane == sub + count, jnp.sum(tangent, axis=1, keepdims=True), 0.0)
    line = jnp.sum(spread, axis=0, keepdims=True)

    if WIDTH > LANES:
        line = jnp.concatenate([line, jnp.zeros((1, WIDTH - LANES), F32)], axis=1)
    for j in range(m * n):
        lines[j] = line
    copy = pltpu.make_async_copy(lines, out_ref, sem)
    copy.start()

    for ref, low in ((near_corner_ref, halo.odd), (far_corner_ref, jnp.logical_not(halo.odd))):
        ref[...] = tail_ref[1, pl.ds(pick(low, 0, count - 1), 1), :]
    for s in range(count):
        head_ref[s] = f_ref[s, 0:2, :]
    head_ref[count, 0:1, :] = halo.below(pl.ds(0, 1))
    head_ref[count, 1:2, :] = halo.above(pl.ds(0, 1))
    copy.wait()


def chunks(m, n, f, part, rim, near, far, start, end, strip):
    count, rows, cols = f.shape
    corner = jax.ShapeDtypeStruct((1, cols), F32)
    return pl.pallas_call(
        functools.partial(chunk_kernel, m, n),
        out_shape=(
            jax.ShapeDtypeStruct((m * n, 1, WIDTH), F32),
            corner,
            corner,
            jax.ShapeDtypeStruct((2, count, cols), F32),
            jax.ShapeDtypeStruct((count + 1, 2, cols), F32),
        ),
        in_specs=[VMEM] * 8,
        out_specs=[ANY] + [VMEM] * 4,
        scratch_shapes=[pltpu.VMEM((m * n, 1, WIDTH), F32), pltpu.SemaphoreType.DMA],
        compiler_params=PARAMS,
        name="chunks",
    )(f, part, rim, near, far, start, end, strip)


def final_kernel(
    m, n, got_ref, near_corner_ref, far_corner_ref, f_ref, drift_ref, near_ref, far_ref, start_ref, end_ref,
    strip_ref, tail_ref, lead_ref, ratio_out, res_out, grad_out, ratio_ref, resid, grad, outer, rim, head_ref, sem,
):
    halo = Halo(m, near_ref, far_ref, start_ref, end_ref)
    count, rows, cols = f_ref.shape
    tiles = rows // TILE
    path = lax.axis_index("path")
    first, last = halo.first, halo.last
    path_lo = jnp.where(first, path, path - 1)
    path_hi = jnp.where(last, path, path + 1)

    def gathered(p):
        total = got_ref[p, :, 0:LANES]
        for i in range(1, n):
            total += got_ref[i * m + p, :, 0:LANES]
        return jnp.broadcast_to(total, (TILE, LANES))

    mine = gathered(path)
    lower = gathered(path_lo)
    upper = gathered(path_hi)
    lane = iota((TILE, LANES), 1)
    sub = iota((TILE, LANES), 0)

    def shift(x, k):
        return pltpu.roll(x, k % LANES, 1)

    def ratios(x):
        return jnp.sqrt(x + EPS) / jnp.sqrt(shift(x, -count) + EPS)

    low = jnp.where(first, 0.0, shift(ratios(lower), 1 - count))
    high = jnp.where(last, 0.0, shift(ratios(upper), count + 1))
    own = ratios(mine)
    ratio_ref[...] = own[0, 0:count]
    copies = [pltpu.make_async_copy(ratio_ref, ratio_out, sem.at[2, 0])]
    copies[0].start()
    ratio = jnp.where(lane == 0, low, jnp.where(lane == count + 1, high, shift(own, 1)))

    def splat(t):
        return jnp.broadcast_to(jnp.sum(jnp.where(lane == t, ratio, 0.0), axis=1, keepdims=True), (TILE, LANES))

    def widen(x):
        return jnp.concatenate([x] * (cols // LANES), axis=1)

    scale = [widen(splat(t)) for t in range(count + 2)]
    column = jnp.sum(jnp.where(lane == sub + 1, ratio, 0.0), axis=1, keepdims=True)
    row = iota((TILE, cols), 0)
    near, far = near_corner_ref[...], far_corner_ref[...]
    corners = (
        (
            pick(first, strip_ref[count, 0:1, :], pick(halo.odd, near, far)),
            pick(last, strip_ref[count, 1:2, :], pick(halo.odd, far, near)),
        ),
        (lead_ref[count, 0:1, :], lead_ref[count, 1:2, :]),
    )

    def at(k):
        return pl.ds(TILE * k, TILE)

    def value(s, k):
        if s < 0:
            return halo.below(at(k)) if s == -1 else halo.below_2(at(k))
        if s >= count:
            return halo.above(at(k)) if s == count else halo.above_2(at(k))
        return f_ref[s, at(k), :]

    def residual_of(s):
        for k in range(tiles):
            if 0 <= s < count:
                drift = drift_ref[s, at(k), :]
                if k == 0:
                    drift += jnp.where(row == 0, tail_ref[1, s : s + 1, :], 0.0)
                if k == tiles - 1:
                    drift += jnp.where(row == TILE - 1, lead_ref[s, 0:1, :], 0.0)
            else:
                slot = 0 if s < 0 else 1
                c = outer[slot, at(k), :]
                above = outer[slot, TILE * k - 1 : TILE * k, :] if k > 0 else corners[0][slot]
                under = outer[slot, TILE * (k + 1) : TILE * (k + 1) + 1, :] if k < tiles - 1 else corners[1][slot]
                up = jnp.where(row == 0, above, pltpu.roll(c, 1, 0))
                dn = jnp.where(row == TILE - 1, under, pltpu.roll(c, TILE - 1, 0))
                drift = up + dn + sides(c) - 3.0 * c - c * c * c
            resid[s + 1, at(k + 1), :] = scale[s + 1] * (value(s + 1, k) - value(s - 1, k)) - drift

    def send(src, dst, slot):
        copy = pltpu.make_async_copy(src, dst, slot)
        copy.start()
        copies.append(copy)

    pieces = PIECES if count % PIECES == 0 else 1
    step = count // pieces
    for i in range(pieces):
        for s in range(i * step, (i + 1) * step):
            residual_of(s)
        span = pl.ds(i * step, step)
        send(resid.at[pl.ds(i * step + 1, step), pl.ds(TILE, rows)], res_out.at[span], sem.at[0, i])

    for k in range(tiles):
        outer[0, at(k), :] = halo.below(at(k))
        outer[1, at(k), :] = halo.above(at(k))
    residual_of(-1)
    residual_of(count)

    for s in range(count):
        rim[0, s : s + 1, :] = f_ref[s, 0:1, :]
        rim[1, s : s + 1, :] = f_ref[s, rows - 1 : rows, :]
        for r in range(2):
            head_ref[r, s : s + 1, :] = lead_ref[s, r : r + 1, :]
    for far, mid, near, (low, high), place in (
        (tail_ref[0], tail_ref[1], rim[0], corners[0], TILE - 1),
        (head_ref[1], head_ref[0], rim[1], corners[1], TILE + rows),
    ):
        ahead = jnp.where(row == count - 1, high, pltpu.roll(mid, count - 1, 0))
        behind = jnp.where(row == 0, low, pltpu.roll(mid, 1, 0))
        edge = column * (ahead - behind) - (far + near + sides(mid) - 3.0 * mid - mid * mid * mid)
        for s in range(count):
            resid[s + 1, place : place + 1, :] = edge[s : s + 1, :]

    def gradient_of(s):
        r = [resid[s + 1, at(k + 1), :] for k in range(tiles)]
        down = [resid[s + 1, TILE - 1 : TILE, :]] + [pltpu.roll(x, 1, 0) for x in r]
        up = [pltpu.roll(x, TILE - 1, 0) for x in r] + [resid[s + 1, TILE + rows : TILE + rows + 1, :]]
        for k in range(tiles):
            c = f_ref[s, at(k), :]
            around = jnp.where(row == 0, down[k], down[k + 1]) + jnp.where(row == TILE - 1, up[k + 1], up[k]) + sides(r[k])
            out = scale[s] * resid[s, at(k + 1), :] - scale[s + 2] * resid[s + 2, at(k + 1), :]
            grad[s, at(k), :] = out - (around - (3.0 + 3.0 * c * c) * r[k])

    for i in range(pieces):
        for s in range(i * step, (i + 1) * step):
            gradient_of(s)
        span = pl.ds(i * step, step)
        send(grad.at[span], grad_out.at[span], sem.at[1, i])
    for copy in copies:
        copy.wait()


def final(m, n, got, corners, f, drift, slabs, strips):
    count, rows, cols = f.shape
    big = jax.ShapeDtypeStruct(f.shape, F32)
    return pl.pallas_call(
        functools.partial(final_kernel, m, n),
        out_shape=(jax.ShapeDtypeStruct((count,), F32), big, big),
        in_specs=[VMEM] * 12,
        out_specs=(ANY, ANY, ANY),
        scratch_shapes=[
            pltpu.VMEM((count,), F32),
            pltpu.VMEM((count + 2, rows + 2 * TILE, cols), F32),
            pltpu.VMEM(f.shape, F32),
            pltpu.VMEM((2, rows, cols), F32),
            pltpu.VMEM((2, count, cols), F32),
            pltpu.VMEM((2, count, cols), F32),
            pltpu.SemaphoreType.DMA((3, PIECES)),
        ],
        compiler_params=PARAMS,
        name="final",
    )(got, *corners, f, drift, *slabs, *strips)


def swap(x, kind):
    size = lax.axis_size("path")
    return lax.ppermute(x, "path", [((i + kind) % size, ((i ^ 1) + kind) % size) for i in range(size)])


def ring(x, step):
    size = lax.axis_size("space")
    return lax.ppermute(x, "space", [(i, (i + step) % size) for i in range(size)])


def body(m, n, f, start, end):
    near, far = slices(f)
    strip = ring(tail_rows(f, start, end), 1)
    far = swap(far, 1)
    near = swap(near, 0)
    part, drift, rim = interior(f)
    slabs = near, far, start, end
    send, near_corner, far_corner, tail, head = chunks(m, n, f, part, rim, *slabs, strip)
    got = lax.all_to_all(send, ("space", "path"), 0, 0, tiled=True)
    lead = ring(head, -1)
    corners = swap(near_corner, 0), swap(far_corner, 1)
    return final(m, n, got, corners, f, drift, slabs, (strip, tail, lead))


def solution(mesh):
    m, n = mesh.shape["path"], mesh.shape["space"]
    in_specs = (P("path", "space", None), P("space", None), P("space", None))
    out_specs = (P("path"), P("path", "space", None), P("path", "space", None))
    return jax.shard_map(
        functools.partial(body, m, n), mesh=mesh, in_specs=in_specs, out_specs=out_specs, check_vma=False
    )
```

```python
import functools

import jax
import jax.numpy as jnp
from jax import lax
from jax.experimental import pallas as pl
from jax.experimental.pallas import tpu as pltpu
from jax.sharding import PartitionSpec as P

F32 = jnp.float32
LANES = 128
TILE = 8
EPS = 1e-06
VMEM = pl.BlockSpec(memory_space=pltpu.VMEM)
ANY = pl.BlockSpec(memory_space=pl.ANY)
PIECES = 4
WIDTH = 384
PARAMS = pltpu.CompilerParams(vmem_limit_bytes=16 * 2**20)


def lanes_sum(x):
    parts = [x[:, i : i + LANES] for i in range(0, x.shape[1], LANES)]
    while len(parts) > 1:
        parts = [a + b for a, b in zip(parts[::2], parts[1::2])] + parts[len(parts) & ~1 :]
    return parts[0]


def sides(x):
    cols = x.shape[1]
    return pltpu.roll(x, 1, 1) + pltpu.roll(x, cols - 1, 1)


def iota(shape, dim):
    return lax.broadcasted_iota(jnp.int32, shape, dim)


def odd(axis):
    return lax.rem(lax.axis_index(axis), 2) == 1


def pick(flag, x, y):
    return jnp.where(flag, x, y)


def slices_kernel(f_ref, near_ref, far_ref):
    count = f_ref.shape[0]
    flag = odd("path")
    base = pick(flag, 0, count - 2)
    for s in range(2):
        near_ref[s] = f_ref[base + s]
    far_ref[...] = f_ref[pick(flag, count - 1, 0)]


def tail_kernel(f_ref, start_ref, end_ref, tail_ref):
    count, rows, _ = f_ref.shape
    tail_ref[count, 0:1, :] = start_ref[rows - 1 :, :]
    tail_ref[count, 1:2, :] = end_ref[rows - 1 :, :]
    for s in range(count):
        tail_ref[s] = f_ref[s, rows - 2 :, :]


def slices(f):
    count, rows, cols = f.shape
    return pl.pallas_call(
        slices_kernel,
        out_shape=(jax.ShapeDtypeStruct((2, rows, cols), F32), jax.ShapeDtypeStruct((rows, cols), F32)),
        in_specs=[VMEM],
        out_specs=[VMEM] * 2,
        compiler_params=PARAMS,
        name="slices",
    )(f)


def tail_rows(f, start, end):
    count, rows, cols = f.shape
    return pl.pallas_call(
        tail_kernel,
        out_shape=jax.ShapeDtypeStruct((count + 1, 2, cols), F32),
        in_specs=[VMEM] * 3,
        out_specs=VMEM,
        compiler_params=PARAMS,
        name="tail_rows",
    )(f, start, end)


class Halo:
    def __init__(self, m, near_ref, far_ref, start_ref, end_ref, rest_ref=None):
        self.odd = odd("path")
        self.first = lax.axis_index("path") == 0
        self.last = lax.axis_index("path") == m - 1
        self.near, self.far, self.rest = near_ref, far_ref, rest_ref
        self.start, self.end = start_ref, end_ref

    def below(self, at):
        return pick(self.first, self.start[at, :], pick(self.odd, self.near[1, at, :], self.far[at, :]))

    def above(self, at):
        return pick(self.last, self.end[at, :], pick(self.odd, self.far[at, :], self.near[0, at, :]))

    def below_2(self, at):
        return pick(self.odd, self.near[0, at, :], self.rest[at, :])

    def above_2(self, at):
        return pick(self.odd, self.rest[at, :], self.near[1, at, :])


def interior_kernel(f_ref, part_ref, drift_ref, rim_ref):
    count, rows, cols = f_ref.shape
    tiles = rows // TILE
    row = iota((TILE, cols), 0)
    part_ref[...] = jnp.zeros_like(part_ref)

    def drift_sum(s, _):
        total = jnp.zeros((TILE, LANES), F32)
        for k in range(tiles):
            c = f_ref[s, pl.ds(TILE * k, TILE), :]
            above = f_ref[s, pl.ds(TILE * k - 1, 1), :] if k > 0 else 0.0
            under = f_ref[s, pl.ds(TILE * (k + 1), 1), :] if k < tiles - 1 else 0.0
            up = jnp.where(row == 0, above, pltpu.roll(c, 1, 0))
            dn = jnp.where(row == TILE - 1, under, pltpu.roll(c, TILE - 1, 0))
            drift = up + dn + sides(c) - 3.0 * c - c * c * c
            drift_ref[s, pl.ds(TILE * k, TILE), :] = drift
            if k == 0:
                rim_ref[0, pl.ds(s, 1), :] = drift[0:1]
                rim_ref[1, pl.ds(s, 1), :] = c[0:1]
                drift = jnp.where(row == 0, 0.0, drift)
            if k == tiles - 1:
                drift = jnp.where(row == TILE - 1, 0.0, drift)
            total += lanes_sum(drift * drift)
        part_ref[pl.ds(s, 1), :] = jnp.sum(total, axis=0, keepdims=True)
        return 0

    def tangent_sum(s, _):
        total = jnp.zeros((TILE, LANES), F32)
        for k in range(tiles):
            tangent = f_ref[s + 1, pl.ds(TILE * k, TILE), :] - f_ref[s - 1, pl.ds(TILE * k, TILE), :]
            total += lanes_sum(tangent * tangent)
        part_ref[pl.ds(count + s, 1), :] = jnp.sum(total, axis=0, keepdims=True)
        return 0

    lax.fori_loop(0, count, drift_sum, 0)
    lax.fori_loop(1, count - 1, tangent_sum, 0)


def interior(f):
    count, rows, cols = f.shape
    return pl.pallas_call(
        interior_kernel,
        out_shape=(
            jax.ShapeDtypeStruct((2 * count, LANES), F32),
            jax.ShapeDtypeStruct(f.shape, F32),
            jax.ShapeDtypeStruct((2, count, cols), F32),
        ),
        in_specs=[VMEM],
        out_specs=[VMEM] * 3,
        cost_estimate=pl.CostEstimate(flops=20 * count * rows * cols, transcendentals=0, bytes_accessed=8 * count * rows * cols),
        compiler_params=PARAMS,
        name="interior",
    )(f)


def chunk_kernel(
    m, n, f_ref, part_ref, rim_ref, near_ref, far_ref, start_ref, end_ref, strip_ref,
    out_ref, near_corner_ref, rest_ref, tail_ref, head_ref, lines, sem,
):
    halo = Halo(m, near_ref, far_ref, start_ref, end_ref)
    count, rows, cols = f_ref.shape
    tiles = rows // TILE

    for s in range(count):
        for r in range(2):
            tail_ref[r, s : s + 1, :] = strip_ref[s, r : r + 1, :]
    r0, r1 = tail_ref[0], tail_ref[1]

    drift_a = r0 + rim_ref[1] + sides(r1) - 3.0 * r1 - r1 * r1 * r1
    drift_b = rim_ref[0] + r1
    drift = part_ref[0:count, :] + lanes_sum(drift_a * drift_a) + lanes_sum(drift_b * drift_b)

    totals = [jnp.zeros((TILE, LANES), F32) for _ in range(2)]
    for k in range(tiles):
        at = pl.ds(TILE * k, TILE)
        tangents = (f_ref[1, at, :] - halo.below(at), halo.above(at) - f_ref[count - 2, at, :])
        totals = [a + lanes_sum(t * t) for a, t in zip(totals, tangents)]
    head_sum, tail_sum = [jnp.sum(a, axis=0, keepdims=True) for a in totals]
    sub = iota((TILE, LANES), 0)
    tangent = part_ref[count : 2 * count, :]
    tangent = jnp.where(sub == 0, head_sum, jnp.where(sub == count - 1, tail_sum, tangent))

    lane = iota((TILE, LANES), 1)
    spread = jnp.where(lane == sub, jnp.sum(drift, axis=1, keepdims=True), 0.0)
    spread += jnp.where(lane == sub + count, jnp.sum(tangent, axis=1, keepdims=True), 0.0)
    line = jnp.sum(spread, axis=0, keepdims=True)

    if WIDTH > LANES:
        line = jnp.concatenate([line, jnp.zeros((1, WIDTH - LANES), F32)], axis=1)
    for j in range(m * n):
        lines[j] = line
    copy = pltpu.make_async_copy(lines, out_ref, sem)
    copy.start()

    near_corner_ref[...] = tail_ref[1, pl.ds(pick(halo.odd, 0, count - 1), 1), :]
    rest_ref[0:rows, :] = f_ref[pick(halo.odd, count - 2, 1)]
    rest_ref[rows:, :] = jnp.broadcast_to(tail_ref[1, pl.ds(pick(halo.odd, count - 1, 0), 1), :], (TILE, cols))
    for s in range(count):
        head_ref[s] = f_ref[s, 0:2, :]
    head_ref[count, 0:1, :] = halo.below(pl.ds(0, 1))
    head_ref[count, 1:2, :] = halo.above(pl.ds(0, 1))
    copy.wait()


def chunks(m, n, f, part, rim, near, far, start, end, strip):
    count, rows, cols = f.shape
    return pl.pallas_call(
        functools.partial(chunk_kernel, m, n),
        out_shape=(
            jax.ShapeDtypeStruct((m * n, 1, WIDTH), F32),
            jax.ShapeDtypeStruct((1, cols), F32),
            jax.ShapeDtypeStruct((rows + TILE, cols), F32),
            jax.ShapeDtypeStruct((2, count, cols), F32),
            jax.ShapeDtypeStruct((count + 1, 2, cols), F32),
        ),
        in_specs=[VMEM] * 8,
        out_specs=[ANY] + [VMEM] * 4,
        scratch_shapes=[pltpu.VMEM((m * n, 1, WIDTH), F32), pltpu.SemaphoreType.DMA],
        compiler_params=PARAMS,
        name="chunks",
    )(f, part, rim, near, far, start, end, strip)


def final_kernel(
    m, n, got_ref, near_corner_ref, rest_ref, f_ref, drift_ref, near_ref, far_ref, start_ref, end_ref,
    strip_ref, tail_ref, lead_ref, ratio_out, res_out, grad_out, ratio_ref, resid, grad, outer, rim, head_ref, sem,
):
    halo = Halo(m, near_ref, far_ref, start_ref, end_ref, rest_ref)
    count, rows, cols = f_ref.shape
    tiles = rows // TILE
    path = lax.axis_index("path")
    first, last = halo.first, halo.last
    path_lo = jnp.where(first, path, path - 1)
    path_hi = jnp.where(last, path, path + 1)

    def gathered(p):
        total = got_ref[p, :, 0:LANES]
        for i in range(1, n):
            total += got_ref[i * m + p, :, 0:LANES]
        return jnp.broadcast_to(total, (TILE, LANES))

    mine = gathered(path)
    lower = gathered(path_lo)
    upper = gathered(path_hi)
    lane = iota((TILE, LANES), 1)
    sub = iota((TILE, LANES), 0)

    def shift(x, k):
        return pltpu.roll(x, k % LANES, 1)

    def ratios(x):
        return jnp.sqrt(x + EPS) / jnp.sqrt(shift(x, -count) + EPS)

    low = jnp.where(first, 0.0, shift(ratios(lower), 1 - count))
    high = jnp.where(last, 0.0, shift(ratios(upper), count + 1))
    own = ratios(mine)
    ratio_ref[...] = own[0, 0:count]
    copies = [pltpu.make_async_copy(ratio_ref, ratio_out, sem.at[2, 0])]
    copies[0].start()
    ratio = jnp.where(lane == 0, low, jnp.where(lane == count + 1, high, shift(own, 1)))

    def splat(t):
        return jnp.broadcast_to(jnp.sum(jnp.where(lane == t, ratio, 0.0), axis=1, keepdims=True), (TILE, LANES))

    def widen(x):
        return jnp.concatenate([x] * (cols // LANES), axis=1)

    scale = [widen(splat(t)) for t in range(count + 2)]
    column = jnp.sum(jnp.where(lane == sub + 1, ratio, 0.0), axis=1, keepdims=True)
    row = iota((TILE, cols), 0)
    near, far = near_corner_ref[...], rest_ref[rows : rows + 1, :]
    corners = (
        (
            pick(first, strip_ref[count, 0:1, :], pick(halo.odd, near, far)),
            pick(last, strip_ref[count, 1:2, :], pick(halo.odd, far, near)),
        ),
        (lead_ref[count, 0:1, :], lead_ref[count, 1:2, :]),
    )

    def at(k):
        return pl.ds(TILE * k, TILE)

    def value(s, k):
        if s < 0:
            return halo.below(at(k)) if s == -1 else halo.below_2(at(k))
        if s >= count:
            return halo.above(at(k)) if s == count else halo.above_2(at(k))
        return f_ref[s, at(k), :]

    def residual_of(s):
        for k in range(tiles):
            if 0 <= s < count:
                drift = drift_ref[s, at(k), :]
                if k == 0:
                    drift += jnp.where(row == 0, tail_ref[1, s : s + 1, :], 0.0)
                if k == tiles - 1:
                    drift += jnp.where(row == TILE - 1, lead_ref[s, 0:1, :], 0.0)
            else:
                slot = 0 if s < 0 else 1
                c = outer[slot, at(k), :]
                above = outer[slot, TILE * k - 1 : TILE * k, :] if k > 0 else corners[0][slot]
                under = outer[slot, TILE * (k + 1) : TILE * (k + 1) + 1, :] if k < tiles - 1 else corners[1][slot]
                up = jnp.where(row == 0, above, pltpu.roll(c, 1, 0))
                dn = jnp.where(row == TILE - 1, under, pltpu.roll(c, TILE - 1, 0))
                drift = up + dn + sides(c) - 3.0 * c - c * c * c
            resid[s + 1, at(k + 1), :] = scale[s + 1] * (value(s + 1, k) - value(s - 1, k)) - drift

    def send(src, dst, slot):
        copy = pltpu.make_async_copy(src, dst, slot)
        copy.start()
        copies.append(copy)

    pieces = PIECES if count % PIECES == 0 else 1
    step = count // pieces
    for i in range(pieces):
        for s in range(i * step, (i + 1) * step):
            residual_of(s)
        span = pl.ds(i * step, step)
        send(resid.at[pl.ds(i * step + 1, step), pl.ds(TILE, rows)], res_out.at[span], sem.at[0, i])

    for k in range(tiles):
        outer[0, at(k), :] = halo.below(at(k))
        outer[1, at(k), :] = halo.above(at(k))
    residual_of(-1)
    residual_of(count)

    for s in range(count):
        rim[0, s : s + 1, :] = f_ref[s, 0:1, :]
        rim[1, s : s + 1, :] = f_ref[s, rows - 1 : rows, :]
        for r in range(2):
            head_ref[r, s : s + 1, :] = lead_ref[s, r : r + 1, :]
    for far, mid, near, (low, high), place in (
        (tail_ref[0], tail_ref[1], rim[0], corners[0], TILE - 1),
        (head_ref[1], head_ref[0], rim[1], corners[1], TILE + rows),
    ):
        ahead = jnp.where(row == count - 1, high, pltpu.roll(mid, count - 1, 0))
        behind = jnp.where(row == 0, low, pltpu.roll(mid, 1, 0))
        edge = column * (ahead - behind) - (far + near + sides(mid) - 3.0 * mid - mid * mid * mid)
        for s in range(count):
            resid[s + 1, place : place + 1, :] = edge[s : s + 1, :]

    def gradient_of(s):
        r = [resid[s + 1, at(k + 1), :] for k in range(tiles)]
        down = [resid[s + 1, TILE - 1 : TILE, :]] + [pltpu.roll(x, 1, 0) for x in r]
        up = [pltpu.roll(x, TILE - 1, 0) for x in r] + [resid[s + 1, TILE + rows : TILE + rows + 1, :]]
        for k in range(tiles):
            c = f_ref[s, at(k), :]
            around = jnp.where(row == 0, down[k], down[k + 1]) + jnp.where(row == TILE - 1, up[k + 1], up[k]) + sides(r[k])
            out = scale[s] * resid[s, at(k + 1), :] - scale[s + 2] * resid[s + 2, at(k + 1), :]
            grad[s, at(k), :] = out - (around - (3.0 + 3.0 * c * c) * r[k])

    for i in range(pieces):
        for s in range(i * step, (i + 1) * step):
            gradient_of(s)
        span = pl.ds(i * step, step)
        send(grad.at[span], grad_out.at[span], sem.at[1, i])
    for copy in copies:
        copy.wait()


def final(m, n, got, corners, f, drift, slabs, strips):
    count, rows, cols = f.shape
    big = jax.ShapeDtypeStruct(f.shape, F32)
    return pl.pallas_call(
        functools.partial(final_kernel, m, n),
        out_shape=(jax.ShapeDtypeStruct((count,), F32), big, big),
        in_specs=[VMEM] * 12,
        out_specs=(ANY, ANY, ANY),
        scratch_shapes=[
            pltpu.VMEM((count,), F32),
            pltpu.VMEM((count + 2, rows + 2 * TILE, cols), F32),
            pltpu.VMEM(f.shape, F32),
            pltpu.VMEM((2, rows, cols), F32),
            pltpu.VMEM((2, count, cols), F32),
            pltpu.VMEM((2, count, cols), F32),
            pltpu.SemaphoreType.DMA((3, PIECES)),
        ],
        compiler_params=PARAMS,
        name="final",
    )(got, *corners, f, drift, *slabs, *strips)


def swap(x, kind):
    size = lax.axis_size("path")
    return lax.ppermute(x, "path", [((i + kind) % size, ((i ^ 1) + kind) % size) for i in range(size)])


def ring(x, step):
    size = lax.axis_size("space")
    return lax.ppermute(x, "space", [(i, (i + step) % size) for i in range(size)])


def body(m, n, f, start, end):
    near, far = slices(f)
    strip = ring(tail_rows(f, start, end), 1)
    far = swap(far, 1)
    near = swap(near, 0)
    part, drift, rim = interior(f)
    slabs = near, far, start, end
    send, near_corner, rest, tail, head = chunks(m, n, f, part, rim, *slabs, strip)
    got = lax.all_to_all(send, ("space", "path"), 0, 0, tiled=True)
    lead = ring(head, -1)
    late = swap(near_corner, 0), swap(rest, 1)
    return final(m, n, got, late, f, drift, slabs, (strip, tail, lead))


def solution(mesh):
    m, n = mesh.shape["path"], mesh.shape["space"]
    in_specs = (P("path", "space", None), P("space", None), P("space", None))
    out_specs = (P("path"), P("path", "space", None), P("path", "space", None))
    return jax.shard_map(
        functools.partial(body, m, n), mesh=mesh, in_specs=in_specs, out_specs=out_specs, check_vma=False
    )
```

```python
import functools

import jax
import jax.numpy as jnp
from jax import lax
from jax.experimental import pallas as pl
from jax.experimental.pallas import tpu as pltpu
from jax.sharding import PartitionSpec as P

F32 = jnp.float32
LANES = 128
TILE = 8
EPS = 1e-06
VMEM = pl.BlockSpec(memory_space=pltpu.VMEM)
ANY = pl.BlockSpec(memory_space=pl.ANY)
PIECES = 4
WIDTH = 384
PARAMS = pltpu.CompilerParams(vmem_limit_bytes=16 * 2**20)


def lanes_sum(x):
    parts = [x[:, i : i + LANES] for i in range(0, x.shape[1], LANES)]
    while len(parts) > 1:
        parts = [a + b for a, b in zip(parts[::2], parts[1::2])] + parts[len(parts) & ~1 :]
    return parts[0]


def sides(x):
    cols = x.shape[1]
    return pltpu.roll(x, 1, 1) + pltpu.roll(x, cols - 1, 1)


def iota(shape, dim):
    return lax.broadcasted_iota(jnp.int32, shape, dim)


def odd(axis):
    return lax.rem(lax.axis_index(axis), 2) == 1


def pick(flag, x, y):
    return jnp.where(flag, x, y)


def slices_kernel(f_ref, near_ref, far_ref, rest_ref):
    count = f_ref.shape[0]
    flag = odd("path")
    base = pick(flag, 0, count - 2)
    for s in range(2):
        near_ref[s] = f_ref[base + s]
    far_ref[...] = f_ref[pick(flag, count - 1, 0)]
    rest_ref[...] = f_ref[pick(flag, count - 2, 1)]


def tail_kernel(f_ref, start_ref, end_ref, tail_ref):
    count, rows, _ = f_ref.shape
    tail_ref[count, 0:1, :] = start_ref[rows - 1 :, :]
    tail_ref[count, 1:2, :] = end_ref[rows - 1 :, :]
    for s in range(count):
        tail_ref[s] = f_ref[s, rows - 2 :, :]


def slices(f):
    count, rows, cols = f.shape
    return pl.pallas_call(
        slices_kernel,
        out_shape=(jax.ShapeDtypeStruct((2, rows, cols), F32),) + (jax.ShapeDtypeStruct((rows, cols), F32),) * 2,
        in_specs=[VMEM],
        out_specs=[VMEM] * 3,
        compiler_params=PARAMS,
        name="slices",
    )(f)


def tail_rows(f, start, end):
    count, rows, cols = f.shape
    return pl.pallas_call(
        tail_kernel,
        out_shape=jax.ShapeDtypeStruct((count + 1, 2, cols), F32),
        in_specs=[VMEM] * 3,
        out_specs=VMEM,
        compiler_params=PARAMS,
        name="tail_rows",
    )(f, start, end)


class Halo:
    def __init__(self, m, near_ref, far_ref, start_ref, end_ref, rest_ref=None):
        self.odd = odd("path")
        self.first = lax.axis_index("path") == 0
        self.last = lax.axis_index("path") == m - 1
        self.near, self.far, self.rest = near_ref, far_ref, rest_ref
        self.start, self.end = start_ref, end_ref

    def below(self, at):
        return pick(self.first, self.start[at, :], pick(self.odd, self.near[1, at, :], self.far[at, :]))

    def above(self, at):
        return pick(self.last, self.end[at, :], pick(self.odd, self.far[at, :], self.near[0, at, :]))

    def below_2(self, at):
        return pick(self.odd, self.near[0, at, :], self.rest[at, :])

    def above_2(self, at):
        return pick(self.odd, self.rest[at, :], self.near[1, at, :])


def interior_kernel(f_ref, part_ref, drift_ref, rim_ref):
    count, rows, cols = f_ref.shape
    tiles = rows // TILE
    row = iota((TILE, cols), 0)
    part_ref[...] = jnp.zeros_like(part_ref)

    def drift_sum(s, _):
        total = jnp.zeros((TILE, LANES), F32)
        for k in range(tiles):
            c = f_ref[s, pl.ds(TILE * k, TILE), :]
            above = f_ref[s, pl.ds(TILE * k - 1, 1), :] if k > 0 else 0.0
            under = f_ref[s, pl.ds(TILE * (k + 1), 1), :] if k < tiles - 1 else 0.0
            up = jnp.where(row == 0, above, pltpu.roll(c, 1, 0))
            dn = jnp.where(row == TILE - 1, under, pltpu.roll(c, TILE - 1, 0))
            drift = up + dn + sides(c) - 3.0 * c - c * c * c
            drift_ref[s, pl.ds(TILE * k, TILE), :] = drift
            if k == 0:
                rim_ref[0, pl.ds(s, 1), :] = drift[0:1]
                rim_ref[1, pl.ds(s, 1), :] = c[0:1]
                drift = jnp.where(row == 0, 0.0, drift)
            if k == tiles - 1:
                drift = jnp.where(row == TILE - 1, 0.0, drift)
            total += lanes_sum(drift * drift)
        part_ref[pl.ds(s, 1), :] = jnp.sum(total, axis=0, keepdims=True)
        return 0

    def tangent_sum(s, _):
        total = jnp.zeros((TILE, LANES), F32)
        for k in range(tiles):
            tangent = f_ref[s + 1, pl.ds(TILE * k, TILE), :] - f_ref[s - 1, pl.ds(TILE * k, TILE), :]
            total += lanes_sum(tangent * tangent)
        part_ref[pl.ds(count + s, 1), :] = jnp.sum(total, axis=0, keepdims=True)
        return 0

    lax.fori_loop(0, count, drift_sum, 0)
    lax.fori_loop(1, count - 1, tangent_sum, 0)


def interior(f):
    count, rows, cols = f.shape
    return pl.pallas_call(
        interior_kernel,
        out_shape=(
            jax.ShapeDtypeStruct((2 * count, LANES), F32),
            jax.ShapeDtypeStruct(f.shape, F32),
            jax.ShapeDtypeStruct((2, count, cols), F32),
        ),
        in_specs=[VMEM],
        out_specs=[VMEM] * 3,
        cost_estimate=pl.CostEstimate(flops=20 * count * rows * cols, transcendentals=0, bytes_accessed=8 * count * rows * cols),
        compiler_params=PARAMS,
        name="interior",
    )(f)


def chunk_kernel(
    m, n, f_ref, part_ref, rim_ref, near_ref, far_ref, start_ref, end_ref, strip_ref,
    out_ref, near_corner_ref, far_corner_ref, tail_ref, head_ref, lines, sem,
):
    halo = Halo(m, near_ref, far_ref, start_ref, end_ref)
    count, rows, cols = f_ref.shape
    tiles = rows // TILE

    for s in range(count):
        for r in range(2):
            tail_ref[r, s : s + 1, :] = strip_ref[s, r : r + 1, :]
    r0, r1 = tail_ref[0], tail_ref[1]

    drift_a = r0 + rim_ref[1] + sides(r1) - 3.0 * r1 - r1 * r1 * r1
    drift_b = rim_ref[0] + r1
    drift = part_ref[0:count, :] + lanes_sum(drift_a * drift_a) + lanes_sum(drift_b * drift_b)

    totals = [jnp.zeros((TILE, LANES), F32) for _ in range(2)]
    for k in range(tiles):
        at = pl.ds(TILE * k, TILE)
        tangents = (f_ref[1, at, :] - halo.below(at), halo.above(at) - f_ref[count - 2, at, :])
        totals = [a + lanes_sum(t * t) for a, t in zip(totals, tangents)]
    head_sum, tail_sum = [jnp.sum(a, axis=0, keepdims=True) for a in totals]
    sub = iota((TILE, LANES), 0)
    tangent = part_ref[count : 2 * count, :]
    tangent = jnp.where(sub == 0, head_sum, jnp.where(sub == count - 1, tail_sum, tangent))

    lane = iota((TILE, LANES), 1)
    spread = jnp.where(lane == sub, jnp.sum(drift, axis=1, keepdims=True), 0.0)
    spread += jnp.where(lane == sub + count, jnp.sum(tangent, axis=1, keepdims=True), 0.0)
    line = jnp.sum(spread, axis=0, keepdims=True)

    if WIDTH > LANES:
        line = jnp.concatenate([line, jnp.zeros((1, WIDTH - LANES), F32)], axis=1)
    for j in range(m * n):
        lines[j] = line
    copy = pltpu.make_async_copy(lines, out_ref, sem)
    copy.start()

    for ref, low in ((near_corner_ref, halo.odd), (far_corner_ref, jnp.logical_not(halo.odd))):
        ref[...] = tail_ref[1, pl.ds(pick(low, 0, count - 1), 1), :]
    for s in range(count):
        head_ref[s] = f_ref[s, 0:2, :]
    head_ref[count, 0:1, :] = halo.below(pl.ds(0, 1))
    head_ref[count, 1:2, :] = halo.above(pl.ds(0, 1))
    copy.wait()


def chunks(m, n, f, part, rim, near, far, start, end, strip):
    count, rows, cols = f.shape
    return pl.pallas_call(
        functools.partial(chunk_kernel, m, n),
        out_shape=(
            jax.ShapeDtypeStruct((m * n, 1, WIDTH), F32),
            jax.ShapeDtypeStruct((1, cols), F32),
            jax.ShapeDtypeStruct((1, cols), F32),
            jax.ShapeDtypeStruct((2, count, cols), F32),
            jax.ShapeDtypeStruct((count + 1, 2, cols), F32),
        ),
        in_specs=[VMEM] * 8,
        out_specs=[ANY] + [VMEM] * 4,
        scratch_shapes=[pltpu.VMEM((m * n, 1, WIDTH), F32), pltpu.SemaphoreType.DMA],
        compiler_params=PARAMS,
        name="chunks",
    )(f, part, rim, near, far, start, end, strip)


def final_kernel(
    m, n, got_ref, near_corner_ref, far_corner_ref, rest_ref, f_ref, drift_ref, near_ref, far_ref, start_ref, end_ref,
    strip_ref, tail_ref, lead_ref, ratio_out, res_out, grad_out, ratio_ref, resid, grad, outer, rim, head_ref, sem,
):
    halo = Halo(m, near_ref, far_ref, start_ref, end_ref, rest_ref)
    count, rows, cols = f_ref.shape
    tiles = rows // TILE
    path = lax.axis_index("path")
    first, last = halo.first, halo.last
    path_lo = jnp.where(first, path, path - 1)
    path_hi = jnp.where(last, path, path + 1)

    def gathered(p):
        total = got_ref[p, :, 0:LANES]
        for i in range(1, n):
            total += got_ref[i * m + p, :, 0:LANES]
        return jnp.broadcast_to(total, (TILE, LANES))

    mine = gathered(path)
    lower = gathered(path_lo)
    upper = gathered(path_hi)
    lane = iota((TILE, LANES), 1)
    sub = iota((TILE, LANES), 0)

    def shift(x, k):
        return pltpu.roll(x, k % LANES, 1)

    def ratios(x):
        return jnp.sqrt(x + EPS) / jnp.sqrt(shift(x, -count) + EPS)

    low = jnp.where(first, 0.0, shift(ratios(lower), 1 - count))
    high = jnp.where(last, 0.0, shift(ratios(upper), count + 1))
    own = ratios(mine)
    ratio_ref[...] = own[0, 0:count]
    copies = [pltpu.make_async_copy(ratio_ref, ratio_out, sem.at[2, 0])]
    copies[0].start()
    ratio = jnp.where(lane == 0, low, jnp.where(lane == count + 1, high, shift(own, 1)))

    def splat(t):
        return jnp.broadcast_to(jnp.sum(jnp.where(lane == t, ratio, 0.0), axis=1, keepdims=True), (TILE, LANES))

    def widen(x):
        return jnp.concatenate([x] * (cols // LANES), axis=1)

    scale = [widen(splat(t)) for t in range(count + 2)]
    column = jnp.sum(jnp.where(lane == sub + 1, ratio, 0.0), axis=1, keepdims=True)
    row = iota((TILE, cols), 0)
    near, far = near_corner_ref[...], far_corner_ref[...]
    corners = (
        (
            pick(first, strip_ref[count, 0:1, :], pick(halo.odd, near, far)),
            pick(last, strip_ref[count, 1:2, :], pick(halo.odd, far, near)),
        ),
        (lead_ref[count, 0:1, :], lead_ref[count, 1:2, :]),
    )

    def at(k):
        return pl.ds(TILE * k, TILE)

    def value(s, k):
        if s < 0:
            return halo.below(at(k)) if s == -1 else halo.below_2(at(k))
        if s >= count:
            return halo.above(at(k)) if s == count else halo.above_2(at(k))
        return f_ref[s, at(k), :]

    def residual_of(s):
        for k in range(tiles):
            if 0 <= s < count:
                drift = drift_ref[s, at(k), :]
                if k == 0:
                    drift += jnp.where(row == 0, tail_ref[1, s : s + 1, :], 0.0)
                if k == tiles - 1:
                    drift += jnp.where(row == TILE - 1, lead_ref[s, 0:1, :], 0.0)
            else:
                slot = 0 if s < 0 else 1
                c = outer[slot, at(k), :]
                above = outer[slot, TILE * k - 1 : TILE * k, :] if k > 0 else corners[0][slot]
                under = outer[slot, TILE * (k + 1) : TILE * (k + 1) + 1, :] if k < tiles - 1 else corners[1][slot]
                up = jnp.where(row == 0, above, pltpu.roll(c, 1, 0))
                dn = jnp.where(row == TILE - 1, under, pltpu.roll(c, TILE - 1, 0))
                drift = up + dn + sides(c) - 3.0 * c - c * c * c
            resid[s + 1, at(k + 1), :] = scale[s + 1] * (value(s + 1, k) - value(s - 1, k)) - drift

    def send(src, dst, slot):
        copy = pltpu.make_async_copy(src, dst, slot)
        copy.start()
        copies.append(copy)

    pieces = PIECES if count % PIECES == 0 else 1
    step = count // pieces
    for i in range(pieces):
        for s in range(i * step, (i + 1) * step):
            residual_of(s)
        span = pl.ds(i * step, step)
        send(resid.at[pl.ds(i * step + 1, step), pl.ds(TILE, rows)], res_out.at[span], sem.at[0, i])

    for k in range(tiles):
        outer[0, at(k), :] = halo.below(at(k))
        outer[1, at(k), :] = halo.above(at(k))
    residual_of(-1)
    residual_of(count)

    for s in range(count):
        rim[0, s : s + 1, :] = f_ref[s, 0:1, :]
        rim[1, s : s + 1, :] = f_ref[s, rows - 1 : rows, :]
        for r in range(2):
            head_ref[r, s : s + 1, :] = lead_ref[s, r : r + 1, :]
    for far, mid, near, (low, high), place in (
        (tail_ref[0], tail_ref[1], rim[0], corners[0], TILE - 1),
        (head_ref[1], head_ref[0], rim[1], corners[1], TILE + rows),
    ):
        ahead = jnp.where(row == count - 1, high, pltpu.roll(mid, count - 1, 0))
        behind = jnp.where(row == 0, low, pltpu.roll(mid, 1, 0))
        edge = column * (ahead - behind) - (far + near + sides(mid) - 3.0 * mid - mid * mid * mid)
        for s in range(count):
            resid[s + 1, place : place + 1, :] = edge[s : s + 1, :]

    def gradient_of(s):
        r = [resid[s + 1, at(k + 1), :] for k in range(tiles)]
        down = [resid[s + 1, TILE - 1 : TILE, :]] + [pltpu.roll(x, 1, 0) for x in r]
        up = [pltpu.roll(x, TILE - 1, 0) for x in r] + [resid[s + 1, TILE + rows : TILE + rows + 1, :]]
        for k in range(tiles):
            c = f_ref[s, at(k), :]
            around = jnp.where(row == 0, down[k], down[k + 1]) + jnp.where(row == TILE - 1, up[k + 1], up[k]) + sides(r[k])
            out = scale[s] * resid[s, at(k + 1), :] - scale[s + 2] * resid[s + 2, at(k + 1), :]
            grad[s, at(k), :] = out - (around - (3.0 + 3.0 * c * c) * r[k])

    for i in range(pieces):
        for s in range(i * step, (i + 1) * step):
            gradient_of(s)
        span = pl.ds(i * step, step)
        send(grad.at[span], grad_out.at[span], sem.at[1, i])
    for copy in copies:
        copy.wait()


def final(m, n, got, corners, f, drift, slabs, strips):
    count, rows, cols = f.shape
    big = jax.ShapeDtypeStruct(f.shape, F32)
    return pl.pallas_call(
        functools.partial(final_kernel, m, n),
        out_shape=(jax.ShapeDtypeStruct((count,), F32), big, big),
        in_specs=[VMEM] * 13,
        out_specs=(ANY, ANY, ANY),
        scratch_shapes=[
            pltpu.VMEM((count,), F32),
            pltpu.VMEM((count + 2, rows + 2 * TILE, cols), F32),
            pltpu.VMEM(f.shape, F32),
            pltpu.VMEM((2, rows, cols), F32),
            pltpu.VMEM((2, count, cols), F32),
            pltpu.VMEM((2, count, cols), F32),
            pltpu.SemaphoreType.DMA((3, PIECES)),
        ],
        compiler_params=PARAMS,
        name="final",
    )(got, *corners, f, drift, *slabs, *strips)


def swap(x, kind):
    size = lax.axis_size("path")
    return lax.ppermute(x, "path", [((i + kind) % size, ((i ^ 1) + kind) % size) for i in range(size)])


def ring(x, step):
    size = lax.axis_size("space")
    return lax.ppermute(x, "space", [(i, (i + step) % size) for i in range(size)])


def body(m, n, f, start, end):
    near, far, rest = slices(f)
    strip = ring(tail_rows(f, start, end), 1)
    far = swap(far, 1)
    near = swap(near, 0)
    rest = swap(rest, 1)
    part, drift, rim = interior(f)
    slabs = near, far, start, end
    send, near_corner, far_corner, tail, head = chunks(m, n, f, part, rim, *slabs, strip)
    got = lax.all_to_all(send, ("space", "path"), 0, 0, tiled=True)
    near_corner, far_corner = swap(near_corner, 0), swap(far_corner, 1)
    head, near_corner, far_corner = lax.optimization_barrier((head, near_corner, far_corner))
    lead = ring(head, -1)
    return final(m, n, got, (near_corner, far_corner, rest), f, drift, slabs, (strip, tail, lead))


def solution(mesh):
    m, n = mesh.shape["path"], mesh.shape["space"]
    in_specs = (P("path", "space", None), P("space", None), P("space", None))
    out_specs = (P("path"), P("path", "space", None), P("path", "space", None))
    return jax.shard_map(
        functools.partial(body, m, n), mesh=mesh, in_specs=in_specs, out_specs=out_specs, check_vma=False
    )
```

```python
import functools

import jax
import jax.numpy as jnp
from jax import lax
from jax.experimental import pallas as pl
from jax.experimental.pallas import tpu as pltpu
from jax.sharding import PartitionSpec as P

F32 = jnp.float32
LANES = 128
TILE = 8
EPS = 1e-06
VMEM = pl.BlockSpec(memory_space=pltpu.VMEM)
ANY = pl.BlockSpec(memory_space=pl.ANY)
PIECES = 4
WIDTH = 384
PARAMS = pltpu.CompilerParams(vmem_limit_bytes=16 * 2**20)


def lanes_sum(x):
    parts = [x[:, i : i + LANES] for i in range(0, x.shape[1], LANES)]
    while len(parts) > 1:
        parts = [a + b for a, b in zip(parts[::2], parts[1::2])] + parts[len(parts) & ~1 :]
    return parts[0]


def sides(x):
    cols = x.shape[1]
    return pltpu.roll(x, 1, 1) + pltpu.roll(x, cols - 1, 1)


def iota(shape, dim):
    return lax.broadcasted_iota(jnp.int32, shape, dim)


def odd(axis):
    return lax.rem(lax.axis_index(axis), 2) == 1


def pick(flag, x, y):
    return jnp.where(flag, x, y)


def slices_kernel(f_ref, near_ref, far_lo_ref, far_hi_ref, rest_ref):
    count = f_ref.shape[0]
    flag = odd("path")
    base = pick(flag, 0, count - 2)
    for s in range(2):
        near_ref[s] = f_ref[base + s]
    half = far_lo_ref.shape[0]
    far_lo_ref[...] = f_ref[pick(flag, count - 1, 0), :half]
    far_hi_ref[...] = f_ref[pick(flag, count - 1, 0), half:]
    rest_ref[...] = f_ref[pick(flag, count - 2, 1)]


def tail_kernel(f_ref, start_ref, end_ref, tail_ref):
    count, rows, _ = f_ref.shape
    tail_ref[count, 0:1, :] = start_ref[rows - 1 :, :]
    tail_ref[count, 1:2, :] = end_ref[rows - 1 :, :]
    for s in range(count):
        tail_ref[s] = f_ref[s, rows - 2 :, :]


def slices(f):
    count, rows, cols = f.shape
    return pl.pallas_call(
        slices_kernel,
        out_shape=(
            jax.ShapeDtypeStruct((2, rows, cols), F32),
            jax.ShapeDtypeStruct((rows // 2, cols), F32),
            jax.ShapeDtypeStruct((rows // 2, cols), F32),
            jax.ShapeDtypeStruct((rows, cols), F32),
        ),
        in_specs=[VMEM],
        out_specs=[VMEM] * 4,
        compiler_params=PARAMS,
        name="slices",
    )(f)


def tail_rows(f, start, end):
    count, rows, cols = f.shape
    return pl.pallas_call(
        tail_kernel,
        out_shape=jax.ShapeDtypeStruct((count + 1, 2, cols), F32),
        in_specs=[VMEM] * 3,
        out_specs=VMEM,
        compiler_params=PARAMS,
        name="tail_rows",
    )(f, start, end)


class Halo:
    def __init__(self, m, near_ref, far_lo_ref, far_hi_ref, start_ref, end_ref, rest_ref=None):
        self.odd = odd("path")
        self.first = lax.axis_index("path") == 0
        self.last = lax.axis_index("path") == m - 1
        self.near, self.halves, self.rest = near_ref, (far_lo_ref, far_hi_ref), rest_ref
        self.start, self.end = start_ref, end_ref

    def far(self, at):
        half = self.halves[0].shape[0]
        return self.halves[at.start // half][pl.ds(at.start % half, at.size), :]

    def below(self, at):
        return pick(self.first, self.start[at, :], pick(self.odd, self.near[1, at, :], self.far(at)))

    def above(self, at):
        return pick(self.last, self.end[at, :], pick(self.odd, self.far(at), self.near[0, at, :]))

    def below_2(self, at):
        return pick(self.odd, self.near[0, at, :], self.rest[at, :])

    def above_2(self, at):
        return pick(self.odd, self.rest[at, :], self.near[1, at, :])


def interior_kernel(f_ref, part_ref, drift_ref, rim_ref):
    count, rows, cols = f_ref.shape
    tiles = rows // TILE
    row = iota((TILE, cols), 0)
    part_ref[...] = jnp.zeros_like(part_ref)

    def drift_sum(s, _):
        total = jnp.zeros((TILE, LANES), F32)
        for k in range(tiles):
            c = f_ref[s, pl.ds(TILE * k, TILE), :]
            above = f_ref[s, pl.ds(TILE * k - 1, 1), :] if k > 0 else 0.0
            under = f_ref[s, pl.ds(TILE * (k + 1), 1), :] if k < tiles - 1 else 0.0
            up = jnp.where(row == 0, above, pltpu.roll(c, 1, 0))
            dn = jnp.where(row == TILE - 1, under, pltpu.roll(c, TILE - 1, 0))
            drift = up + dn + sides(c) - 3.0 * c - c * c * c
            drift_ref[s, pl.ds(TILE * k, TILE), :] = drift
            if k == 0:
                rim_ref[0, pl.ds(s, 1), :] = drift[0:1]
                rim_ref[1, pl.ds(s, 1), :] = c[0:1]
                drift = jnp.where(row == 0, 0.0, drift)
            if k == tiles - 1:
                drift = jnp.where(row == TILE - 1, 0.0, drift)
            total += lanes_sum(drift * drift)
        part_ref[pl.ds(s, 1), :] = jnp.sum(total, axis=0, keepdims=True)
        return 0

    def tangent_sum(s, _):
        total = jnp.zeros((TILE, LANES), F32)
        for k in range(tiles):
            tangent = f_ref[s + 1, pl.ds(TILE * k, TILE), :] - f_ref[s - 1, pl.ds(TILE * k, TILE), :]
            total += lanes_sum(tangent * tangent)
        part_ref[pl.ds(count + s, 1), :] = jnp.sum(total, axis=0, keepdims=True)
        return 0

    lax.fori_loop(0, count, drift_sum, 0)
    lax.fori_loop(1, count - 1, tangent_sum, 0)


def interior(f):
    count, rows, cols = f.shape
    return pl.pallas_call(
        interior_kernel,
        out_shape=(
            jax.ShapeDtypeStruct((2 * count, LANES), F32),
            jax.ShapeDtypeStruct(f.shape, F32),
            jax.ShapeDtypeStruct((2, count, cols), F32),
        ),
        in_specs=[VMEM],
        out_specs=[VMEM] * 3,
        cost_estimate=pl.CostEstimate(flops=20 * count * rows * cols, transcendentals=0, bytes_accessed=8 * count * rows * cols),
        compiler_params=PARAMS,
        name="interior",
    )(f)


def chunk_kernel(
    m, n, f_ref, part_ref, rim_ref, near_ref, far_lo_ref, far_hi_ref, start_ref, end_ref, strip_ref,
    out_ref, near_corner_ref, far_corner_ref, tail_ref, head_ref, lines, sem,
):
    halo = Halo(m, near_ref, far_lo_ref, far_hi_ref, start_ref, end_ref)
    count, rows, cols = f_ref.shape
    tiles = rows // TILE

    for s in range(count):
        for r in range(2):
            tail_ref[r, s : s + 1, :] = strip_ref[s, r : r + 1, :]
    r0, r1 = tail_ref[0], tail_ref[1]

    drift_a = r0 + rim_ref[1] + sides(r1) - 3.0 * r1 - r1 * r1 * r1
    drift_b = rim_ref[0] + r1
    drift = part_ref[0:count, :] + lanes_sum(drift_a * drift_a) + lanes_sum(drift_b * drift_b)

    totals = [jnp.zeros((TILE, LANES), F32) for _ in range(2)]
    for k in range(tiles):
        at = pl.ds(TILE * k, TILE)
        tangents = (f_ref[1, at, :] - halo.below(at), halo.above(at) - f_ref[count - 2, at, :])
        totals = [a + lanes_sum(t * t) for a, t in zip(totals, tangents)]
    head_sum, tail_sum = [jnp.sum(a, axis=0, keepdims=True) for a in totals]
    sub = iota((TILE, LANES), 0)
    tangent = part_ref[count : 2 * count, :]
    tangent = jnp.where(sub == 0, head_sum, jnp.where(sub == count - 1, tail_sum, tangent))

    lane = iota((TILE, LANES), 1)
    spread = jnp.where(lane == sub, jnp.sum(drift, axis=1, keepdims=True), 0.0)
    spread += jnp.where(lane == sub + count, jnp.sum(tangent, axis=1, keepdims=True), 0.0)
    line = jnp.sum(spread, axis=0, keepdims=True)

    if WIDTH > LANES:
        line = jnp.concatenate([line, jnp.zeros((1, WIDTH - LANES), F32)], axis=1)
    for j in range(m * n):
        lines[j] = line
    copy = pltpu.make_async_copy(lines, out_ref, sem)
    copy.start()

    for ref, low in ((near_corner_ref, halo.odd), (far_corner_ref, jnp.logical_not(halo.odd))):
        ref[...] = tail_ref[1, pl.ds(pick(low, 0, count - 1), 1), :]
    for s in range(count):
        head_ref[s] = f_ref[s, 0:2, :]
    head_ref[count, 0:1, :] = halo.below(pl.ds(0, 1))
    head_ref[count, 1:2, :] = halo.above(pl.ds(0, 1))
    copy.wait()


def chunks(m, n, f, part, rim, *halo):
    count, rows, cols = f.shape
    return pl.pallas_call(
        functools.partial(chunk_kernel, m, n),
        out_shape=(
            jax.ShapeDtypeStruct((m * n, 1, WIDTH), F32),
            jax.ShapeDtypeStruct((1, cols), F32),
            jax.ShapeDtypeStruct((1, cols), F32),
            jax.ShapeDtypeStruct((2, count, cols), F32),
            jax.ShapeDtypeStruct((count + 1, 2, cols), F32),
        ),
        in_specs=[VMEM] * 9,
        out_specs=[ANY] + [VMEM] * 4,
        scratch_shapes=[pltpu.VMEM((m * n, 1, WIDTH), F32), pltpu.SemaphoreType.DMA],
        compiler_params=PARAMS,
        name="chunks",
    )(f, part, rim, *halo)


def final_kernel(
    m, n, got_ref, near_corner_ref, far_corner_ref, rest_ref, f_ref, drift_ref, near_ref, far_lo_ref, far_hi_ref, start_ref, end_ref,
    strip_ref, tail_ref, lead_ref, ratio_out, res_out, grad_out, ratio_ref, resid, grad, outer, rim, head_ref, sem,
):
    halo = Halo(m, near_ref, far_lo_ref, far_hi_ref, start_ref, end_ref, rest_ref)
    count, rows, cols = f_ref.shape
    tiles = rows // TILE
    path = lax.axis_index("path")
    first, last = halo.first, halo.last
    path_lo = jnp.where(first, path, path - 1)
    path_hi = jnp.where(last, path, path + 1)

    def gathered(p):
        total = got_ref[p, :, 0:LANES]
        for i in range(1, n):
            total += got_ref[i * m + p, :, 0:LANES]
        return jnp.broadcast_to(total, (TILE, LANES))

    mine = gathered(path)
    lower = gathered(path_lo)
    upper = gathered(path_hi)
    lane = iota((TILE, LANES), 1)
    sub = iota((TILE, LANES), 0)

    def shift(x, k):
        return pltpu.roll(x, k % LANES, 1)

    def ratios(x):
        return jnp.sqrt(x + EPS) / jnp.sqrt(shift(x, -count) + EPS)

    low = jnp.where(first, 0.0, shift(ratios(lower), 1 - count))
    high = jnp.where(last, 0.0, shift(ratios(upper), count + 1))
    own = ratios(mine)
    ratio_ref[...] = own[0, 0:count]
    copies = [pltpu.make_async_copy(ratio_ref, ratio_out, sem.at[2, 0])]
    copies[0].start()
    ratio = jnp.where(lane == 0, low, jnp.where(lane == count + 1, high, shift(own, 1)))

    def splat(t):
        return jnp.broadcast_to(jnp.sum(jnp.where(lane == t, ratio, 0.0), axis=1, keepdims=True), (TILE, LANES))

    def widen(x):
        return jnp.concatenate([x] * (cols // LANES), axis=1)

    scale = [widen(splat(t)) for t in range(count + 2)]
    column = jnp.sum(jnp.where(lane == sub + 1, ratio, 0.0), axis=1, keepdims=True)
    row = iota((TILE, cols), 0)
    near, far = near_corner_ref[...], far_corner_ref[...]
    corners = (
        (
            pick(first, strip_ref[count, 0:1, :], pick(halo.odd, near, far)),
            pick(last, strip_ref[count, 1:2, :], pick(halo.odd, far, near)),
        ),
        (lead_ref[count, 0:1, :], lead_ref[count, 1:2, :]),
    )

    def at(k):
        return pl.ds(TILE * k, TILE)

    def value(s, k):
        if s < 0:
            return halo.below(at(k)) if s == -1 else halo.below_2(at(k))
        if s >= count:
            return halo.above(at(k)) if s == count else halo.above_2(at(k))
        return f_ref[s, at(k), :]

    def residual_of(s):
        for k in range(tiles):
            if 0 <= s < count:
                drift = drift_ref[s, at(k), :]
                if k == 0:
                    drift += jnp.where(row == 0, tail_ref[1, s : s + 1, :], 0.0)
                if k == tiles - 1:
                    drift += jnp.where(row == TILE - 1, lead_ref[s, 0:1, :], 0.0)
            else:
                slot = 0 if s < 0 else 1
                c = outer[slot, at(k), :]
                above = outer[slot, TILE * k - 1 : TILE * k, :] if k > 0 else corners[0][slot]
                under = outer[slot, TILE * (k + 1) : TILE * (k + 1) + 1, :] if k < tiles - 1 else corners[1][slot]
                up = jnp.where(row == 0, above, pltpu.roll(c, 1, 0))
                dn = jnp.where(row == TILE - 1, under, pltpu.roll(c, TILE - 1, 0))
                drift = up + dn + sides(c) - 3.0 * c - c * c * c
            resid[s + 1, at(k + 1), :] = scale[s + 1] * (value(s + 1, k) - value(s - 1, k)) - drift

    def send(src, dst, slot):
        copy = pltpu.make_async_copy(src, dst, slot)
        copy.start()
        copies.append(copy)

    pieces = PIECES if count % PIECES == 0 else 1
    step = count // pieces
    for i in range(pieces):
        for s in range(i * step, (i + 1) * step):
            residual_of(s)
        span = pl.ds(i * step, step)
        send(resid.at[pl.ds(i * step + 1, step), pl.ds(TILE, rows)], res_out.at[span], sem.at[0, i])

    for k in range(tiles):
        outer[0, at(k), :] = halo.below(at(k))
        outer[1, at(k), :] = halo.above(at(k))
    residual_of(-1)
    residual_of(count)

    for s in range(count):
        rim[0, s : s + 1, :] = f_ref[s, 0:1, :]
        rim[1, s : s + 1, :] = f_ref[s, rows - 1 : rows, :]
        for r in range(2):
            head_ref[r, s : s + 1, :] = lead_ref[s, r : r + 1, :]
    for far, mid, near, (low, high), place in (
        (tail_ref[0], tail_ref[1], rim[0], corners[0], TILE - 1),
        (head_ref[1], head_ref[0], rim[1], corners[1], TILE + rows),
    ):
        ahead = jnp.where(row == count - 1, high, pltpu.roll(mid, count - 1, 0))
        behind = jnp.where(row == 0, low, pltpu.roll(mid, 1, 0))
        edge = column * (ahead - behind) - (far + near + sides(mid) - 3.0 * mid - mid * mid * mid)
        for s in range(count):
            resid[s + 1, place : place + 1, :] = edge[s : s + 1, :]

    def gradient_of(s):
        r = [resid[s + 1, at(k + 1), :] for k in range(tiles)]
        down = [resid[s + 1, TILE - 1 : TILE, :]] + [pltpu.roll(x, 1, 0) for x in r]
        up = [pltpu.roll(x, TILE - 1, 0) for x in r] + [resid[s + 1, TILE + rows : TILE + rows + 1, :]]
        for k in range(tiles):
            c = f_ref[s, at(k), :]
            around = jnp.where(row == 0, down[k], down[k + 1]) + jnp.where(row == TILE - 1, up[k + 1], up[k]) + sides(r[k])
            out = scale[s] * resid[s, at(k + 1), :] - scale[s + 2] * resid[s + 2, at(k + 1), :]
            grad[s, at(k), :] = out - (around - (3.0 + 3.0 * c * c) * r[k])

    for i in range(pieces):
        for s in range(i * step, (i + 1) * step):
            gradient_of(s)
        span = pl.ds(i * step, step)
        send(grad.at[span], grad_out.at[span], sem.at[1, i])
    for copy in copies:
        copy.wait()


def final(m, n, got, corners, f, drift, slabs, strips):
    count, rows, cols = f.shape
    big = jax.ShapeDtypeStruct(f.shape, F32)
    return pl.pallas_call(
        functools.partial(final_kernel, m, n),
        out_shape=(jax.ShapeDtypeStruct((count,), F32), big, big),
        in_specs=[VMEM] * 14,
        out_specs=(ANY, ANY, ANY),
        scratch_shapes=[
            pltpu.VMEM((count,), F32),
            pltpu.VMEM((count + 2, rows + 2 * TILE, cols), F32),
            pltpu.VMEM(f.shape, F32),
            pltpu.VMEM((2, rows, cols), F32),
            pltpu.VMEM((2, count, cols), F32),
            pltpu.VMEM((2, count, cols), F32),
            pltpu.SemaphoreType.DMA((3, PIECES)),
        ],
        compiler_params=PARAMS,
        name="final",
    )(got, *corners, f, drift, *slabs, *strips)


def swap(x, kind):
    size = lax.axis_size("path")
    return lax.ppermute(x, "path", [((i + kind) % size, ((i ^ 1) + kind) % size) for i in range(size)])


def ring(x, step):
    size = lax.axis_size("space")
    return lax.ppermute(x, "space", [(i, (i + step) % size) for i in range(size)])


def body(m, n, f, start, end):
    near, far_lo, far_hi, rest = slices(f)
    strip = ring(tail_rows(f, start, end), 1)
    far_lo, far_hi = swap(far_lo, 1), swap(far_hi, 1)
    near = swap(near, 0)
    rest = swap(rest, 1)
    part, drift, rim = interior(f)
    slabs = near, far_lo, far_hi, start, end
    send, near_corner, far_corner, tail, head = chunks(m, n, f, part, rim, *slabs, strip)
    got = lax.all_to_all(send, ("space", "path"), 0, 0, tiled=True)
    near_corner, far_corner = swap(near_corner, 0), swap(far_corner, 1)
    lead = ring(head, -1)
    return final(m, n, got, (near_corner, far_corner, rest), f, drift, slabs, (strip, tail, lead))


def solution(mesh):
    m, n = mesh.shape["path"], mesh.shape["space"]
    in_specs = (P("path", "space", None), P("space", None), P("space", None))
    out_specs = (P("path"), P("path", "space", None), P("path", "space", None))
    return jax.shard_map(
        functools.partial(body, m, n), mesh=mesh, in_specs=in_specs, out_specs=out_specs, check_vma=False
    )
```

```python
import functools

import jax
import jax.numpy as jnp
from jax import lax
from jax.experimental import pallas as pl
from jax.experimental.pallas import tpu as pltpu
from jax.sharding import PartitionSpec as P

F32 = jnp.float32
LANES = 128
TILE = 8
EPS = 1e-06
VMEM = pl.BlockSpec(memory_space=pltpu.VMEM)
ANY = pl.BlockSpec(memory_space=pl.ANY)
PIECES = 4
WIDTH = 256
PARAMS = pltpu.CompilerParams(vmem_limit_bytes=16 * 2**20)


def lanes_sum(x):
    parts = [x[:, i : i + LANES] for i in range(0, x.shape[1], LANES)]
    while len(parts) > 1:
        parts = [a + b for a, b in zip(parts[::2], parts[1::2])] + parts[len(parts) & ~1 :]
    return parts[0]


def sides(x):
    cols = x.shape[1]
    return pltpu.roll(x, 1, 1) + pltpu.roll(x, cols - 1, 1)


def iota(shape, dim):
    return lax.broadcasted_iota(jnp.int32, shape, dim)


def odd(axis):
    return lax.rem(lax.axis_index(axis), 2) == 1


def pick(flag, x, y):
    return jnp.where(flag, x, y)


def slices_kernel(f_ref, near_ref, far_ref):
    count = f_ref.shape[0]
    flag = odd("path")
    base = pick(flag, 0, count - 2)
    for s in range(2):
        near_ref[s] = f_ref[base + s]
    far_ref[...] = f_ref[pick(flag, count - 1, 0)]


def tail_kernel(f_ref, start_ref, end_ref, tail_ref):
    count, rows, _ = f_ref.shape
    tail_ref[count, 0:1, :] = start_ref[rows - 1 :, :]
    tail_ref[count, 1:2, :] = end_ref[rows - 1 :, :]
    for s in range(count):
        tail_ref[s] = f_ref[s, rows - 2 :, :]


def slices(f):
    count, rows, cols = f.shape
    return pl.pallas_call(
        slices_kernel,
        out_shape=(jax.ShapeDtypeStruct((2, rows, cols), F32), jax.ShapeDtypeStruct((rows, cols), F32)),
        in_specs=[VMEM],
        out_specs=[VMEM] * 2,
        compiler_params=PARAMS,
        name="slices",
    )(f)


def tail_rows(f, start, end):
    count, rows, cols = f.shape
    return pl.pallas_call(
        tail_kernel,
        out_shape=jax.ShapeDtypeStruct((count + 1, 2, cols), F32),
        in_specs=[VMEM] * 3,
        out_specs=VMEM,
        compiler_params=PARAMS,
        name="tail_rows",
    )(f, start, end)


class Halo:
    def __init__(self, m, near_ref, far_ref, start_ref, end_ref, rest_ref=None):
        self.odd = odd("path")
        self.first = lax.axis_index("path") == 0
        self.last = lax.axis_index("path") == m - 1
        self.near, self.far, self.rest = near_ref, far_ref, rest_ref
        self.start, self.end = start_ref, end_ref

    def below(self, at):
        return pick(self.first, self.start[at, :], pick(self.odd, self.near[1, at, :], self.far[at, :]))

    def above(self, at):
        return pick(self.last, self.end[at, :], pick(self.odd, self.far[at, :], self.near[0, at, :]))

    def below_2(self, at):
        return pick(self.odd, self.near[0, at, :], self.rest[at, :])

    def above_2(self, at):
        return pick(self.odd, self.rest[at, :], self.near[1, at, :])


def interior_kernel(f_ref, part_ref, drift_ref, rim_ref):
    count, rows, cols = f_ref.shape
    tiles = rows // TILE
    row = iota((TILE, cols), 0)
    part_ref[...] = jnp.zeros_like(part_ref)

    def drift_sum(s, _):
        total = jnp.zeros((TILE, LANES), F32)
        for k in range(tiles):
            c = f_ref[s, pl.ds(TILE * k, TILE), :]
            above = f_ref[s, pl.ds(TILE * k - 1, 1), :] if k > 0 else 0.0
            under = f_ref[s, pl.ds(TILE * (k + 1), 1), :] if k < tiles - 1 else 0.0
            up = jnp.where(row == 0, above, pltpu.roll(c, 1, 0))
            dn = jnp.where(row == TILE - 1, under, pltpu.roll(c, TILE - 1, 0))
            drift = up + dn + sides(c) - 3.0 * c - c * c * c
            drift_ref[s, pl.ds(TILE * k, TILE), :] = drift
            if k == 0:
                rim_ref[0, pl.ds(s, 1), :] = drift[0:1]
                rim_ref[1, pl.ds(s, 1), :] = c[0:1]
                drift = jnp.where(row == 0, 0.0, drift)
            if k == tiles - 1:
                drift = jnp.where(row == TILE - 1, 0.0, drift)
            total += lanes_sum(drift * drift)
        part_ref[pl.ds(s, 1), :] = jnp.sum(total, axis=0, keepdims=True)
        return 0

    def tangent_sum(s, _):
        total = jnp.zeros((TILE, LANES), F32)
        for k in range(tiles):
            tangent = f_ref[s + 1, pl.ds(TILE * k, TILE), :] - f_ref[s - 1, pl.ds(TILE * k, TILE), :]
            total += lanes_sum(tangent * tangent)
        part_ref[pl.ds(count + s, 1), :] = jnp.sum(total, axis=0, keepdims=True)
        return 0

    lax.fori_loop(0, count, drift_sum, 0)
    lax.fori_loop(1, count - 1, tangent_sum, 0)


def interior(f):
    count, rows, cols = f.shape
    return pl.pallas_call(
        interior_kernel,
        out_shape=(
            jax.ShapeDtypeStruct((2 * count, LANES), F32),
            jax.ShapeDtypeStruct(f.shape, F32),
            jax.ShapeDtypeStruct((2, count, cols), F32),
        ),
        in_specs=[VMEM],
        out_specs=[VMEM] * 3,
        cost_estimate=pl.CostEstimate(flops=20 * count * rows * cols, transcendentals=0, bytes_accessed=8 * count * rows * cols),
        compiler_params=PARAMS,
        name="interior",
    )(f)


def chunk_kernel(
    m, n, f_ref, part_ref, rim_ref, near_ref, far_ref, start_ref, end_ref, strip_ref,
    out_ref, near_corner_ref, rest_ref, tail_ref, head_ref, second_ref, lines, sem,
):
    halo = Halo(m, near_ref, far_ref, start_ref, end_ref)
    count, rows, cols = f_ref.shape
    tiles = rows // TILE

    for s in range(count):
        for r in range(2):
            tail_ref[r, s : s + 1, :] = strip_ref[s, r : r + 1, :]
    r0, r1 = tail_ref[0], tail_ref[1]

    drift_a = r0 + rim_ref[1] + sides(r1) - 3.0 * r1 - r1 * r1 * r1
    drift_b = rim_ref[0] + r1
    drift = part_ref[0:count, :] + lanes_sum(drift_a * drift_a) + lanes_sum(drift_b * drift_b)

    totals = [jnp.zeros((TILE, LANES), F32) for _ in range(2)]
    for k in range(tiles):
        at = pl.ds(TILE * k, TILE)
        tangents = (f_ref[1, at, :] - halo.below(at), halo.above(at) - f_ref[count - 2, at, :])
        totals = [a + lanes_sum(t * t) for a, t in zip(totals, tangents)]
    head_sum, tail_sum = [jnp.sum(a, axis=0, keepdims=True) for a in totals]
    sub = iota((TILE, LANES), 0)
    tangent = part_ref[count : 2 * count, :]
    tangent = jnp.where(sub == 0, head_sum, jnp.where(sub == count - 1, tail_sum, tangent))

    lane = iota((TILE, LANES), 1)
    spread = jnp.where(lane == sub, jnp.sum(drift, axis=1, keepdims=True), 0.0)
    spread += jnp.where(lane == sub + count, jnp.sum(tangent, axis=1, keepdims=True), 0.0)
    line = jnp.sum(spread, axis=0, keepdims=True)

    if WIDTH > LANES:
        line = jnp.concatenate([line, jnp.zeros((1, WIDTH - LANES), F32)], axis=1)
    for j in range(m * n):
        lines[j] = line
    copy = pltpu.make_async_copy(lines, out_ref, sem)
    copy.start()

    near_corner_ref[...] = tail_ref[1, pl.ds(pick(halo.odd, 0, count - 1), 1), :]
    rest_ref[0:rows, :] = f_ref[pick(halo.odd, count - 2, 1)]
    rest_ref[rows:, :] = jnp.broadcast_to(tail_ref[1, pl.ds(pick(halo.odd, count - 1, 0), 1), :], (TILE, cols))
    for s in range(count):
        head_ref[s // 2, s % 2 : s % 2 + 1, :] = f_ref[s, 0:1, :]
        second_ref[s // 2, s % 2 : s % 2 + 1, :] = f_ref[s, 1:2, :]
    head_ref[count // 2, 0:1, :] = halo.below(pl.ds(0, 1))
    head_ref[count // 2, 1:2, :] = halo.above(pl.ds(0, 1))
    copy.wait()


def chunks(m, n, f, part, rim, near, far, start, end, strip):
    count, rows, cols = f.shape
    return pl.pallas_call(
        functools.partial(chunk_kernel, m, n),
        out_shape=(
            jax.ShapeDtypeStruct((m * n, 1, WIDTH), F32),
            jax.ShapeDtypeStruct((1, cols), F32),
            jax.ShapeDtypeStruct((rows + TILE, cols), F32),
            jax.ShapeDtypeStruct((2, count, cols), F32),
            jax.ShapeDtypeStruct((count // 2 + 1, 2, cols), F32),
            jax.ShapeDtypeStruct((count // 2, 2, cols), F32),
        ),
        in_specs=[VMEM] * 8,
        out_specs=[ANY] + [VMEM] * 5,
        scratch_shapes=[pltpu.VMEM((m * n, 1, WIDTH), F32), pltpu.SemaphoreType.DMA],
        compiler_params=PARAMS,
        name="chunks",
    )(f, part, rim, near, far, start, end, strip)


def final_kernel(
    m, n, got_ref, near_corner_ref, rest_ref, f_ref, drift_ref, near_ref, far_ref, start_ref, end_ref,
    strip_ref, tail_ref, lead_ref, lead_b_ref, ratio_out, res_out, grad_out, ratio_ref, resid, grad, outer, rim, head_ref, sem,
):
    halo = Halo(m, near_ref, far_ref, start_ref, end_ref, rest_ref)
    count, rows, cols = f_ref.shape
    tiles = rows // TILE
    path = lax.axis_index("path")
    first, last = halo.first, halo.last
    path_lo = jnp.where(first, path, path - 1)
    path_hi = jnp.where(last, path, path + 1)

    def gathered(p):
        total = got_ref[p, :, 0:LANES]
        for i in range(1, n):
            total += got_ref[i * m + p, :, 0:LANES]
        return jnp.broadcast_to(total, (TILE, LANES))

    mine = gathered(path)
    lower = gathered(path_lo)
    upper = gathered(path_hi)
    lane = iota((TILE, LANES), 1)
    sub = iota((TILE, LANES), 0)

    def shift(x, k):
        return pltpu.roll(x, k % LANES, 1)

    def ratios(x):
        return jnp.sqrt(x + EPS) / jnp.sqrt(shift(x, -count) + EPS)

    low = jnp.where(first, 0.0, shift(ratios(lower), 1 - count))
    high = jnp.where(last, 0.0, shift(ratios(upper), count + 1))
    own = ratios(mine)
    ratio_ref[...] = own[0, 0:count]
    copies = [pltpu.make_async_copy(ratio_ref, ratio_out, sem.at[2, 0])]
    copies[0].start()
    ratio = jnp.where(lane == 0, low, jnp.where(lane == count + 1, high, shift(own, 1)))

    def splat(t):
        return jnp.broadcast_to(jnp.sum(jnp.where(lane == t, ratio, 0.0), axis=1, keepdims=True), (TILE, LANES))

    def widen(x):
        return jnp.concatenate([x] * (cols // LANES), axis=1)

    scale = [widen(splat(t)) for t in range(count + 2)]
    column = jnp.sum(jnp.where(lane == sub + 1, ratio, 0.0), axis=1, keepdims=True)
    row = iota((TILE, cols), 0)
    near, far = near_corner_ref[...], rest_ref[rows : rows + 1, :]
    corners = (
        (
            pick(first, strip_ref[count, 0:1, :], pick(halo.odd, near, far)),
            pick(last, strip_ref[count, 1:2, :], pick(halo.odd, far, near)),
        ),
        (lead_ref[count // 2, 0:1, :], lead_ref[count // 2, 1:2, :]),
    )

    def at(k):
        return pl.ds(TILE * k, TILE)

    def value(s, k):
        if s < 0:
            return halo.below(at(k)) if s == -1 else halo.below_2(at(k))
        if s >= count:
            return halo.above(at(k)) if s == count else halo.above_2(at(k))
        return f_ref[s, at(k), :]

    def residual_of(s):
        for k in range(tiles):
            if 0 <= s < count:
                drift = drift_ref[s, at(k), :]
                if k == 0:
                    drift += jnp.where(row == 0, tail_ref[1, s : s + 1, :], 0.0)
                if k == tiles - 1:
                    drift += jnp.where(row == TILE - 1, lead_ref[s // 2, s % 2 : s % 2 + 1, :], 0.0)
            else:
                slot = 0 if s < 0 else 1
                c = outer[slot, at(k), :]
                above = outer[slot, TILE * k - 1 : TILE * k, :] if k > 0 else corners[0][slot]
                under = outer[slot, TILE * (k + 1) : TILE * (k + 1) + 1, :] if k < tiles - 1 else corners[1][slot]
                up = jnp.where(row == 0, above, pltpu.roll(c, 1, 0))
                dn = jnp.where(row == TILE - 1, under, pltpu.roll(c, TILE - 1, 0))
                drift = up + dn + sides(c) - 3.0 * c - c * c * c
            resid[s + 1, at(k + 1), :] = scale[s + 1] * (value(s + 1, k) - value(s - 1, k)) - drift

    def send(src, dst, slot):
        copy = pltpu.make_async_copy(src, dst, slot)
        copy.start()
        copies.append(copy)

    pieces = PIECES if count % PIECES == 0 else 1
    step = count // pieces
    for i in range(pieces):
        for s in range(i * step, (i + 1) * step):
            residual_of(s)
        span = pl.ds(i * step, step)
        send(resid.at[pl.ds(i * step + 1, step), pl.ds(TILE, rows)], res_out.at[span], sem.at[0, i])

    for k in range(tiles):
        outer[0, at(k), :] = halo.below(at(k))
        outer[1, at(k), :] = halo.above(at(k))
    residual_of(-1)
    residual_of(count)

    for s in range(count):
        rim[0, s : s + 1, :] = f_ref[s, 0:1, :]
        rim[1, s : s + 1, :] = f_ref[s, rows - 1 : rows, :]
        for r, ref in enumerate((lead_ref, lead_b_ref)):
            head_ref[r, s : s + 1, :] = ref[s // 2, s % 2 : s % 2 + 1, :]
    for far, mid, near, (low, high), place in (
        (tail_ref[0], tail_ref[1], rim[0], corners[0], TILE - 1),
        (head_ref[1], head_ref[0], rim[1], corners[1], TILE + rows),
    ):
        ahead = jnp.where(row == count - 1, high, pltpu.roll(mid, count - 1, 0))
        behind = jnp.where(row == 0, low, pltpu.roll(mid, 1, 0))
        edge = column * (ahead - behind) - (far + near + sides(mid) - 3.0 * mid - mid * mid * mid)
        for s in range(count):
            resid[s + 1, place : place + 1, :] = edge[s : s + 1, :]

    def gradient_of(s):
        r = [resid[s + 1, at(k + 1), :] for k in range(tiles)]
        down = [resid[s + 1, TILE - 1 : TILE, :]] + [pltpu.roll(x, 1, 0) for x in r]
        up = [pltpu.roll(x, TILE - 1, 0) for x in r] + [resid[s + 1, TILE + rows : TILE + rows + 1, :]]
        for k in range(tiles):
            c = f_ref[s, at(k), :]
            around = jnp.where(row == 0, down[k], down[k + 1]) + jnp.where(row == TILE - 1, up[k + 1], up[k]) + sides(r[k])
            out = scale[s] * resid[s, at(k + 1), :] - scale[s + 2] * resid[s + 2, at(k + 1), :]
            grad[s, at(k), :] = out - (around - (3.0 + 3.0 * c * c) * r[k])

    for i in range(pieces):
        for s in range(i * step, (i + 1) * step):
            gradient_of(s)
        span = pl.ds(i * step, step)
        send(grad.at[span], grad_out.at[span], sem.at[1, i])
    for copy in copies:
        copy.wait()


def final(m, n, got, corners, f, drift, slabs, strips):
    count, rows, cols = f.shape
    big = jax.ShapeDtypeStruct(f.shape, F32)
    return pl.pallas_call(
        functools.partial(final_kernel, m, n),
        out_shape=(jax.ShapeDtypeStruct((count,), F32), big, big),
        in_specs=[VMEM] * 13,
        out_specs=(ANY, ANY, ANY),
        scratch_shapes=[
            pltpu.VMEM((count,), F32),
            pltpu.VMEM((count + 2, rows + 2 * TILE, cols), F32),
            pltpu.VMEM(f.shape, F32),
            pltpu.VMEM((2, rows, cols), F32),
            pltpu.VMEM((2, count, cols), F32),
            pltpu.VMEM((2, count, cols), F32),
            pltpu.SemaphoreType.DMA((3, PIECES)),
        ],
        compiler_params=PARAMS,
        name="final",
    )(got, *corners, f, drift, *slabs, *strips)


def swap(x, kind):
    size = lax.axis_size("path")
    return lax.ppermute(x, "path", [((i + kind) % size, ((i ^ 1) + kind) % size) for i in range(size)])


def ring(x, step):
    size = lax.axis_size("space")
    return lax.ppermute(x, "space", [(i, (i + step) % size) for i in range(size)])


def body(m, n, f, start, end):
    near, far = slices(f)
    strip = ring(tail_rows(f, start, end), 1)
    far = swap(far, 1)
    near = swap(near, 0)
    part, drift, rim = interior(f)
    slabs = near, far, start, end
    send, near_corner, rest, tail, head, second = chunks(m, n, f, part, rim, *slabs, strip)
    got = lax.all_to_all(send, ("space", "path"), 0, 0, tiled=True)
    lead, lead_b = ring(head, -1), ring(second, -1)
    late = swap(near_corner, 0), swap(rest, 1)
    return final(m, n, got, late, f, drift, slabs, (strip, tail, lead, lead_b))


def solution(mesh):
    m, n = mesh.shape["path"], mesh.shape["space"]
    in_specs = (P("path", "space", None), P("space", None), P("space", None))
    out_specs = (P("path"), P("path", "space", None), P("path", "space", None))
    return jax.shard_map(
        functools.partial(body, m, n), mesh=mesh, in_specs=in_specs, out_specs=out_specs, check_vma=False
    )
```

```python
import functools

import jax
import jax.numpy as jnp
from jax import lax
from jax.experimental import pallas as pl
from jax.experimental.pallas import tpu as pltpu
from jax.sharding import PartitionSpec as P

F32 = jnp.float32
LANES = 128
TILE = 8
EPS = 1e-06
VMEM = pl.BlockSpec(memory_space=pltpu.VMEM)
ANY = pl.BlockSpec(memory_space=pl.ANY)
PIECES = 4
WIDTH = 128
RATIO_FLOPS = 10**9
PARAMS = pltpu.CompilerParams(vmem_limit_bytes=16 * 2**20)


def lanes_sum(x):
    parts = [x[:, i : i + LANES] for i in range(0, x.shape[1], LANES)]
    while len(parts) > 1:
        parts = [a + b for a, b in zip(parts[::2], parts[1::2])] + parts[len(parts) & ~1 :]
    return parts[0]


def sides(x):
    cols = x.shape[1]
    return pltpu.roll(x, 1, 1) + pltpu.roll(x, cols - 1, 1)


def iota(shape, dim):
    return lax.broadcasted_iota(jnp.int32, shape, dim)


def odd(axis):
    return lax.rem(lax.axis_index(axis), 2) == 1


def pick(flag, x, y):
    return jnp.where(flag, x, y)


def slices_kernel(f_ref, near_ref, far_ref):
    count = f_ref.shape[0]
    flag = odd("path")
    base = pick(flag, 0, count - 2)
    for s in range(2):
        near_ref[s] = f_ref[base + s]
    far_ref[...] = f_ref[pick(flag, count - 1, 0)]


def tail_kernel(f_ref, start_ref, end_ref, tail_ref):
    count, rows, _ = f_ref.shape
    tail_ref[count, 0:1, :] = start_ref[rows - 1 :, :]
    tail_ref[count, 1:2, :] = end_ref[rows - 1 :, :]
    for s in range(count):
        tail_ref[s] = f_ref[s, rows - 2 :, :]


def slices(f):
    count, rows, cols = f.shape
    return pl.pallas_call(
        slices_kernel,
        out_shape=(jax.ShapeDtypeStruct((2, rows, cols), F32), jax.ShapeDtypeStruct((rows, cols), F32)),
        in_specs=[VMEM],
        out_specs=[VMEM] * 2,
        compiler_params=PARAMS,
        name="slices",
    )(f)


def tail_rows(f, start, end):
    count, rows, cols = f.shape
    return pl.pallas_call(
        tail_kernel,
        out_shape=jax.ShapeDtypeStruct((count + 1, 2, cols), F32),
        in_specs=[VMEM] * 3,
        out_specs=VMEM,
        compiler_params=PARAMS,
        name="tail_rows",
    )(f, start, end)


class Halo:
    def __init__(self, m, near_ref, far_ref, start_ref, end_ref, rest_ref=None):
        self.odd = odd("path")
        self.first = lax.axis_index("path") == 0
        self.last = lax.axis_index("path") == m - 1
        self.near, self.far, self.rest = near_ref, far_ref, rest_ref
        self.start, self.end = start_ref, end_ref

    def below(self, at):
        return pick(self.first, self.start[at, :], pick(self.odd, self.near[1, at, :], self.far[at, :]))

    def above(self, at):
        return pick(self.last, self.end[at, :], pick(self.odd, self.far[at, :], self.near[0, at, :]))

    def below_2(self, at):
        return pick(self.odd, self.near[0, at, :], self.rest[at, :])

    def above_2(self, at):
        return pick(self.odd, self.rest[at, :], self.near[1, at, :])


def interior_kernel(f_ref, part_ref, drift_ref, rim_ref):
    count, rows, cols = f_ref.shape
    tiles = rows // TILE
    row = iota((TILE, cols), 0)
    part_ref[...] = jnp.zeros_like(part_ref)

    def drift_sum(s, _):
        total = jnp.zeros((TILE, LANES), F32)
        for k in range(tiles):
            c = f_ref[s, pl.ds(TILE * k, TILE), :]
            above = f_ref[s, pl.ds(TILE * k - 1, 1), :] if k > 0 else 0.0
            under = f_ref[s, pl.ds(TILE * (k + 1), 1), :] if k < tiles - 1 else 0.0
            up = jnp.where(row == 0, above, pltpu.roll(c, 1, 0))
            dn = jnp.where(row == TILE - 1, under, pltpu.roll(c, TILE - 1, 0))
            drift = up + dn + sides(c) - 3.0 * c - c * c * c
            drift_ref[s, pl.ds(TILE * k, TILE), :] = drift
            if k == 0:
                rim_ref[0, pl.ds(s, 1), :] = drift[0:1]
                rim_ref[1, pl.ds(s, 1), :] = c[0:1]
                drift = jnp.where(row == 0, 0.0, drift)
            if k == tiles - 1:
                drift = jnp.where(row == TILE - 1, 0.0, drift)
            total += lanes_sum(drift * drift)
        part_ref[pl.ds(s, 1), :] = jnp.sum(total, axis=0, keepdims=True)
        return 0

    def tangent_sum(s, _):
        total = jnp.zeros((TILE, LANES), F32)
        for k in range(tiles):
            tangent = f_ref[s + 1, pl.ds(TILE * k, TILE), :] - f_ref[s - 1, pl.ds(TILE * k, TILE), :]
            total += lanes_sum(tangent * tangent)
        part_ref[pl.ds(count + s, 1), :] = jnp.sum(total, axis=0, keepdims=True)
        return 0

    lax.fori_loop(0, count, drift_sum, 0)
    lax.fori_loop(1, count - 1, tangent_sum, 0)


def interior(f):
    count, rows, cols = f.shape
    return pl.pallas_call(
        interior_kernel,
        out_shape=(
            jax.ShapeDtypeStruct((2 * count, LANES), F32),
            jax.ShapeDtypeStruct(f.shape, F32),
            jax.ShapeDtypeStruct((2, count, cols), F32),
        ),
        in_specs=[VMEM],
        out_specs=[VMEM] * 3,
        cost_estimate=pl.CostEstimate(flops=20 * count * rows * cols, transcendentals=0, bytes_accessed=8 * count * rows * cols),
        compiler_params=PARAMS,
        name="interior",
    )(f)


def chunk_kernel(
    m, n, f_ref, part_ref, rim_ref, near_ref, far_ref, start_ref, end_ref, strip_ref,
    out_ref, near_corner_ref, rest_ref, tail_ref, head_ref, lines, sem,
):
    halo = Halo(m, near_ref, far_ref, start_ref, end_ref)
    count, rows, cols = f_ref.shape
    tiles = rows // TILE

    for s in range(count):
        for r in range(2):
            tail_ref[r, s : s + 1, :] = strip_ref[s, r : r + 1, :]
    r0, r1 = tail_ref[0], tail_ref[1]

    drift_a = r0 + rim_ref[1] + sides(r1) - 3.0 * r1 - r1 * r1 * r1
    drift_b = rim_ref[0] + r1
    drift = part_ref[0:count, :] + lanes_sum(drift_a * drift_a) + lanes_sum(drift_b * drift_b)

    totals = [jnp.zeros((TILE, LANES), F32) for _ in range(2)]
    for k in range(tiles):
        at = pl.ds(TILE * k, TILE)
        tangents = (f_ref[1, at, :] - halo.below(at), halo.above(at) - f_ref[count - 2, at, :])
        totals = [a + lanes_sum(t * t) for a, t in zip(totals, tangents)]
    head_sum, tail_sum = [jnp.sum(a, axis=0, keepdims=True) for a in totals]
    sub = iota((TILE, LANES), 0)
    tangent = part_ref[count : 2 * count, :]
    tangent = jnp.where(sub == 0, head_sum, jnp.where(sub == count - 1, tail_sum, tangent))

    lane = iota((TILE, LANES), 1)
    spread = jnp.where(lane == sub, jnp.sum(drift, axis=1, keepdims=True), 0.0)
    spread += jnp.where(lane == sub + count, jnp.sum(tangent, axis=1, keepdims=True), 0.0)
    line = jnp.sum(spread, axis=0, keepdims=True)

    if WIDTH > LANES:
        line = jnp.concatenate([line, jnp.zeros((1, WIDTH - LANES), F32)], axis=1)
    for j in range(m * n):
        lines[j] = line
    copy = pltpu.make_async_copy(lines, out_ref, sem)
    copy.start()

    near_corner_ref[...] = tail_ref[1, pl.ds(pick(halo.odd, 0, count - 1), 1), :]
    rest_ref[0:rows, :] = f_ref[pick(halo.odd, count - 2, 1)]
    rest_ref[rows:, :] = jnp.broadcast_to(tail_ref[1, pl.ds(pick(halo.odd, count - 1, 0), 1), :], (TILE, cols))
    for s in range(count):
        head_ref[s] = f_ref[s, 0:2, :]
    head_ref[count, 0:1, :] = halo.below(pl.ds(0, 1))
    head_ref[count, 1:2, :] = halo.above(pl.ds(0, 1))
    copy.wait()


def chunks(m, n, f, part, rim, near, far, start, end, strip):
    count, rows, cols = f.shape
    return pl.pallas_call(
        functools.partial(chunk_kernel, m, n),
        out_shape=(
            jax.ShapeDtypeStruct((m * n, 1, WIDTH), F32),
            jax.ShapeDtypeStruct((1, cols), F32),
            jax.ShapeDtypeStruct((rows + TILE, cols), F32),
            jax.ShapeDtypeStruct((2, count, cols), F32),
            jax.ShapeDtypeStruct((count + 1, 2, cols), F32),
        ),
        in_specs=[VMEM] * 8,
        out_specs=[ANY] + [VMEM] * 4,
        scratch_shapes=[pltpu.VMEM((m * n, 1, WIDTH), F32), pltpu.SemaphoreType.DMA],
        compiler_params=PARAMS,
        name="chunks",
    )(f, part, rim, near, far, start, end, strip)


def ratio_kernel(m, n, got_ref, scale_ref):
    count = scale_ref.shape[0] - 4
    path = lax.axis_index("path")
    first, last = path == 0, path == m - 1
    path_lo = jnp.where(first, path, path - 1)
    path_hi = jnp.where(last, path, path + 1)

    def gathered(p):
        total = got_ref[p, :, 0:LANES]
        for i in range(1, n):
            total += got_ref[i * m + p, :, 0:LANES]
        return jnp.broadcast_to(total, (TILE, LANES))

    mine = gathered(path)
    lower = gathered(path_lo)
    upper = gathered(path_hi)
    lane = iota((TILE, LANES), 1)
    sub = iota((TILE, LANES), 0)

    def shift(x, k):
        return pltpu.roll(x, k % LANES, 1)

    def ratios(x):
        return jnp.sqrt(x + EPS) / jnp.sqrt(shift(x, -count) + EPS)

    low = jnp.where(first, 0.0, shift(ratios(lower), 1 - count))
    high = jnp.where(last, 0.0, shift(ratios(upper), count + 1))
    own = ratios(mine)
    ratio = jnp.where(lane == 0, low, jnp.where(lane == count + 1, high, shift(own, 1)))

    def splat(t):
        return jnp.broadcast_to(jnp.sum(jnp.where(lane == t, ratio, 0.0), axis=1, keepdims=True), (TILE, LANES))

    for t in range(count + 2):
        scale_ref[t] = splat(t)
    column = jnp.sum(jnp.where(lane == sub + 1, ratio, 0.0), axis=1, keepdims=True)
    scale_ref[count + 2] = jnp.broadcast_to(column, (TILE, LANES))
    scale_ref[count + 3] = own


def speed_ratios(m, n, count, got):
    return pl.pallas_call(
        functools.partial(ratio_kernel, m, n),
        out_shape=jax.ShapeDtypeStruct((count + 4, TILE, LANES), F32),
        in_specs=[VMEM],
        out_specs=VMEM,
        cost_estimate=pl.CostEstimate(flops=RATIO_FLOPS, transcendentals=0, bytes_accessed=0),
        compiler_params=PARAMS,
        name="speed_ratios",
    )(got)


def final_kernel(
    m, scale_ref, near_corner_ref, rest_ref, f_ref, drift_ref, near_ref, far_ref, start_ref, end_ref,
    strip_ref, tail_ref, lead_ref, ratio_out, res_out, grad_out, ratio_ref, resid, grad, outer, rim, head_ref, sem,
):
    halo = Halo(m, near_ref, far_ref, start_ref, end_ref, rest_ref)
    count, rows, cols = f_ref.shape
    tiles = rows // TILE
    first, last = halo.first, halo.last
    ratio_ref[...] = scale_ref[count + 3][0, 0:count]
    copies = [pltpu.make_async_copy(ratio_ref, ratio_out, sem.at[2, 0])]
    copies[0].start()

    def widen(x):
        return jnp.concatenate([x] * (cols // LANES), axis=1)

    scale = [widen(scale_ref[t]) for t in range(count + 2)]
    column = widen(scale_ref[count + 2])
    row = iota((TILE, cols), 0)
    near, far = near_corner_ref[...], rest_ref[rows : rows + 1, :]
    corners = (
        (
            pick(first, strip_ref[count, 0:1, :], pick(halo.odd, near, far)),
            pick(last, strip_ref[count, 1:2, :], pick(halo.odd, far, near)),
        ),
        (lead_ref[count, 0:1, :], lead_ref[count, 1:2, :]),
    )

    def at(k):
        return pl.ds(TILE * k, TILE)

    def value(s, k):
        if s < 0:
            return halo.below(at(k)) if s == -1 else halo.below_2(at(k))
        if s >= count:
            return halo.above(at(k)) if s == count else halo.above_2(at(k))
        return f_ref[s, at(k), :]

    def residual_of(s):
        for k in range(tiles):
            if 0 <= s < count:
                drift = drift_ref[s, at(k), :]
                if k == 0:
                    drift += jnp.where(row == 0, tail_ref[1, s : s + 1, :], 0.0)
                if k == tiles - 1:
                    drift += jnp.where(row == TILE - 1, lead_ref[s, 0:1, :], 0.0)
            else:
                slot = 0 if s < 0 else 1
                c = outer[slot, at(k), :]
                above = outer[slot, TILE * k - 1 : TILE * k, :] if k > 0 else corners[0][slot]
                under = outer[slot, TILE * (k + 1) : TILE * (k + 1) + 1, :] if k < tiles - 1 else corners[1][slot]
                up = jnp.where(row == 0, above, pltpu.roll(c, 1, 0))
                dn = jnp.where(row == TILE - 1, under, pltpu.roll(c, TILE - 1, 0))
                drift = up + dn + sides(c) - 3.0 * c - c * c * c
            resid[s + 1, at(k + 1), :] = scale[s + 1] * (value(s + 1, k) - value(s - 1, k)) - drift

    def send(src, dst, slot):
        copy = pltpu.make_async_copy(src, dst, slot)
        copy.start()
        copies.append(copy)

    pieces = PIECES if count % PIECES == 0 else 1
    step = count // pieces
    for i in range(pieces):
        for s in range(i * step, (i + 1) * step):
            residual_of(s)
        span = pl.ds(i * step, step)
        send(resid.at[pl.ds(i * step + 1, step), pl.ds(TILE, rows)], res_out.at[span], sem.at[0, i])

    for k in range(tiles):
        outer[0, at(k), :] = halo.below(at(k))
        outer[1, at(k), :] = halo.above(at(k))
    residual_of(-1)
    residual_of(count)

    for s in range(count):
        rim[0, s : s + 1, :] = f_ref[s, 0:1, :]
        rim[1, s : s + 1, :] = f_ref[s, rows - 1 : rows, :]
        for r in range(2):
            head_ref[r, s : s + 1, :] = lead_ref[s, r : r + 1, :]
    for far, mid, near, (low, high), place in (
        (tail_ref[0], tail_ref[1], rim[0], corners[0], TILE - 1),
        (head_ref[1], head_ref[0], rim[1], corners[1], TILE + rows),
    ):
        ahead = jnp.where(row == count - 1, high, pltpu.roll(mid, count - 1, 0))
        behind = jnp.where(row == 0, low, pltpu.roll(mid, 1, 0))
        edge = column * (ahead - behind) - (far + near + sides(mid) - 3.0 * mid - mid * mid * mid)
        for s in range(count):
            resid[s + 1, place : place + 1, :] = edge[s : s + 1, :]

    def gradient_of(s):
        r = [resid[s + 1, at(k + 1), :] for k in range(tiles)]
        down = [resid[s + 1, TILE - 1 : TILE, :]] + [pltpu.roll(x, 1, 0) for x in r]
        up = [pltpu.roll(x, TILE - 1, 0) for x in r] + [resid[s + 1, TILE + rows : TILE + rows + 1, :]]
        for k in range(tiles):
            c = f_ref[s, at(k), :]
            around = jnp.where(row == 0, down[k], down[k + 1]) + jnp.where(row == TILE - 1, up[k + 1], up[k]) + sides(r[k])
            out = scale[s] * resid[s, at(k + 1), :] - scale[s + 2] * resid[s + 2, at(k + 1), :]
            grad[s, at(k), :] = out - (around - (3.0 + 3.0 * c * c) * r[k])

    for i in range(pieces):
        for s in range(i * step, (i + 1) * step):
            gradient_of(s)
        span = pl.ds(i * step, step)
        send(grad.at[span], grad_out.at[span], sem.at[1, i])
    for copy in copies:
        copy.wait()


def final(m, scale, corners, f, drift, slabs, strips):
    count, rows, cols = f.shape
    big = jax.ShapeDtypeStruct(f.shape, F32)
    return pl.pallas_call(
        functools.partial(final_kernel, m),
        out_shape=(jax.ShapeDtypeStruct((count,), F32), big, big),
        in_specs=[VMEM] * 12,
        out_specs=(ANY, ANY, ANY),
        scratch_shapes=[
            pltpu.VMEM((count,), F32),
            pltpu.VMEM((count + 2, rows + 2 * TILE, cols), F32),
            pltpu.VMEM(f.shape, F32),
            pltpu.VMEM((2, rows, cols), F32),
            pltpu.VMEM((2, count, cols), F32),
            pltpu.VMEM((2, count, cols), F32),
            pltpu.SemaphoreType.DMA((3, PIECES)),
        ],
        compiler_params=PARAMS,
        name="final",
    )(scale, *corners, f, drift, *slabs, *strips)


def swap(x, kind):
    size = lax.axis_size("path")
    return lax.ppermute(x, "path", [((i + kind) % size, ((i ^ 1) + kind) % size) for i in range(size)])


def ring(x, step):
    size = lax.axis_size("space")
    return lax.ppermute(x, "space", [(i, (i + step) % size) for i in range(size)])


def body(m, n, f, start, end):
    near, far = slices(f)
    strip = ring(tail_rows(f, start, end), 1)
    far = swap(far, 1)
    near = swap(near, 0)
    part, drift, rim = interior(f)
    slabs = near, far, start, end
    send, near_corner, rest, tail, head = chunks(m, n, f, part, rim, *slabs, strip)
    got = lax.all_to_all(send, ("space", "path"), 0, 0, tiled=True)
    lead = ring(head, -1)
    late = swap(near_corner, 0), swap(rest, 1)
    scale = speed_ratios(m, n, f.shape[0], got)
    return final(m, scale, late, f, drift, slabs, (strip, tail, lead))


def solution(mesh):
    m, n = mesh.shape["path"], mesh.shape["space"]
    in_specs = (P("path", "space", None), P("space", None), P("space", None))
    out_specs = (P("path"), P("path", "space", None), P("path", "space", None))
    return jax.shard_map(
        functools.partial(body, m, n), mesh=mesh, in_specs=in_specs, out_specs=out_specs, check_vma=False
    )
```

```python
import functools

import jax
import jax.numpy as jnp
from jax import lax
from jax.experimental import pallas as pl
from jax.experimental.pallas import tpu as pltpu
from jax.sharding import PartitionSpec as P

F32 = jnp.float32
LANES = 128
TILE = 8
EPS = 1e-06
VMEM = pl.BlockSpec(memory_space=pltpu.VMEM)
ANY = pl.BlockSpec(memory_space=pl.ANY)
PIECES = 4
WIDTH = 128
RATIO_FLOPS = 10**9
PARAMS = pltpu.CompilerParams(vmem_limit_bytes=16 * 2**20)


def lanes_sum(x):
    parts = [x[:, i : i + LANES] for i in range(0, x.shape[1], LANES)]
    while len(parts) > 1:
        parts = [a + b for a, b in zip(parts[::2], parts[1::2])] + parts[len(parts) & ~1 :]
    return parts[0]


def sides(x):
    cols = x.shape[1]
    return pltpu.roll(x, 1, 1) + pltpu.roll(x, cols - 1, 1)


def iota(shape, dim):
    return lax.broadcasted_iota(jnp.int32, shape, dim)


def odd(axis):
    return lax.rem(lax.axis_index(axis), 2) == 1


def pick(flag, x, y):
    return jnp.where(flag, x, y)


def slices_kernel(f_ref, near_ref, far_ref):
    count = f_ref.shape[0]
    flag = odd("path")
    base = pick(flag, 0, count - 2)
    for s in range(2):
        near_ref[s] = f_ref[base + s]
    far_ref[...] = f_ref[pick(flag, count - 1, 0)]


def tail_kernel(f_ref, start_ref, end_ref, tail_ref):
    count, rows, _ = f_ref.shape
    tail_ref[count, 0:1, :] = start_ref[rows - 1 :, :]
    tail_ref[count, 1:2, :] = end_ref[rows - 1 :, :]
    for s in range(count):
        tail_ref[s] = f_ref[s, rows - 2 :, :]


def slices(f):
    count, rows, cols = f.shape
    return pl.pallas_call(
        slices_kernel,
        out_shape=(jax.ShapeDtypeStruct((2, rows, cols), F32), jax.ShapeDtypeStruct((rows, cols), F32)),
        in_specs=[VMEM],
        out_specs=[VMEM] * 2,
        compiler_params=PARAMS,
        name="slices",
    )(f)


def tail_rows(f, start, end):
    count, rows, cols = f.shape
    return pl.pallas_call(
        tail_kernel,
        out_shape=jax.ShapeDtypeStruct((count + 1, 2, cols), F32),
        in_specs=[VMEM] * 3,
        out_specs=VMEM,
        compiler_params=PARAMS,
        name="tail_rows",
    )(f, start, end)


class Halo:
    def __init__(self, m, near_ref, far_ref, start_ref, end_ref, rest_ref=None):
        self.odd = odd("path")
        self.first = lax.axis_index("path") == 0
        self.last = lax.axis_index("path") == m - 1
        self.near, self.far, self.rest = near_ref, far_ref, rest_ref
        self.start, self.end = start_ref, end_ref

    def below(self, at):
        return pick(self.first, self.start[at, :], pick(self.odd, self.near[1, at, :], self.far[at, :]))

    def above(self, at):
        return pick(self.last, self.end[at, :], pick(self.odd, self.far[at, :], self.near[0, at, :]))

    def below_2(self, at):
        return pick(self.odd, self.near[0, at, :], self.rest[at, :])

    def above_2(self, at):
        return pick(self.odd, self.rest[at, :], self.near[1, at, :])


def interior_kernel(f_ref, part_ref, drift_ref, rim_ref):
    count, rows, cols = f_ref.shape
    tiles = rows // TILE
    row = iota((TILE, cols), 0)
    part_ref[...] = jnp.zeros_like(part_ref)

    def drift_sum(s, _):
        total = jnp.zeros((TILE, LANES), F32)
        for k in range(tiles):
            c = f_ref[s, pl.ds(TILE * k, TILE), :]
            above = f_ref[s, pl.ds(TILE * k - 1, 1), :] if k > 0 else 0.0
            under = f_ref[s, pl.ds(TILE * (k + 1), 1), :] if k < tiles - 1 else 0.0
            up = jnp.where(row == 0, above, pltpu.roll(c, 1, 0))
            dn = jnp.where(row == TILE - 1, under, pltpu.roll(c, TILE - 1, 0))
            drift = up + dn + sides(c) - 3.0 * c - c * c * c
            drift_ref[s, pl.ds(TILE * k, TILE), :] = drift
            if k == 0:
                rim_ref[0, pl.ds(s, 1), :] = drift[0:1]
                rim_ref[1, pl.ds(s, 1), :] = c[0:1]
                drift = jnp.where(row == 0, 0.0, drift)
            if k == tiles - 1:
                drift = jnp.where(row == TILE - 1, 0.0, drift)
            total += lanes_sum(drift * drift)
        part_ref[pl.ds(s, 1), :] = jnp.sum(total, axis=0, keepdims=True)
        return 0

    def tangent_sum(s, _):
        total = jnp.zeros((TILE, LANES), F32)
        for k in range(tiles):
            tangent = f_ref[s + 1, pl.ds(TILE * k, TILE), :] - f_ref[s - 1, pl.ds(TILE * k, TILE), :]
            total += lanes_sum(tangent * tangent)
        part_ref[pl.ds(count + s, 1), :] = jnp.sum(total, axis=0, keepdims=True)
        return 0

    lax.fori_loop(0, count, drift_sum, 0)
    lax.fori_loop(1, count - 1, tangent_sum, 0)


def interior(f):
    count, rows, cols = f.shape
    return pl.pallas_call(
        interior_kernel,
        out_shape=(
            jax.ShapeDtypeStruct((2 * count, LANES), F32),
            jax.ShapeDtypeStruct(f.shape, F32),
            jax.ShapeDtypeStruct((2, count, cols), F32),
        ),
        in_specs=[VMEM],
        out_specs=[VMEM] * 3,
        cost_estimate=pl.CostEstimate(flops=20 * count * rows * cols, transcendentals=0, bytes_accessed=8 * count * rows * cols),
        compiler_params=PARAMS,
        name="interior",
    )(f)


def ends_kernel(m, f_ref, near_ref, far_ref, start_ref, end_ref, ends_ref):
    halo = Halo(m, near_ref, far_ref, start_ref, end_ref)
    count, rows, _ = f_ref.shape
    totals = [jnp.zeros((TILE, LANES), F32) for _ in range(2)]
    for k in range(rows // TILE):
        at = pl.ds(TILE * k, TILE)
        tangents = (f_ref[1, at, :] - halo.below(at), halo.above(at) - f_ref[count - 2, at, :])
        totals = [a + lanes_sum(t * t) for a, t in zip(totals, tangents)]
    for i, total in enumerate(totals):
        ends_ref[i : i + 1, :] = jnp.sum(total, axis=0, keepdims=True)


def ends(m, f, near, far, start, end):
    return pl.pallas_call(
        functools.partial(ends_kernel, m),
        out_shape=jax.ShapeDtypeStruct((2, LANES), F32),
        in_specs=[VMEM] * 5,
        out_specs=VMEM,
        compiler_params=PARAMS,
        name="ends",
    )(f, near, far, start, end)


def chunk_kernel(
    m, n, f_ref, part_ref, ends_ref, rim_ref, near_ref, far_ref, start_ref, end_ref, strip_ref,
    out_ref, near_corner_ref, rest_ref, tail_ref, head_ref, lines, sem,
):
    halo = Halo(m, near_ref, far_ref, start_ref, end_ref)
    count, rows, cols = f_ref.shape
    tiles = rows // TILE

    for s in range(count):
        for r in range(2):
            tail_ref[r, s : s + 1, :] = strip_ref[s, r : r + 1, :]
    r0, r1 = tail_ref[0], tail_ref[1]

    drift_a = r0 + rim_ref[1] + sides(r1) - 3.0 * r1 - r1 * r1 * r1
    drift_b = rim_ref[0] + r1
    drift = part_ref[0:count, :] + lanes_sum(drift_a * drift_a) + lanes_sum(drift_b * drift_b)

    sub = iota((TILE, LANES), 0)
    tangent = part_ref[count : 2 * count, :]
    tangent = jnp.where(sub == 0, ends_ref[0:1, :], jnp.where(sub == count - 1, ends_ref[1:2, :], tangent))

    lane = iota((TILE, LANES), 1)
    spread = jnp.where(lane == sub, jnp.sum(drift, axis=1, keepdims=True), 0.0)
    spread += jnp.where(lane == sub + count, jnp.sum(tangent, axis=1, keepdims=True), 0.0)
    line = jnp.sum(spread, axis=0, keepdims=True)

    if WIDTH > LANES:
        line = jnp.concatenate([line, jnp.zeros((1, WIDTH - LANES), F32)], axis=1)
    for j in range(m * n):
        lines[j] = line
    copy = pltpu.make_async_copy(lines, out_ref, sem)
    copy.start()

    near_corner_ref[...] = tail_ref[1, pl.ds(pick(halo.odd, 0, count - 1), 1), :]
    rest_ref[0:rows, :] = f_ref[pick(halo.odd, count - 2, 1)]
    rest_ref[rows:, :] = jnp.broadcast_to(tail_ref[1, pl.ds(pick(halo.odd, count - 1, 0), 1), :], (TILE, cols))
    for s in range(count):
        head_ref[s] = f_ref[s, 0:2, :]
    head_ref[count, 0:1, :] = halo.below(pl.ds(0, 1))
    head_ref[count, 1:2, :] = halo.above(pl.ds(0, 1))
    copy.wait()


def chunks(m, n, f, part, sums, rim, near, far, start, end, strip):
    count, rows, cols = f.shape
    return pl.pallas_call(
        functools.partial(chunk_kernel, m, n),
        out_shape=(
            jax.ShapeDtypeStruct((m * n, 1, WIDTH), F32),
            jax.ShapeDtypeStruct((1, cols), F32),
            jax.ShapeDtypeStruct((rows + TILE, cols), F32),
            jax.ShapeDtypeStruct((2, count, cols), F32),
            jax.ShapeDtypeStruct((count + 1, 2, cols), F32),
        ),
        in_specs=[VMEM] * 9,
        out_specs=[ANY] + [VMEM] * 4,
        scratch_shapes=[pltpu.VMEM((m * n, 1, WIDTH), F32), pltpu.SemaphoreType.DMA],
        compiler_params=PARAMS,
        name="chunks",
    )(f, part, sums, rim, near, far, start, end, strip)


def ratio_kernel(m, n, got_ref, scale_ref):
    count = scale_ref.shape[0] - 4
    path = lax.axis_index("path")
    first, last = path == 0, path == m - 1
    path_lo = jnp.where(first, path, path - 1)
    path_hi = jnp.where(last, path, path + 1)

    def gathered(p):
        total = got_ref[p, :, 0:LANES]
        for i in range(1, n):
            total += got_ref[i * m + p, :, 0:LANES]
        return jnp.broadcast_to(total, (TILE, LANES))

    mine = gathered(path)
    lower = gathered(path_lo)
    upper = gathered(path_hi)
    lane = iota((TILE, LANES), 1)
    sub = iota((TILE, LANES), 0)

    def shift(x, k):
        return pltpu.roll(x, k % LANES, 1)

    def ratios(x):
        return jnp.sqrt(x + EPS) / jnp.sqrt(shift(x, -count) + EPS)

    low = jnp.where(first, 0.0, shift(ratios(lower), 1 - count))
    high = jnp.where(last, 0.0, shift(ratios(upper), count + 1))
    own = ratios(mine)
    ratio = jnp.where(lane == 0, low, jnp.where(lane == count + 1, high, shift(own, 1)))

    def splat(t):
        return jnp.broadcast_to(jnp.sum(jnp.where(lane == t, ratio, 0.0), axis=1, keepdims=True), (TILE, LANES))

    for t in range(count + 2):
        scale_ref[t] = splat(t)
    column = jnp.sum(jnp.where(lane == sub + 1, ratio, 0.0), axis=1, keepdims=True)
    scale_ref[count + 2] = jnp.broadcast_to(column, (TILE, LANES))
    scale_ref[count + 3] = own


def speed_ratios(m, n, count, got):
    return pl.pallas_call(
        functools.partial(ratio_kernel, m, n),
        out_shape=jax.ShapeDtypeStruct((count + 4, TILE, LANES), F32),
        in_specs=[VMEM],
        out_specs=VMEM,
        cost_estimate=pl.CostEstimate(flops=RATIO_FLOPS, transcendentals=0, bytes_accessed=0),
        compiler_params=PARAMS,
        name="speed_ratios",
    )(got)


def final_kernel(
    m, scale_ref, near_corner_ref, rest_ref, f_ref, drift_ref, near_ref, far_ref, start_ref, end_ref,
    strip_ref, tail_ref, lead_ref, ratio_out, res_out, grad_out, ratio_ref, resid, grad, outer, rim, head_ref, sem,
):
    halo = Halo(m, near_ref, far_ref, start_ref, end_ref, rest_ref)
    count, rows, cols = f_ref.shape
    tiles = rows // TILE
    first, last = halo.first, halo.last
    ratio_ref[...] = scale_ref[count + 3][0, 0:count]
    copies = [pltpu.make_async_copy(ratio_ref, ratio_out, sem.at[2, 0])]
    copies[0].start()

    def widen(x):
        return jnp.concatenate([x] * (cols // LANES), axis=1)

    scale = [widen(scale_ref[t]) for t in range(count + 2)]
    column = widen(scale_ref[count + 2])
    row = iota((TILE, cols), 0)
    near, far = near_corner_ref[...], rest_ref[rows : rows + 1, :]
    corners = (
        (
            pick(first, strip_ref[count, 0:1, :], pick(halo.odd, near, far)),
            pick(last, strip_ref[count, 1:2, :], pick(halo.odd, far, near)),
        ),
        (lead_ref[count, 0:1, :], lead_ref[count, 1:2, :]),
    )

    def at(k):
        return pl.ds(TILE * k, TILE)

    def value(s, k):
        if s < 0:
            return halo.below(at(k)) if s == -1 else halo.below_2(at(k))
        if s >= count:
            return halo.above(at(k)) if s == count else halo.above_2(at(k))
        return f_ref[s, at(k), :]

    def residual_of(s):
        for k in range(tiles):
            if 0 <= s < count:
                drift = drift_ref[s, at(k), :]
                if k == 0:
                    drift += jnp.where(row == 0, tail_ref[1, s : s + 1, :], 0.0)
                if k == tiles - 1:
                    drift += jnp.where(row == TILE - 1, lead_ref[s, 0:1, :], 0.0)
            else:
                slot = 0 if s < 0 else 1
                c = outer[slot, at(k), :]
                above = outer[slot, TILE * k - 1 : TILE * k, :] if k > 0 else corners[0][slot]
                under = outer[slot, TILE * (k + 1) : TILE * (k + 1) + 1, :] if k < tiles - 1 else corners[1][slot]
                up = jnp.where(row == 0, above, pltpu.roll(c, 1, 0))
                dn = jnp.where(row == TILE - 1, under, pltpu.roll(c, TILE - 1, 0))
                drift = up + dn + sides(c) - 3.0 * c - c * c * c
            resid[s + 1, at(k + 1), :] = scale[s + 1] * (value(s + 1, k) - value(s - 1, k)) - drift

    def send(src, dst, slot):
        copy = pltpu.make_async_copy(src, dst, slot)
        copy.start()
        copies.append(copy)

    pieces = PIECES if count % PIECES == 0 else 1
    step = count // pieces
    for i in range(pieces):
        for s in range(i * step, (i + 1) * step):
            residual_of(s)
        span = pl.ds(i * step, step)
        send(resid.at[pl.ds(i * step + 1, step), pl.ds(TILE, rows)], res_out.at[span], sem.at[0, i])

    for k in range(tiles):
        outer[0, at(k), :] = halo.below(at(k))
        outer[1, at(k), :] = halo.above(at(k))
    residual_of(-1)
    residual_of(count)

    for s in range(count):
        rim[0, s : s + 1, :] = f_ref[s, 0:1, :]
        rim[1, s : s + 1, :] = f_ref[s, rows - 1 : rows, :]
        for r in range(2):
            head_ref[r, s : s + 1, :] = lead_ref[s, r : r + 1, :]
    for far, mid, near, (low, high), place in (
        (tail_ref[0], tail_ref[1], rim[0], corners[0], TILE - 1),
        (head_ref[1], head_ref[0], rim[1], corners[1], TILE + rows),
    ):
        ahead = jnp.where(row == count - 1, high, pltpu.roll(mid, count - 1, 0))
        behind = jnp.where(row == 0, low, pltpu.roll(mid, 1, 0))
        edge = column * (ahead - behind) - (far + near + sides(mid) - 3.0 * mid - mid * mid * mid)
        for s in range(count):
            resid[s + 1, place : place + 1, :] = edge[s : s + 1, :]

    def gradient_of(s):
        r = [resid[s + 1, at(k + 1), :] for k in range(tiles)]
        down = [resid[s + 1, TILE - 1 : TILE, :]] + [pltpu.roll(x, 1, 0) for x in r]
        up = [pltpu.roll(x, TILE - 1, 0) for x in r] + [resid[s + 1, TILE + rows : TILE + rows + 1, :]]
        for k in range(tiles):
            c = f_ref[s, at(k), :]
            around = jnp.where(row == 0, down[k], down[k + 1]) + jnp.where(row == TILE - 1, up[k + 1], up[k]) + sides(r[k])
            out = scale[s] * resid[s, at(k + 1), :] - scale[s + 2] * resid[s + 2, at(k + 1), :]
            grad[s, at(k), :] = out - (around - (3.0 + 3.0 * c * c) * r[k])

    for i in range(pieces):
        for s in range(i * step, (i + 1) * step):
            gradient_of(s)
        span = pl.ds(i * step, step)
        send(grad.at[span], grad_out.at[span], sem.at[1, i])
    for copy in copies:
        copy.wait()


def final(m, scale, corners, f, drift, slabs, strips):
    count, rows, cols = f.shape
    big = jax.ShapeDtypeStruct(f.shape, F32)
    return pl.pallas_call(
        functools.partial(final_kernel, m),
        out_shape=(jax.ShapeDtypeStruct((count,), F32), big, big),
        in_specs=[VMEM] * 12,
        out_specs=(ANY, ANY, ANY),
        scratch_shapes=[
            pltpu.VMEM((count,), F32),
            pltpu.VMEM((count + 2, rows + 2 * TILE, cols), F32),
            pltpu.VMEM(f.shape, F32),
            pltpu.VMEM((2, rows, cols), F32),
            pltpu.VMEM((2, count, cols), F32),
            pltpu.VMEM((2, count, cols), F32),
            pltpu.SemaphoreType.DMA((3, PIECES)),
        ],
        compiler_params=PARAMS,
        name="final",
    )(scale, *corners, f, drift, *slabs, *strips)


def swap(x, kind):
    size = lax.axis_size("path")
    return lax.ppermute(x, "path", [((i + kind) % size, ((i ^ 1) + kind) % size) for i in range(size)])


def ring(x, step):
    size = lax.axis_size("space")
    return lax.ppermute(x, "space", [(i, (i + step) % size) for i in range(size)])


def body(m, n, f, start, end):
    near, far = slices(f)
    strip = ring(tail_rows(f, start, end), 1)
    far = swap(far, 1)
    near = swap(near, 0)
    part, drift, rim = interior(f)
    slabs = near, far, start, end
    send, near_corner, rest, tail, head = chunks(m, n, f, part, ends(m, f, *slabs), rim, *slabs, strip)
    got = lax.all_to_all(send, ("space", "path"), 0, 0, tiled=True)
    lead = ring(head, -1)
    late = swap(near_corner, 0), swap(rest, 1)
    scale = speed_ratios(m, n, f.shape[0], got)
    return final(m, scale, late, f, drift, slabs, (strip, tail, lead))


def solution(mesh):
    m, n = mesh.shape["path"], mesh.shape["space"]
    in_specs = (P("path", "space", None), P("space", None), P("space", None))
    out_specs = (P("path"), P("path", "space", None), P("path", "space", None))
    return jax.shard_map(
        functools.partial(body, m, n), mesh=mesh, in_specs=in_specs, out_specs=out_specs, check_vma=False
    )
```

```python
import functools

import jax
import jax.numpy as jnp
from jax import lax
from jax.experimental import pallas as pl
from jax.experimental.pallas import tpu as pltpu
from jax.sharding import PartitionSpec as P

F32 = jnp.float32
LANES = 128
TILE = 8
EPS = 1e-06
VMEM = pl.BlockSpec(memory_space=pltpu.VMEM)
ANY = pl.BlockSpec(memory_space=pl.ANY)
PIECES = 4
WIDTH = 128
RATIO_FLOPS = 10**9
PARAMS = pltpu.CompilerParams(vmem_limit_bytes=16 * 2**20)


def lanes_sum(x):
    parts = [x[:, i : i + LANES] for i in range(0, x.shape[1], LANES)]
    while len(parts) > 1:
        parts = [a + b for a, b in zip(parts[::2], parts[1::2])] + parts[len(parts) & ~1 :]
    return parts[0]


def sides(x):
    cols = x.shape[1]
    return pltpu.roll(x, 1, 1) + pltpu.roll(x, cols - 1, 1)


def iota(shape, dim):
    return lax.broadcasted_iota(jnp.int32, shape, dim)


def odd(axis):
    return lax.rem(lax.axis_index(axis), 2) == 1


def pick(flag, x, y):
    return jnp.where(flag, x, y)


def slices_kernel(f_ref, near_ref, far_ref):
    count = f_ref.shape[0]
    flag = odd("path")
    base = pick(flag, 0, count - 2)
    for s in range(2):
        near_ref[s] = f_ref[base + s]
    far_ref[...] = f_ref[pick(flag, count - 1, 0)]


def tail_kernel(f_ref, start_ref, end_ref, tail_ref):
    count, rows, _ = f_ref.shape
    tail_ref[count, 0:1, :] = start_ref[rows - 1 :, :]
    tail_ref[count, 1:2, :] = end_ref[rows - 1 :, :]
    for s in range(count):
        tail_ref[s] = f_ref[s, rows - 2 :, :]


def slices(f):
    count, rows, cols = f.shape
    return pl.pallas_call(
        slices_kernel,
        out_shape=(jax.ShapeDtypeStruct((2, rows, cols), F32), jax.ShapeDtypeStruct((rows, cols), F32)),
        in_specs=[VMEM],
        out_specs=[VMEM] * 2,
        compiler_params=PARAMS,
        name="slices",
    )(f)


def tail_rows(f, start, end):
    count, rows, cols = f.shape
    return pl.pallas_call(
        tail_kernel,
        out_shape=jax.ShapeDtypeStruct((count + 1, 2, cols), F32),
        in_specs=[VMEM] * 3,
        out_specs=VMEM,
        compiler_params=PARAMS,
        name="tail_rows",
    )(f, start, end)


class Halo:
    def __init__(self, m, near_ref, far_ref, start_ref, end_ref, rest_ref=None):
        self.odd = odd("path")
        self.first = lax.axis_index("path") == 0
        self.last = lax.axis_index("path") == m - 1
        self.near, self.far, self.rest = near_ref, far_ref, rest_ref
        self.start, self.end = start_ref, end_ref

    def below(self, at):
        return pick(self.first, self.start[at, :], pick(self.odd, self.near[1, at, :], self.far[at, :]))

    def above(self, at):
        return pick(self.last, self.end[at, :], pick(self.odd, self.far[at, :], self.near[0, at, :]))

    def below_2(self, at):
        return pick(self.odd, self.near[0, at, :], self.rest[at, :])

    def above_2(self, at):
        return pick(self.odd, self.rest[at, :], self.near[1, at, :])


def interior_kernel(f_ref, part_ref, drift_ref, rim_ref):
    count, rows, cols = f_ref.shape
    tiles = rows // TILE
    row = iota((TILE, cols), 0)
    part_ref[...] = jnp.zeros_like(part_ref)

    def drift_sum(s, _):
        total = jnp.zeros((TILE, LANES), F32)
        for k in range(tiles):
            c = f_ref[s, pl.ds(TILE * k, TILE), :]
            above = f_ref[s, pl.ds(TILE * k - 1, 1), :] if k > 0 else 0.0
            under = f_ref[s, pl.ds(TILE * (k + 1), 1), :] if k < tiles - 1 else 0.0
            up = jnp.where(row == 0, above, pltpu.roll(c, 1, 0))
            dn = jnp.where(row == TILE - 1, under, pltpu.roll(c, TILE - 1, 0))
            drift = up + dn + sides(c) - 3.0 * c - c * c * c
            drift_ref[s, pl.ds(TILE * k, TILE), :] = drift
            if k == 0:
                rim_ref[0, pl.ds(s, 1), :] = drift[0:1]
                rim_ref[1, pl.ds(s, 1), :] = c[0:1]
                drift = jnp.where(row == 0, 0.0, drift)
            if k == tiles - 1:
                drift = jnp.where(row == TILE - 1, 0.0, drift)
            total += lanes_sum(drift * drift)
        part_ref[pl.ds(s, 1), :] = jnp.sum(total, axis=0, keepdims=True)
        return 0

    def tangent_sum(s, _):
        total = jnp.zeros((TILE, LANES), F32)
        for k in range(tiles):
            tangent = f_ref[s + 1, pl.ds(TILE * k, TILE), :] - f_ref[s - 1, pl.ds(TILE * k, TILE), :]
            total += lanes_sum(tangent * tangent)
        part_ref[pl.ds(count + s, 1), :] = jnp.sum(total, axis=0, keepdims=True)
        return 0

    lax.fori_loop(0, count, drift_sum, 0)
    lax.fori_loop(1, count - 1, tangent_sum, 0)


def interior(f):
    count, rows, cols = f.shape
    return pl.pallas_call(
        interior_kernel,
        out_shape=(
            jax.ShapeDtypeStruct((2 * count, LANES), F32),
            jax.ShapeDtypeStruct(f.shape, F32),
            jax.ShapeDtypeStruct((2, count, cols), F32),
        ),
        in_specs=[VMEM],
        out_specs=[VMEM] * 3,
        cost_estimate=pl.CostEstimate(flops=20 * count * rows * cols, transcendentals=0, bytes_accessed=8 * count * rows * cols),
        compiler_params=PARAMS,
        name="interior",
    )(f)


def chunk_kernel(
    m, n, f_ref, part_ref, rim_ref, near_ref, far_ref, start_ref, end_ref, strip_ref,
    out_ref, near_corner_ref, rest_ref, tail_ref, head_ref, lines, sem,
):
    halo = Halo(m, near_ref, far_ref, start_ref, end_ref)
    count, rows, cols = f_ref.shape
    tiles = rows // TILE

    for s in range(count):
        for r in range(2):
            tail_ref[r, s : s + 1, :] = strip_ref[s, r : r + 1, :]
    r0, r1 = tail_ref[0], tail_ref[1]

    drift_a = r0 + rim_ref[1] + sides(r1) - 3.0 * r1 - r1 * r1 * r1
    drift_b = rim_ref[0] + r1
    drift = part_ref[0:count, :] + lanes_sum(drift_a * drift_a) + lanes_sum(drift_b * drift_b)

    totals = [jnp.zeros((TILE, LANES), F32) for _ in range(2)]
    for k in range(tiles):
        at = pl.ds(TILE * k, TILE)
        tangents = (f_ref[1, at, :] - halo.below(at), halo.above(at) - f_ref[count - 2, at, :])
        totals = [a + lanes_sum(t * t) for a, t in zip(totals, tangents)]
    head_sum, tail_sum = [jnp.sum(a, axis=0, keepdims=True) for a in totals]
    sub = iota((TILE, LANES), 0)
    tangent = part_ref[count : 2 * count, :]
    tangent = jnp.where(sub == 0, head_sum, jnp.where(sub == count - 1, tail_sum, tangent))

    lane = iota((TILE, LANES), 1)
    spread = jnp.where(lane == sub, jnp.sum(drift, axis=1, keepdims=True), 0.0)
    spread += jnp.where(lane == sub + count, jnp.sum(tangent, axis=1, keepdims=True), 0.0)
    line = jnp.sum(spread, axis=0, keepdims=True)

    if WIDTH > LANES:
        line = jnp.concatenate([line, jnp.zeros((1, WIDTH - LANES), F32)], axis=1)
    for j in range(m * n):
        lines[j] = line
    copy = pltpu.make_async_copy(lines, out_ref, sem)
    copy.start()

    near_corner_ref[...] = tail_ref[1, pl.ds(pick(halo.odd, 0, count - 1), 1), :]
    rest_ref[0:rows, :] = f_ref[pick(halo.odd, count - 2, 1)]
    rest_ref[rows:, :] = jnp.broadcast_to(tail_ref[1, pl.ds(pick(halo.odd, count - 1, 0), 1), :], (TILE, cols))
    for s in range(count):
        head_ref[s] = f_ref[s, 0:2, :]
    head_ref[count, 0:1, :] = halo.below(pl.ds(0, 1))
    head_ref[count, 1:2, :] = halo.above(pl.ds(0, 1))
    copy.wait()


def chunks(m, n, f, part, rim, near, far, start, end, strip):
    count, rows, cols = f.shape
    return pl.pallas_call(
        functools.partial(chunk_kernel, m, n),
        out_shape=(
            jax.ShapeDtypeStruct((m * n, 1, WIDTH), F32),
            jax.ShapeDtypeStruct((1, cols), F32),
            jax.ShapeDtypeStruct((rows + TILE, cols), F32),
            jax.ShapeDtypeStruct((2, count, cols), F32),
            jax.ShapeDtypeStruct((count + 1, 2, cols), F32),
        ),
        in_specs=[VMEM] * 8,
        out_specs=[ANY] + [VMEM] * 4,
        scratch_shapes=[pltpu.VMEM((m * n, 1, WIDTH), F32), pltpu.SemaphoreType.DMA],
        compiler_params=PARAMS,
        name="chunks",
    )(f, part, rim, near, far, start, end, strip)


def ratio_kernel(m, n, got_ref, scale_ref):
    count = scale_ref.shape[0] - 4
    path = lax.axis_index("path")
    first, last = path == 0, path == m - 1
    path_lo = jnp.where(first, path, path - 1)
    path_hi = jnp.where(last, path, path + 1)

    def gathered(p):
        total = got_ref[p, :, 0:LANES]
        for i in range(1, n):
            total += got_ref[i * m + p, :, 0:LANES]
        return jnp.broadcast_to(total, (TILE, LANES))

    mine = gathered(path)
    lower = gathered(path_lo)
    upper = gathered(path_hi)
    lane = iota((TILE, LANES), 1)
    sub = iota((TILE, LANES), 0)

    def shift(x, k):
        return pltpu.roll(x, k % LANES, 1)

    def ratios(x):
        return jnp.sqrt(x + EPS) / jnp.sqrt(shift(x, -count) + EPS)

    low = jnp.where(first, 0.0, shift(ratios(lower), 1 - count))
    high = jnp.where(last, 0.0, shift(ratios(upper), count + 1))
    own = ratios(mine)
    ratio = jnp.where(lane == 0, low, jnp.where(lane == count + 1, high, shift(own, 1)))

    def splat(t):
        return jnp.broadcast_to(jnp.sum(jnp.where(lane == t, ratio, 0.0), axis=1, keepdims=True), (TILE, LANES))

    for t in range(count + 2):
        scale_ref[t] = splat(t)
    column = jnp.sum(jnp.where(lane == sub + 1, ratio, 0.0), axis=1, keepdims=True)
    scale_ref[count + 2] = jnp.broadcast_to(column, (TILE, LANES))
    scale_ref[count + 3] = own


def speed_ratios(m, n, count, got):
    return pl.pallas_call(
        functools.partial(ratio_kernel, m, n),
        out_shape=jax.ShapeDtypeStruct((count + 4, TILE, LANES), F32),
        in_specs=[VMEM],
        out_specs=VMEM,
        cost_estimate=pl.CostEstimate(flops=RATIO_FLOPS, transcendentals=0, bytes_accessed=0),
        compiler_params=PARAMS,
        name="speed_ratios",
    )(got)


def final_kernel(
    m, scale_ref, near_corner_ref, rest_ref, f_ref, drift_ref, near_ref, far_ref, start_ref, end_ref,
    strip_ref, tail_ref, lead_ref, ratio_out, res_out, grad_out, ratio_ref, resid, grad, outer, rim, head_ref, sem,
):
    halo = Halo(m, near_ref, far_ref, start_ref, end_ref, rest_ref)
    count, rows, cols = f_ref.shape
    tiles = rows // TILE
    first, last = halo.first, halo.last
    ratio_ref[...] = scale_ref[count + 3][0, 0:count]
    copies = [pltpu.make_async_copy(ratio_ref, ratio_out, sem.at[2, 0])]
    copies[0].start()

    def widen(x):
        return jnp.concatenate([x] * (cols // LANES), axis=1)

    scale = [widen(scale_ref[t]) for t in range(count + 2)]
    column = widen(scale_ref[count + 2])
    row = iota((TILE, cols), 0)
    near, far = near_corner_ref[...], rest_ref[rows : rows + 1, :]
    corners = (
        (
            pick(first, strip_ref[count, 0:1, :], pick(halo.odd, near, far)),
            pick(last, strip_ref[count, 1:2, :], pick(halo.odd, far, near)),
        ),
        (lead_ref[count, 0:1, :], lead_ref[count, 1:2, :]),
    )

    def at(k):
        return pl.ds(TILE * k, TILE)

    def value(s, k):
        if s < 0:
            return halo.below(at(k)) if s == -1 else halo.below_2(at(k))
        if s >= count:
            return halo.above(at(k)) if s == count else halo.above_2(at(k))
        return f_ref[s, at(k), :]

    def residual_of(s):
        for k in range(tiles):
            if 0 <= s < count:
                drift = drift_ref[s, at(k), :]
                if k == 0:
                    drift += jnp.where(row == 0, tail_ref[1, s : s + 1, :], 0.0)
                if k == tiles - 1:
                    drift += jnp.where(row == TILE - 1, lead_ref[s, 0:1, :], 0.0)
            else:
                slot = 0 if s < 0 else 1
                c = outer[slot, at(k), :]
                above = outer[slot, TILE * k - 1 : TILE * k, :] if k > 0 else corners[0][slot]
                under = outer[slot, TILE * (k + 1) : TILE * (k + 1) + 1, :] if k < tiles - 1 else corners[1][slot]
                up = jnp.where(row == 0, above, pltpu.roll(c, 1, 0))
                dn = jnp.where(row == TILE - 1, under, pltpu.roll(c, TILE - 1, 0))
                drift = up + dn + sides(c) - 3.0 * c - c * c * c
            resid[s + 1, at(k + 1), :] = scale[s + 1] * (value(s + 1, k) - value(s - 1, k)) - drift

    def send(src, dst, slot):
        copy = pltpu.make_async_copy(src, dst, slot)
        copy.start()
        copies.append(copy)

    half = count // 2
    res_cuts = (0, half, count)
    grad_cuts = (0, half, count - 2, count - 1, count)
    for i, (lo, hi) in enumerate(zip(res_cuts, res_cuts[1:])):
        for s in range(lo, hi):
            residual_of(s)
        span = pl.ds(lo, hi - lo)
        send(resid.at[pl.ds(lo + 1, hi - lo), pl.ds(TILE, rows)], res_out.at[span], sem.at[0, i])

    for k in range(tiles):
        outer[0, at(k), :] = halo.below(at(k))
        outer[1, at(k), :] = halo.above(at(k))
    residual_of(-1)
    residual_of(count)

    for s in range(count):
        rim[0, s : s + 1, :] = f_ref[s, 0:1, :]
        rim[1, s : s + 1, :] = f_ref[s, rows - 1 : rows, :]
        for r in range(2):
            head_ref[r, s : s + 1, :] = lead_ref[s, r : r + 1, :]
    for far, mid, near, (low, high), place in (
        (tail_ref[0], tail_ref[1], rim[0], corners[0], TILE - 1),
        (head_ref[1], head_ref[0], rim[1], corners[1], TILE + rows),
    ):
        ahead = jnp.where(row == count - 1, high, pltpu.roll(mid, count - 1, 0))
        behind = jnp.where(row == 0, low, pltpu.roll(mid, 1, 0))
        edge = column * (ahead - behind) - (far + near + sides(mid) - 3.0 * mid - mid * mid * mid)
        for s in range(count):
            resid[s + 1, place : place + 1, :] = edge[s : s + 1, :]

    def gradient_of(s):
        r = [resid[s + 1, at(k + 1), :] for k in range(tiles)]
        down = [resid[s + 1, TILE - 1 : TILE, :]] + [pltpu.roll(x, 1, 0) for x in r]
        up = [pltpu.roll(x, TILE - 1, 0) for x in r] + [resid[s + 1, TILE + rows : TILE + rows + 1, :]]
        for k in range(tiles):
            c = f_ref[s, at(k), :]
            around = jnp.where(row == 0, down[k], down[k + 1]) + jnp.where(row == TILE - 1, up[k + 1], up[k]) + sides(r[k])
            out = scale[s] * resid[s, at(k + 1), :] - scale[s + 2] * resid[s + 2, at(k + 1), :]
            grad[s, at(k), :] = out - (around - (3.0 + 3.0 * c * c) * r[k])

    for i, (lo, hi) in enumerate(zip(grad_cuts, grad_cuts[1:])):
        for s in range(lo, hi):
            gradient_of(s)
        span = pl.ds(lo, hi - lo)
        send(grad.at[span], grad_out.at[span], sem.at[1, i])
    for copy in copies:
        copy.wait()


def final(m, scale, corners, f, drift, slabs, strips):
    count, rows, cols = f.shape
    big = jax.ShapeDtypeStruct(f.shape, F32)
    return pl.pallas_call(
        functools.partial(final_kernel, m),
        out_shape=(jax.ShapeDtypeStruct((count,), F32), big, big),
        in_specs=[VMEM] * 12,
        out_specs=(ANY, ANY, ANY),
        scratch_shapes=[
            pltpu.VMEM((count,), F32),
            pltpu.VMEM((count + 2, rows + 2 * TILE, cols), F32),
            pltpu.VMEM(f.shape, F32),
            pltpu.VMEM((2, rows, cols), F32),
            pltpu.VMEM((2, count, cols), F32),
            pltpu.VMEM((2, count, cols), F32),
            pltpu.SemaphoreType.DMA((3, PIECES)),
        ],
        compiler_params=PARAMS,
        name="final",
    )(scale, *corners, f, drift, *slabs, *strips)


def swap(x, kind):
    size = lax.axis_size("path")
    return lax.ppermute(x, "path", [((i + kind) % size, ((i ^ 1) + kind) % size) for i in range(size)])


def ring(x, step):
    size = lax.axis_size("space")
    return lax.ppermute(x, "space", [(i, (i + step) % size) for i in range(size)])


def body(m, n, f, start, end):
    near, far = slices(f)
    strip = ring(tail_rows(f, start, end), 1)
    far = swap(far, 1)
    near = swap(near, 0)
    part, drift, rim = interior(f)
    slabs = near, far, start, end
    send, near_corner, rest, tail, head = chunks(m, n, f, part, rim, *slabs, strip)
    got = lax.all_to_all(send, ("space", "path"), 0, 0, tiled=True)
    lead = ring(head, -1)
    late = swap(near_corner, 0), swap(rest, 1)
    scale = speed_ratios(m, n, f.shape[0], got)
    return final(m, scale, late, f, drift, slabs, (strip, tail, lead))


def solution(mesh):
    m, n = mesh.shape["path"], mesh.shape["space"]
    in_specs = (P("path", "space", None), P("space", None), P("space", None))
    out_specs = (P("path"), P("path", "space", None), P("path", "space", None))
    return jax.shard_map(
        functools.partial(body, m, n), mesh=mesh, in_specs=in_specs, out_specs=out_specs, check_vma=False
    )
```
